32 devices in a mesh: fsdp: 8 (over y, x, core), tensor: 4 (over z).
Axes of the slice: x: 2, y: 2, z: 4, core: 2. Of those that a mesh axis runs over, the one named last changes fastest.
Arguments:
- tokens: bfloat16 [2, 8192, 1024], P(None, ('fsdp', 'tensor')), may hold values from -6 to 6
- segment: int32 [2, 8192], P(None, 'fsdp'), may hold values from 0 to 12, as said below
- route: int32 [2, 8192, 1], P(None, 'fsdp'), may hold values from 0 to 7; in each aligned block of 256 rows (0 to 255, 256 to 511, ..., all dimensions but the last counted through in order) at most 48 rows name the same one
- w_qkv: bfloat16 [3, 1024, 1024], P(None, 'fsdp', 'tensor'), may hold values from -0.1875 to 0.1875
- bias_qv: bfloat16 [2, 16, 64], P(None, 'tensor', 'fsdp'), may hold values from -0.4375 to 0.4375
- w_o: bfloat16 [1024, 1024], P('tensor', 'fsdp'), may hold values from -3 to 3
- w_router: bfloat16 [1024, 8], P(('fsdp', 'tensor')), may hold values from -0.125 to 0.125
- w_up: bfloat16 [8, 1024, 4096], P(None, 'fsdp', 'tensor'), may hold values from -0.1875 to 0.1875
- w_down: bfloat16 [8, 4096, 1024], P(None, 'tensor', 'fsdp'), may hold values from -1.5 to 1.5
- norm_gains: bfloat16 [2, 1024], P(None, ('fsdp', 'tensor')), may hold values from 0.5 to 1.5
- shifts: bfloat16 [4, 1024], P(None, ('fsdp', 'tensor')), may hold values from -2 to 2
- cotangent: bfloat16 [2, 8192, 1024], P(None, ('fsdp', 'tensor')), may hold values from -6 to 6
Outputs:
- output: bfloat16 [2, 8192, 1024], P(None, ('fsdp', 'tensor'))
- input_grad: float32 [2, 8192, 1024], P(None, ('fsdp', 'tensor'))
- grad_w_qkv: float32 [3, 1024, 1024], P(None, 'fsdp', 'tensor')
- grad_bias_qv: float32 [2, 16, 64], P(None, 'tensor', 'fsdp')
- grad_w_o: float32 [1024, 1024], P('tensor', 'fsdp')
- grad_w_router: float32 [1024, 8], P(('fsdp', 'tensor'))
- grad_w_up: float32 [8, 1024, 4096], P(None, 'fsdp', 'tensor')
- grad_w_down: float32 [8, 4096, 1024], P(None, 'tensor', 'fsdp')
- grad_norm_gains: float32 [2, 1024], P(None, ('fsdp', 'tensor'))
- grad_shifts: float32 [3, 1024], P(None, ('fsdp', 'tensor'))
- grad_expert_shift: float32 [1024], P(('fsdp', 'tensor'))
The draws below stay inside these ranges and needn't reach their ends.
Inputs may be any that keep to these rules, and one draw needn't show every extreme that they name: `segment`: within each tree the first 256 tokens hold 0; then four runs of 192 tokens follow, run b holding 1 + b, then 5 + 2 b, then 6 + 2 b, each of the three segments 64 // 2 tokens or more. `route`: within the rows of one device (aligned blocks of 1024 / 4 tokens of a tree, the tree split evenly over tensor) no expert is named by more than 48 tokens, a bound that some block reaches in such a block; hence no expert is named by more than 192 tokens of a tree.
All inputs are finite; a program needn't handle non-finite values.
Results may differ from the reference program's by a relative error of at most 0.03.
Values may be sent and summed in bfloat16 or wider, within the bound.
A program may use at most 256 MiB of HBM per device.

```python
import math
import jax
import jax.numpy as jnp
import numpy as np
from jax import lax

D = 1024
HEADS = 16
DH = 64
FF = 4096
EXPERTS = 8
MICRO = 2
TRUNK = 256
BRANCH = 64
TREE = 1024
LCAP = 48
CAP = 192
SEQ = 8192
N_TENSOR = 4


def draw_segment(key, part):
    tree_total = MICRO * SEQ // TREE
    first_key, second_key = jax.random.split(key)
    branch_len = jax.random.randint(first_key, (tree_total, 4, 1), BRANCH // 2, 3 * BRANCH // 2 + 1)
    remaining = 3 * BRANCH - branch_len
    leaf_len = jax.random.randint(second_key, (tree_total, 4, 1), BRANCH // 2, remaining - BRANCH // 2 + 1)
    offsets = jnp.arange(3 * BRANCH, dtype=jnp.int32)[None, None, :]
    branch_ids = jnp.arange(4, dtype=jnp.int32)[None, :, None]
    labels = jnp.where(offsets < branch_len, 1 + branch_ids, jnp.where(offsets < branch_len + leaf_len, 5 + 2 * branch_ids, 6 + 2 * branch_ids))
    trunk_ids = jnp.zeros((tree_total, TRUNK), jnp.int32)
    whole = jnp.concatenate([trunk_ids, labels.reshape(tree_total, 12 * BRANCH).astype(jnp.int32)], axis=1)
    return whole.reshape(MICRO, SEQ).astype(jnp.int32)


def with_spikes(drawn, key, source, target, parts, factor):
    owner, partner = [(jnp.arange(drawn.shape[axis_at]) // (drawn.shape[axis_at] // parts)).reshape([-1 if axis == axis_at else 1 for axis in range(drawn.ndim)]) for axis_at in (source, target)]
    chosen = jax.random.permutation(key, parts)[partner]
    strong = (owner == chosen) | (owner == (partner + parts // 2) % parts)
    return jnp.where(strong, factor * drawn, drawn)


def steps_of(key, dims, pieces, least, high):
    level, own = 1.0, jax.random.fold_in(key, 6)
    for dim, shards_of in pieces:
        draws = jnp.exp(jax.random.uniform(jax.random.fold_in(own, dim), (shards_of,), jnp.float32, least / len(pieces), high / len(pieces)))
        level = level * jnp.repeat(draws, dims[dim] // shards_of).reshape([-1 if axis == dim else 1 for axis in range(len(dims))])
    return level


def routed_block(key, own, number, rows, amount, top, reach, skew):
    order = jax.random.permutation(key, amount)
    crowded, ordinary = shares(amount, rows * top, reach, skew, True), shares(amount, rows * top, reach, skew, False)
    places = jnp.arange(amount)

    def named(sizes, rotation):
        used = int((sizes > 0).sum())
        fixed = max(1, used // 4)
        passed = fixed + (places - fixed + rotation * (used - fixed)) % max(1, amount - fixed)
        return jnp.zeros((amount,), jnp.int32).at[order[jnp.where(places < fixed, places, passed)]].set(jnp.asarray(sizes, jnp.int32))

    sizes = jnp.where(number % 4 == 0, named(crowded, number // 4), named(ordinary, number - number // 4 - 1))
    mixed = jax.random.permutation(jax.random.fold_in(own, 3), amount)
    giver, receiver = mixed[0:amount // 2 * 2:2], mixed[1:amount // 2 * 2:2]
    slack = jnp.minimum(sizes[giver] - 1, reach - sizes[receiver]) // 2
    slack = jnp.where((giver == order[0]) | (receiver == order[0]) | (sizes[receiver] == 0), 0, jnp.maximum(slack, 0))
    passed = jax.random.randint(jax.random.fold_in(own, 4), (amount // 2,), 0, 1 << 20) % (slack + 1)
    sizes = sizes.at[giver].add(-passed).at[receiver].add(passed)
    items = jnp.searchsorted(jnp.cumsum(sizes), jnp.arange(rows * top), side="right").astype(jnp.int32)
    listing = items.reshape(top, rows).T
    listing = listing[jax.random.permutation(jax.random.fold_in(own, 1), rows)]
    rotation = jax.random.randint(jax.random.fold_in(own, 2), (rows, 1), 0, top)
    return jnp.take_along_axis(listing, (jnp.arange(top)[None, :] + rotation) % top, axis=1)


def shares(number_of, total, bound, slope, full):
    loads = [(1 << 20) // math.isqrt(grade ** slope) + 1 for grade in range(1, number_of + 1)]
    largest = bound if full else min(bound, max(-(-total // number_of), total * loads[0] // sum(loads)))
    least = 1 if total - largest >= number_of - 1 else 0
    counts, rest = [largest] + [least] * (number_of - 1), total - largest - least * (number_of - 1)
    while rest > 0:
        free = [i for i in range(1, number_of) if counts[i] < largest] or [i for i in range(1, number_of) if counts[i] < bound]
        mass, budget = sum([loads[i] for i in free]), rest
        for i in free:
            extra = min(bound - counts[i], max(1, budget * loads[i] // mass), rest)
            counts[i] = counts[i] + extra
            rest = rest - extra
    return np.array(counts)


def bell_draw(rng, extent, scale, limit, pieces=(), kind=jnp.bfloat16):
    array = scale * jax.random.normal(rng, extent, jnp.float32)
    if pieces:
        array = array * steps_of(rng, extent, pieces, -0.22, 0.18)
    return jnp.clip(array, -limit, limit).astype(kind)


def noise_with(stream_key, extent, spread, bound, shards, heavy, kind=jnp.bfloat16):
    values = spread * jax.random.normal(stream_key, extent, jnp.float32)
    if shards:
        values = values * steps_of(stream_key, extent, shards, -0.22, 0.18)
    return jnp.clip(with_spikes(values, jax.random.fold_in(stream_key, 3), *heavy), -bound, bound).astype(kind)


def setup_inputs(seed: int = 0) -> dict:
    arg_keys = jax.random.split(jax.random.key(seed), 13)
    tokens = bell_draw(arg_keys[0], (MICRO, SEQ, D), 1.0, 6.0, ((1, 32),))
    segment = draw_segment(jax.random.fold_in(arg_keys[12], 71), 0)
    route_keys = jax.random.split(jax.random.fold_in(arg_keys[2], 1), MICRO * SEQ // (TREE // N_TENSOR))
    route_turns = jax.random.permutation(jax.random.fold_in(arg_keys[2], 3), MICRO * SEQ // (TREE // N_TENSOR))
    route = jax.vmap(lambda own, number: routed_block(jax.random.fold_in(arg_keys[2], 2), own, number, TREE // N_TENSOR, EXPERTS, 1, LCAP, 1))(route_keys, route_turns).reshape((MICRO, SEQ, 1))
    w_qkv = bell_draw(arg_keys[3], (3, D, D), D ** -0.5, 0.1875, ((1, 8), (2, 4)))
    bias_qv = bell_draw(arg_keys[4], (2, HEADS, DH), 0.03, 0.4375, ((1, 4), (2, 8)))
    w_o = bell_draw(arg_keys[5], (D, D), (max(D // 256, 1)) ** -0.5, 3.0, ((0, 4), (1, 8)))
    w_router = bell_draw(arg_keys[6], (D, EXPERTS), (2 * D) ** -0.5, 0.125, ((0, 32),))
    w_up = bell_draw(arg_keys[7], (EXPERTS, D, FF), D ** -0.5, 0.1875, ((1, 8), (2, 4)))
    w_down = bell_draw(arg_keys[8], (EXPERTS, FF, D), (max(FF // 256, 1)) ** -0.5, 1.5, ((1, 4), (2, 8)))
    norm_gains = jnp.clip(1.0 + 0.1 * jax.random.normal(arg_keys[9], (2, D), jnp.float32), 0.5, 1.5).astype(jnp.bfloat16)
    shifts = bell_draw(arg_keys[10], (4, D), 0.15, 2.0, ((1, 32),))
    cotangent = noise_with(arg_keys[11], (MICRO, SEQ, D), 1.0, 6.0, ((1, 32),), (1, 2, 32, 2.75))
    return dict(tokens=tokens, segment=segment, route=route, w_qkv=w_qkv, bias_qv=bias_qv, w_o=w_o, w_router=w_router, w_up=w_up, w_down=w_down, norm_gains=norm_gains, shifts=shifts, cotangent=cotangent)


@jax.custom_vjp
def low(v):
    return lax.optimization_barrier(v.astype(jnp.bfloat16)).astype(jnp.float32)

@jax.custom_vjp
def low_back(v):
    return v

def low_keep(v):
    return (low(v), None)

def low_pass(kept, grad):
    return (grad,)

def back_keep(v):
    return (v, None)

def back_low(kept, grad):
    return (low(grad),)
low.defvjp(low_keep, low_pass)
low_back.defvjp(back_keep, back_low)
EPSILON = 1e-05
MASKED = -1e+30
HIGHEST = lax.Precision.HIGHEST

def layer_norm(row_data, gain_row, shift_row):
    centered = row_data - lax.optimization_barrier(jnp.mean(row_data, axis=-1, keepdims=True))
    variance = lax.optimization_barrier(jnp.mean(centered * centered, axis=-1, keepdims=True))
    return centered * lax.rsqrt(variance + EPSILON) * gain_row + shift_row

def matmul(left, right):
    return jnp.dot(left, right, precision=HIGHEST, preferred_element_type=jnp.float32)

def tree_mask(segments):
    query_seg = segments[:, None]
    key_seg = segments[None, :]
    related = (key_seg == 0) | (key_seg == query_seg) | (query_seg >= 5) & (key_seg == (query_seg - 5) // 2 + 1)
    row_index = jnp.arange(segments.shape[0])[:, None]
    col_index = jnp.arange(segments.shape[0])[None, :]
    return related & (col_index <= row_index)

def attend_head(queries, key_rows, value_rows, allowed):
    scores = low_back(jnp.where(allowed, matmul(queries, key_rows.T) * DH ** (-0.5), MASKED))
    weights = low(jax.nn.softmax(scores, axis=-1))
    return matmul(weights, value_rows)

def tree_forward(inputs, segments, routes, weight_set):
    w_qkv, bias_qv, w_o, w_router, w_up, w_down, norm_gains, shifts = weight_set
    normed_in = low(layer_norm(inputs, norm_gains[0], shifts[0]))
    queries = low(low_back(matmul(normed_in, w_qkv[0]) + bias_qv[0].reshape(D)))
    key_rows = low(low_back(matmul(normed_in, w_qkv[1])))
    value_rows = low(low_back(matmul(normed_in, w_qkv[2]) + bias_qv[1].reshape(D)))
    allowed = tree_mask(segments)

    def per_head(items):
        return attend_head(items[0], items[1], items[2], allowed)

    def by_heads(block_data):
        return block_data.reshape(TREE, HEADS, DH).transpose(1, 0, 2)
    attended = lax.map(jax.checkpoint(per_head), (by_heads(queries), by_heads(key_rows), by_heads(value_rows)))
    heads_out = low(low_back(attended.transpose(1, 0, 2).reshape(TREE, D)))
    residual = inputs + low_back(matmul(heads_out, w_o)) + shifts[2]
    normed_mid = low(layer_norm(residual, norm_gains[1], shifts[1]))
    router_probs = jax.nn.softmax(matmul(normed_mid, w_router), axis=-1)
    chosen = routes[:, None] == jnp.arange(EXPERTS, dtype=jnp.int32)[None, :]
    gate_value = lax.optimization_barrier(jnp.sum(jnp.where(chosen, router_probs, 0.0), axis=-1))
    running = jnp.cumsum(chosen.astype(jnp.int32), axis=0).astype(jnp.int32)
    slot_index = (routes * CAP + lax.optimization_barrier(jnp.sum(jnp.where(chosen, running, 0), axis=-1)) - 1).astype(jnp.int32)
    routed = jnp.zeros((EXPERTS * CAP, D), jnp.float32).at[slot_index].set(normed_mid).reshape(EXPERTS, CAP, D)
    hidden = low_back(jnp.einsum('ecd,edf->ecf', routed, w_up, precision=HIGHEST))
    activated = low(jax.nn.gelu(hidden, approximate=True))
    expert_rows = low_back(jnp.einsum('ecf,efd->ecd', activated, w_down, precision=HIGHEST)).reshape(EXPERTS * CAP, D)
    return residual + gate_value[:, None] * expert_rows[slot_index] + shifts[3]

def reference(tokens, segment, route, w_qkv, bias_qv, w_o, w_router, w_up, w_down, norm_gains, shifts, cotangent):
    weight_set = tuple((operand.astype(jnp.float32) for operand in (w_qkv, bias_qv, w_o, w_router, w_up, w_down, norm_gains, shifts)))
    trees = tokens.astype(jnp.float32).reshape(-1, TREE, D)
    tree_segments = segment.reshape(-1, TREE).astype(jnp.int32)
    tree_routes = route.reshape(-1, TREE).astype(jnp.int32)

    def forward(inputs, weights_in):

        def one_tree(items):
            return tree_forward(items[0], items[1], items[2], weights_in)
        return lax.map(jax.checkpoint(one_tree), (inputs, tree_segments, tree_routes))
    outputs, pullback = jax.vjp(forward, trees, weight_set)
    grad_inputs, grad_weights = pullback(cotangent.astype(jnp.float32).reshape(-1, TREE, D))
    return (outputs.reshape(tokens.shape).astype(jnp.bfloat16), grad_inputs.reshape(tokens.shape), grad_weights[0], grad_weights[1], grad_weights[2], grad_weights[3], grad_weights[4], grad_weights[5], grad_weights[6], grad_weights[7][:3], grad_weights[7][3])
```

```python
from functools import partial

import jax
import jax.numpy as jnp
from jax import lax
from jax.experimental import pallas as pl
from jax.experimental.pallas import tpu as pltpu
from jax.sharding import PartitionSpec as P

EPSILON = 1e-05
MASKED = -1e30
HIGHEST = lax.Precision.HIGHEST


def norm_rows(row_data, gain_row, shift_row):
    centered = row_data - jnp.mean(row_data, axis=-1, keepdims=True)
    inv_scale = lax.rsqrt(jnp.mean(centered * centered, axis=-1, keepdims=True) + EPSILON)
    normed = centered * inv_scale
    return (normed * gain_row + shift_row, normed, inv_scale)


def norm_back(grad_out, normed, inv_scale, gain_row):
    grad_normed = grad_out * gain_row
    interior = (
        grad_normed
        - jnp.mean(grad_normed, axis=-1, keepdims=True)
        - normed * jnp.mean(grad_normed * normed, axis=-1, keepdims=True)
    )
    return (inv_scale * interior, jnp.sum(grad_out * normed, axis=0), jnp.sum(grad_out, axis=0))


def tree_allowed(query_segs, key_segs, row_start):
    query_seg = query_segs[:, None]
    key_seg = key_segs[None, :]
    related = (
        (key_seg == 0)
        | (key_seg == query_seg)
        | (query_seg >= 5) & (key_seg == (query_seg - 5) // 2 + 1)
    )
    row_index = row_start + jnp.arange(query_segs.shape[0])[:, None]
    col_index = jnp.arange(key_segs.shape[0])[None, :]
    return related & (col_index <= row_index)


def block_scores(queries, key_rows, allowed, factor):
    scaled = (
        jnp.einsum("qhd,khd->hqk", queries, key_rows, preferred_element_type=jnp.float32) * factor
    )
    return jnp.where(allowed[None], scaled, MASKED)


def attend_forward(queries, key_rows, value_rows, segments, block_len):
    tree_len = queries.shape[0]
    factor = queries.shape[-1] ** (-0.5)
    outputs, totals = ([], [])
    for row_start in range(0, tree_len, block_len):
        row_stop = row_start + block_len
        allowed = tree_allowed(segments[row_start:row_stop], segments[:row_stop], row_start)
        scores = block_scores(queries[row_start:row_stop], key_rows[:row_stop], allowed, factor)
        peak_score = jnp.max(scores, axis=-1, keepdims=True)
        exponent = jnp.exp(scores - peak_score)
        denom_sum = jnp.sum(exponent, axis=-1, keepdims=True)
        weights = (exponent / denom_sum).astype(jnp.bfloat16)
        outputs.append(
            jnp.einsum(
                "hqk,khd->qhd", weights, value_rows[:row_stop], preferred_element_type=jnp.float32
            )
        )
        totals.append(peak_score + jnp.log(denom_sum))
    return (jnp.concatenate(outputs, axis=0), jnp.concatenate(totals, axis=1))


def attend_backward(queries, key_rows, value_rows, segments, grad_heads, log_sums, block_len):
    tree_len = queries.shape[0]
    factor = queries.shape[-1] ** (-0.5)
    grad_keys = jnp.zeros(key_rows.shape, jnp.float32)
    grad_values = jnp.zeros(value_rows.shape, jnp.float32)
    grad_queries = []
    for row_start in range(0, tree_len, block_len):
        row_stop = row_start + block_len
        allowed = tree_allowed(segments[row_start:row_stop], segments[:row_stop], row_start)
        scores = block_scores(queries[row_start:row_stop], key_rows[:row_stop], allowed, factor)
        weights = jnp.exp(scores - log_sums[:, row_start:row_stop])
        grad_weights = jnp.einsum(
            "qhd,khd->hqk",
            grad_heads[row_start:row_stop],
            value_rows[:row_stop],
            preferred_element_type=jnp.float32,
        )
        grad_scores = (
            weights * (grad_weights - jnp.sum(weights * grad_weights, axis=-1, keepdims=True))
        ).astype(jnp.bfloat16)
        grad_queries.append(
            jnp.einsum(
                "hqk,khd->qhd", grad_scores, key_rows[:row_stop], preferred_element_type=jnp.float32
            )
            * factor
        )
        grad_keys = grad_keys.at[:row_stop].add(
            jnp.einsum(
                "hqk,qhd->khd",
                grad_scores,
                queries[row_start:row_stop],
                preferred_element_type=jnp.float32,
            )
            * factor
        )
        grad_values = grad_values.at[:row_stop].add(
            jnp.einsum(
                "hqk,qhd->khd",
                weights.astype(jnp.bfloat16),
                grad_heads[row_start:row_stop],
                preferred_element_type=jnp.float32,
            )
        )
    return (jnp.concatenate(grad_queries, axis=0), grad_keys, grad_values)


def gelu_back(hidden, grad_act):
    return jax.vjp(partial(jax.nn.gelu, approximate=True), hidden)[1](grad_act)[0].astype(
        jnp.bfloat16
    )


def plain_body(
    tokens,
    segment,
    route,
    w_qkv,
    bias_qv,
    w_o,
    w_router,
    w_up,
    w_down,
    norm_gains,
    shifts,
    cotangent,
):
    micro_count, local_rows, model_width = tokens.shape
    tree_len = segment.shape[1]
    block_len = min(512, tree_len)
    expert_count = w_up.shape[0]
    tensor_count = lax.axis_size("tensor")
    local_cap = max(2, 3 * local_rows // (2 * expert_count))
    tree_cap = tensor_count * local_cap
    slot_count = expert_count * tree_cap
    position = lax.axis_index("tensor") * local_rows
    gains_all, shifts_all, router_all = (
        lax.all_gather(norm_gains, ("fsdp", "tensor"), axis=1, tiled=True),
        lax.all_gather(shifts, ("fsdp", "tensor"), axis=1, tiled=True),
        lax.all_gather(w_router, ("fsdp", "tensor"), axis=0, tiled=True),
    )
    gains_all = gains_all.astype(jnp.float32)
    shifts_all = shifts_all.astype(jnp.float32)
    router_wide = router_all.astype(jnp.float32)
    qkv_all, bias_all, out_all = (
        lax.all_gather(w_qkv, "fsdp", axis=1, tiled=True),
        lax.all_gather(bias_qv, "fsdp", axis=2, tiled=True),
        lax.all_gather(w_o, "fsdp", axis=1, tiled=True),
    )
    head_width = qkv_all.shape[2]
    head_count = bias_all.shape[1]
    bias_rows = bias_all.reshape(2, head_width).astype(jnp.float32)
    qkv_bias = jnp.stack([bias_rows[0], jnp.zeros_like(bias_rows[0]), bias_rows[1]])
    up_grad = jnp.zeros((expert_count, model_width, w_up.shape[2]), jnp.float32)
    down_grad = jnp.zeros((expert_count, w_down.shape[1], model_width), jnp.float32)
    qkv_grad = jnp.zeros(qkv_all.shape, jnp.float32)
    bias_grad = jnp.zeros((2, head_width), jnp.float32)
    out_grad = jnp.zeros(out_all.shape, jnp.float32)
    router_grad = jnp.zeros(router_wide.shape, jnp.float32)
    gain_grad = jnp.zeros(gains_all.shape, jnp.float32)
    shift_grad = jnp.zeros(shifts_all.shape, jnp.float32)
    expert_ids = jnp.arange(expert_count, dtype=jnp.int32)
    results, input_grads = ([], [])
    for micro_index in range(micro_count):
        segments = segment[micro_index]
        routes_all = route[micro_index, :, 0]
        inputs = tokens[micro_index].astype(jnp.float32)
        normed_in, plain_in, scale_in = norm_rows(inputs, gains_all[0], shifts_all[0])
        normed_tree = lax.all_gather(normed_in.astype(jnp.bfloat16), "tensor", axis=0, tiled=True)
        projected = (
            jnp.einsum("td,jdc->tjc", normed_tree, qkv_all, preferred_element_type=jnp.float32)
            + qkv_bias
        ).astype(jnp.bfloat16)
        queries = projected[:, 0].reshape(tree_len, head_count, -1)
        key_rows = projected[:, 1].reshape(tree_len, head_count, -1)
        value_rows = projected[:, 2].reshape(tree_len, head_count, -1)
        attended, log_sums = attend_forward(queries, key_rows, value_rows, segments, block_len)
        heads_low = attended.reshape(tree_len, head_width).astype(jnp.bfloat16)
        attention_rows = lax.psum_scatter(
            jnp.dot(heads_low, out_all, preferred_element_type=jnp.float32).astype(jnp.bfloat16),
            "tensor",
            scatter_dimension=0,
            tiled=True,
        ).astype(jnp.float32)
        residual = inputs + attention_rows + shifts_all[2]
        normed_mid, plain_mid, scale_mid = norm_rows(residual, gains_all[1], shifts_all[1])
        mid_low = normed_mid.astype(jnp.bfloat16)
        router_probs = jax.nn.softmax(
            jnp.dot(mid_low, router_all, preferred_element_type=jnp.float32), axis=-1
        )
        own_routes = lax.dynamic_slice_in_dim(routes_all, position, local_rows)
        own_choice = own_routes[:, None] == expert_ids[None, :]
        gate_value = jnp.sum(jnp.where(own_choice, router_probs, 0.0), axis=-1)
        grad_final = cotangent[micro_index].astype(jnp.float32)
        grad_returned = (gate_value[:, None] * grad_final).astype(jnp.bfloat16)
        up_all, down_all = (
            lax.all_gather(w_up, "fsdp", axis=1, tiled=True),
            lax.all_gather(w_down, "fsdp", axis=2, tiled=True),
        )
        chosen = routes_all[:, None] == expert_ids[None, :]
        running = jnp.cumsum(chosen.astype(jnp.int32), axis=0)
        slot_index = routes_all * tree_cap + jnp.sum(jnp.where(chosen, running, 0), axis=-1) - 1
        slot_token = (
            jnp.zeros((slot_count,), jnp.int32)
            .at[slot_index]
            .set(jnp.arange(tree_len, dtype=jnp.int32))
        )
        slot_filled = jnp.zeros((slot_count,), jnp.bool_).at[slot_index].set(True)
        mid_tree = lax.all_gather(mid_low, "tensor", axis=0, tiled=True)
        routed = jnp.where(slot_filled[:, None], mid_tree[slot_token], 0).reshape(
            expert_count, tree_cap, model_width
        )
        hidden = jnp.einsum("ecd,edf->ecf", routed, up_all, preferred_element_type=jnp.float32)
        activated = jax.nn.gelu(hidden, approximate=True).astype(jnp.bfloat16)
        expert_rows = jnp.einsum(
            "ecf,efd->ecd", activated, down_all, preferred_element_type=jnp.float32
        ).reshape(slot_count, model_width)
        returned = lax.psum_scatter(
            expert_rows[slot_index].astype(jnp.bfloat16), "tensor", scatter_dimension=0, tiled=True
        ).astype(jnp.float32)
        grad_tree = lax.all_gather(grad_returned, "tensor", axis=0, tiled=True)
        grad_expert = jnp.where(slot_filled[:, None], grad_tree[slot_token], 0).reshape(
            expert_count, tree_cap, model_width
        )
        down_grad = down_grad + jnp.einsum(
            "ecf,ecd->efd", activated, grad_expert, preferred_element_type=jnp.float32
        )
        grad_act = jnp.einsum(
            "ecd,efd->ecf", grad_expert, down_all, preferred_element_type=jnp.float32
        )
        grad_hidden = gelu_back(hidden, grad_act)
        up_grad = up_grad + jnp.einsum(
            "ecd,ecf->edf", routed, grad_hidden, preferred_element_type=jnp.float32
        )
        grad_routed = jnp.einsum(
            "ecf,edf->ecd", grad_hidden, up_all, preferred_element_type=jnp.float32
        ).reshape(slot_count, model_width)
        grad_mid = lax.psum_scatter(
            grad_routed[slot_index].astype(jnp.bfloat16), "tensor", scatter_dimension=0, tiled=True
        ).astype(jnp.float32)
        results.append(
            (residual + gate_value[:, None] * returned + shifts_all[3]).astype(jnp.bfloat16)
        )
        grad_gate = jnp.sum(grad_final * returned, axis=-1)
        grad_logits = router_probs * (
            jnp.where(own_choice, grad_gate[:, None], 0.0) - (gate_value * grad_gate)[:, None]
        )
        router_grad = router_grad + jnp.einsum(
            "td,te->de", mid_low.astype(jnp.float32), grad_logits, precision=HIGHEST
        )
        grad_mid = grad_mid + jnp.einsum("te,de->td", grad_logits, router_wide, precision=HIGHEST)
        grad_from_mid, gain_mid, shift_mid = norm_back(grad_mid, plain_mid, scale_mid, gains_all[1])
        grad_mixed = grad_final + grad_from_mid
        proj_tree = lax.all_gather(grad_mixed.astype(jnp.bfloat16), "tensor", axis=0, tiled=True)
        out_grad = out_grad + jnp.einsum(
            "tc,td->cd", heads_low, proj_tree, preferred_element_type=jnp.float32
        )
        grad_heads = jnp.einsum(
            "td,cd->tc", proj_tree, out_all, preferred_element_type=jnp.float32
        ).astype(jnp.bfloat16)
        grad_queries, grad_keys, grad_values = attend_backward(
            queries,
            key_rows,
            value_rows,
            segments,
            grad_heads.reshape(tree_len, head_count, -1),
            log_sums,
            block_len,
        )
        grad_proj_all = jnp.stack(
            [
                grad_queries.reshape(tree_len, head_width),
                grad_keys.reshape(tree_len, head_width),
                grad_values.reshape(tree_len, head_width),
            ],
            axis=1,
        ).astype(jnp.bfloat16)
        qkv_grad = qkv_grad + jnp.einsum(
            "td,tjc->jdc", normed_tree, grad_proj_all, preferred_element_type=jnp.float32
        )
        bias_grad = bias_grad + jnp.sum(grad_proj_all[:, 0::2].astype(jnp.float32), axis=0)
        grad_normed = lax.psum_scatter(
            jnp.einsum(
                "tjc,jdc->td", grad_proj_all, qkv_all, preferred_element_type=jnp.float32
            ).astype(jnp.bfloat16),
            "tensor",
            scatter_dimension=0,
            tiled=True,
        ).astype(jnp.float32)
        grad_from_in, gain_in, shift_in = norm_back(grad_normed, plain_in, scale_in, gains_all[0])
        input_grads.append(grad_mixed + grad_from_in)
        gain_grad = gain_grad + jnp.stack([gain_in, gain_mid])
        shift_grad = shift_grad + jnp.stack(
            [shift_in, shift_mid, jnp.sum(grad_mixed, axis=0), jnp.sum(grad_final, axis=0)]
        )
    weight_sums = (
        lax.psum_scatter(
            qkv_grad.astype(jnp.bfloat16), "fsdp", scatter_dimension=1, tiled=True
        ).astype(jnp.float32),
        lax.psum_scatter(
            bias_grad.reshape(2, head_count, -1).astype(jnp.bfloat16),
            "fsdp",
            scatter_dimension=2,
            tiled=True,
        ).astype(jnp.float32),
        lax.psum_scatter(
            out_grad.astype(jnp.bfloat16), "fsdp", scatter_dimension=1, tiled=True
        ).astype(jnp.float32),
    )
    up_final, down_final = (
        lax.psum_scatter(
            up_grad.astype(jnp.bfloat16), "fsdp", scatter_dimension=1, tiled=True
        ).astype(jnp.float32),
        lax.psum_scatter(
            down_grad.astype(jnp.bfloat16), "fsdp", scatter_dimension=2, tiled=True
        ).astype(jnp.float32),
    )
    small_sums = (
        lax.psum_scatter(gain_grad, ("fsdp", "tensor"), scatter_dimension=1, tiled=True),
        lax.psum_scatter(shift_grad, ("fsdp", "tensor"), scatter_dimension=1, tiled=True),
        lax.psum_scatter(router_grad, ("fsdp", "tensor"), scatter_dimension=0, tiled=True),
    )
    return (
        jnp.stack(results),
        jnp.stack(input_grads),
        weight_sums[0],
        weight_sums[1],
        weight_sums[2],
        small_sums[2],
        up_final,
        down_final,
        small_sums[0],
        small_sums[1][:3],
        small_sums[1][3],
    )


MESH = pl.DeviceIdType.MESH
BF = jnp.bfloat16
F32 = jnp.float32


def fits(mesh):
    return mesh.shape["fsdp"] == 8 and mesh.shape["tensor"] == 4


def flip(index, bit):
    return index + bit * (1 - 2 * (lax.rem(index // bit, 2)))


def place(fsdp, tensor):
    return {"fsdp": fsdp, "tensor": tensor}


def greet(partners):
    barrier = pltpu.get_barrier_semaphore()
    for fsdp, tensor in partners:
        pl.semaphore_signal(barrier, inc=1, device_id=place(fsdp, tensor), device_id_type=MESH)
    pl.semaphore_wait(barrier, len(partners))


def greet_all(mine):
    barrier = pltpu.get_barrier_semaphore()

    def signal(step, carry):
        other = lax.rem(mine + step, 32)
        pl.semaphore_signal(
            barrier, inc=1, device_id=place(other // 4, lax.rem(other, 4)), device_id_type=MESH
        )
        return carry

    lax.fori_loop(1, 32, signal, 0)
    pl.semaphore_wait(barrier, 31)


class Sender:
    def __init__(self, send_sem, recv_sem):
        self.send_sem, self.recv_sem, self.count = send_sem, recv_sem, 0
        self.open = []

    def copy(self, source, target, fsdp, tensor):
        made = pltpu.make_async_remote_copy(
            src_ref=source,
            dst_ref=target,
            send_sem=self.send_sem.at[self.count],
            recv_sem=self.recv_sem.at[self.count],
            device_id=place(fsdp, tensor),
            device_id_type=MESH,
        )
        self.count += 1
        made.start()
        self.open.append(made)
        return made

    def finish(self):
        for made in self.open:
            made.wait_send()


def gather_kernel(
    w4, small, tokens, up, down, full4, small_all, trunk, halo, up_own, down_own,
    send_sem, recv_sem, local_sem, up_send, up_recv, down_send, down_recv, trunk_send, trunk_recv,
):
    me_f, me_z = lax.axis_index("fsdp"), lax.axis_index("tensor")
    mine = me_f * 4 + me_z
    core = lax.rem(me_f, 2)
    greet_all(mine)
    sender = Sender(send_sem, recv_sem)

    def rows(fsdp):
        return pl.ds(pl.multiple_of(fsdp * 128, 128), 128)

    def cols(first, width):
        return pl.ds(pl.multiple_of(first * 256, 256), width)

    local = [
        pltpu.make_async_copy(w4, full4.at[:, rows(me_f), cols(me_z, 256)], local_sem.at[0]),
        pltpu.make_async_copy(small, small_all.at[me_f, me_z], local_sem.at[1]),
    ]
    for copy in local:
        copy.start()
    first = [
        sender.copy(w4, full4.at[:, rows(me_f), cols(me_z, 256)], me_f, flip(me_z, 1)),
        sender.copy(small, small_all.at[me_f, me_z], me_f, flip(me_z, 1)),
    ]

    piece = [(micro, half) for micro in range(2) for half in range(2)]

    def trunk_copy(index, source):
        micro, half = piece[index]
        return pltpu.make_async_remote_copy(
            src_ref=source.at[micro, pl.ds(half * 128, 128)],
            dst_ref=trunk.at[micro, pl.ds(half * 128, 128)],
            send_sem=trunk_send.at[index],
            recv_sem=trunk_recv.at[index],
            device_id=place(me_f, lax.rem(me_z + 1, 4)),
            device_id_type=MESH,
        )

    halo_copy = pltpu.make_async_remote_copy(
        src_ref=tokens.at[:, pl.ds(128, 128)],
        dst_ref=halo,
        send_sem=trunk_send.at[4],
        recv_sem=trunk_recv.at[4],
        device_id=place(me_f, lax.rem(me_z + 1, 4)),
        device_id_type=MESH,
    )

    @pl.when(me_z == 0)
    def _():
        for index in range(4):
            trunk_copy(index, tokens).start()

    @pl.when(me_z < 3)
    def _():
        halo_copy.start()

    def expert_copies(step):
        other = lax.rem(mine + step, 32)
        fsdp, tensor = other // 4, lax.rem(other, 4)
        expert = 2 * tensor + fsdp // 4
        quarter = pl.ds(pl.multiple_of(lax.rem(fsdp, 4) * 256, 256), 256)
        return (
            (up.at[expert, :, quarter], up_own.at[rows(me_f), cols(me_z, 256)]),
            (down.at[expert, quarter, :], down_own.at[cols(me_z, 256), rows(me_f)]),
            (fsdp, tensor),
        )

    def remote(step):
        ups, downs, (fsdp, tensor) = expert_copies(step)
        return [
            pltpu.make_async_remote_copy(
                src_ref=pair[0], dst_ref=pair[1], send_sem=sems[0].at[step],
                recv_sem=sems[1].at[step], device_id=place(fsdp, tensor), device_id_type=MESH,
            )
            for pair, sems in ((ups, (up_send, up_recv)), (downs, (down_send, down_recv)))
        ]

    def start_step(step, carry):
        for copy in remote(step):
            copy.start()
        return carry

    lax.fori_loop(1, 32, start_step, 0)
    ups, downs, _ = expert_copies(0)
    own = [
        pltpu.make_async_copy(ups[0], ups[1], local_sem.at[2]),
        pltpu.make_async_copy(downs[0], downs[1], local_sem.at[3]),
    ]
    for copy in own:
        copy.start()

    for copy in first:
        copy.wait_recv()
    for copy in local:
        copy.wait()
    pair = me_z // 2 * 2
    second = [
        sender.copy(
            full4.at[:, rows(me_f), cols(pair, 512)], full4.at[:, rows(me_f), cols(pair, 512)],
            me_f, flip(me_z, 2),
        ),
        sender.copy(
            small_all.at[me_f, pl.ds(pair, 2)], small_all.at[me_f, pl.ds(pair, 2)],
            me_f, flip(me_z, 2),
        ),
    ]
    for copy in second:
        copy.wait_recv()

    across = flip(me_f, 2) * (1 - core) + flip(me_f, 4) * core
    along = flip(me_f, 4) * (1 - core) + flip(me_f, 2) * core

    def blocks(fsdp_list, target):
        made = []
        for fsdp in fsdp_list:
            made.append(sender.copy(full4.at[:, rows(fsdp)], full4.at[:, rows(fsdp)], target, me_z))
            made.append(sender.copy(small_all.at[fsdp], small_all.at[fsdp], target, me_z))
        for copy in made:
            copy.wait_recv()

    blocks([me_f], across)
    blocks([me_f, across], along)
    blocks([core, core + 2, core + 4, core + 6], flip(me_f, 1))

    for index in range(4):
        @pl.when(me_z > 0)
        def _(index=index):
            trunk_copy(index, trunk).wait_recv()

        @pl.when((me_z > 0) & (me_z < 3))
        def _(index=index):
            trunk_copy(index, trunk).start()

    @pl.when(me_z > 0)
    def _():
        halo_copy.wait_recv()

    @pl.when(me_z == 0)
    def _():
        keep = [
            pltpu.make_async_copy(tokens, trunk, local_sem.at[0]),
            pltpu.make_async_copy(tokens.at[:, pl.ds(128, 128)], halo, local_sem.at[1]),
        ]
        for copy in keep:
            copy.start()
        for copy in keep:
            copy.wait()

    @pl.when(me_z < 3)
    def _():
        for index in range(4):
            trunk_copy(index, trunk).wait_send()
        halo_copy.wait_send()

    for copy in own:
        copy.wait()

    def end_step(step, carry):
        for copy in remote(step):
            copy.wait_send()
            copy.wait_recv()
        return carry

    lax.fori_loop(1, 32, end_step, 0)
    sender.finish()


def any_spec(count):
    return [pl.BlockSpec(memory_space=pl.ANY)] * count


def gather_all(w4, small, tokens, up, down):
    shapes = [
        jax.ShapeDtypeStruct((4, 1024, 1024), BF),
        jax.ShapeDtypeStruct((8, 4, 16, 128), BF),
        jax.ShapeDtypeStruct((2, 256, 1024), BF),
        jax.ShapeDtypeStruct((2, 128, 1024), BF),
        jax.ShapeDtypeStruct((1024, 1024), BF),
        jax.ShapeDtypeStruct((1024, 1024), BF),
    ]
    dma = pltpu.SemaphoreType.DMA
    return pl.pallas_call(
        gather_kernel,
        out_shape=shapes,
        in_specs=any_spec(5),
        out_specs=any_spec(6),
        scratch_shapes=[
            dma((20,)), dma((20,)), dma((4,)),
            dma((32,)), dma((32,)), dma((32,)), dma((32,)), dma((5,)), dma((5,)),
        ],
        compiler_params=pltpu.CompilerParams(collective_id=0, has_side_effects=True),
        name="gather_all",
    )(w4, small, tokens, up, down)


def dispatch_kernel(slots, arrived, send_sem, recv_sem, local_sem):
    me_f, me_z = lax.axis_index("fsdp"), lax.axis_index("tensor")
    me_y, me_x, core = me_f // 4, lax.rem(me_f // 2, 2), lax.rem(me_f, 2)
    partners = [(flip(me_f, 2), me_z), (flip(me_f, 1), me_z)]
    for step in range(1, 8):
        partners.append(
            (lax.rem(me_y + step // 4, 2) * 4 + lax.rem(me_f, 4), lax.rem(me_z + step, 4))
        )
    greet(partners)
    sender = Sender(send_sem, recv_sem)
    origin = me_y * 4 + me_z
    first = []
    for kind in range(2):
        made = []
        for fsdp, tensor in partners[2:]:
            made.append(
                sender.copy(
                    slots.at[kind, 2 * tensor + fsdp // 4],
                    arrived.at[kind, me_x, core, origin],
                    fsdp, tensor,
                )
            )
        own = pltpu.make_async_copy(
            slots.at[kind, 2 * me_z + me_y], arrived.at[kind, me_x, core, origin], local_sem.at[kind]
        )
        own.start()
        made.append(own)
        first.append(made)
    second = []
    for kind in range(2):
        for copy in first[kind][:-1]:
            copy.wait_recv()
        first[kind][-1].wait()
        second.append(
            sender.copy(
                arrived.at[kind, me_x, core], arrived.at[kind, me_x, core], flip(me_f, 2), me_z
            )
        )
    third = []
    for kind in range(2):
        second[kind].wait_recv()
        third.append(
            sender.copy(
                arrived.at[kind, :, core], arrived.at[kind, :, core], flip(me_f, 1), me_z
            )
        )
    for copy in third:
        copy.wait_recv()
    sender.finish()


def dispatch(slots, cap):
    dma = pltpu.SemaphoreType.DMA
    return pl.pallas_call(
        dispatch_kernel,
        out_shape=jax.ShapeDtypeStruct((2, 2, 2, 8, 2, cap, 1024), BF),
        in_specs=any_spec(1),
        out_specs=pl.BlockSpec(memory_space=pl.ANY),
        scratch_shapes=[dma((18,)), dma((18,)), dma((2,))],
        compiler_params=pltpu.CompilerParams(collective_id=1, has_side_effects=True),
        name="dispatch",
    )(slots)


def add_into(target, source, count):
    def step(index, carry):
        target[index] = (target[index].astype(F32) + source[index].astype(F32)).astype(BF)
        return carry

    lax.fori_loop(0, count, step, 0)


def combine_kernel(parts, returned, own, got, got_x, send_sem, recv_sem, local_sem):
    me_f, me_z = lax.axis_index("fsdp"), lax.axis_index("tensor")
    me_y, me_x, core = me_f // 4, lax.rem(me_f // 2, 2), lax.rem(me_f, 2)
    partners = [(flip(me_f, 2), me_z), (flip(me_f, 1), me_z)]
    for step in range(1, 8):
        partners.append(
            (lax.rem(me_y + step // 4, 2) * 4 + lax.rem(me_f, 4), lax.rem(me_z + step, 4))
        )
    greet(partners)
    sender = Sender(send_sem, recv_sem)
    first, keep = [], []
    for kind in range(2):
        first.append(
            sender.copy(parts.at[kind, :, 1 - core], got.at[kind], flip(me_f, 1), me_z)
        )
        copy = pltpu.make_async_copy(parts.at[kind, :, core], own.at[kind], local_sem.at[kind])
        copy.start()
        keep.append(copy)
    second = []
    for kind in range(2):
        keep[kind].wait()
        first[kind].wait_recv()
        for side in range(2):
            add_into(own.at[kind, side], got.at[kind, side], 16)
        second.append(
            sender.copy(own.at[kind, 1 - me_x], got_x.at[kind], flip(me_f, 2), me_z)
        )
    last = []
    for kind in range(2):
        second[kind].wait_recv()
        add_into(own.at[kind, me_x], got_x.at[kind], 16)
        for fsdp, tensor in partners[2:]:
            back = fsdp // 4 * 4 + tensor
            last.append(
                sender.copy(
                    own.at[kind, me_x, pl.ds(back * 2, 2)],
                    returned.at[kind, 2 * me_z + me_y],
                    fsdp, tensor,
                )
            )
        copy = pltpu.make_async_copy(
            own.at[kind, me_x, pl.ds((me_y * 4 + me_z) * 2, 2)],
            returned.at[kind, 2 * me_z + me_y],
            local_sem.at[kind],
        )
        copy.start()
        keep.append(copy)
    for copy in last:
        copy.wait_recv()
    for copy in keep[2:]:
        copy.wait()
    sender.finish()


def combine(parts, cap):
    dma = pltpu.SemaphoreType.DMA
    return pl.pallas_call(
        combine_kernel,
        out_shape=jax.ShapeDtypeStruct((2, 8, 2, cap, 1024), BF),
        in_specs=any_spec(1),
        out_specs=pl.BlockSpec(memory_space=pl.ANY),
        scratch_shapes=[
            pltpu.VMEM((2, 2, 16, cap, 1024), BF),
            pltpu.VMEM((2, 2, 16, cap, 1024), BF),
            pltpu.VMEM((2, 16, cap, 1024), BF),
            dma((18,)), dma((18,)), dma((2,)),
        ],
        compiler_params=pltpu.CompilerParams(
            collective_id=2, has_side_effects=True, vmem_limit_bytes=48 << 20
        ),
        name="combine",
    )(parts)


def scatter_kernel(
    up_grad, down_grad, grad4, small, trunk, halo,
    up_out, down_out, out4, small_out, trunk_out, halo_out,
    keep, got, cut, cut_got, cut_a, cut_got_a, small_got, trunk_got, trunk_own,
    send_sem, recv_sem, local_sem, up_send, up_recv, down_send, down_recv,
    small_send, small_recv, trunk_send, trunk_recv,
):
    me_f, me_z = lax.axis_index("fsdp"), lax.axis_index("tensor")
    mine = me_f * 4 + me_z
    core = lax.rem(me_f, 2)
    me_y, me_x = me_f // 4, lax.rem(me_f // 2, 2)
    greet_all(mine)
    sender = Sender(send_sem, recv_sem)

    def rows(fsdp):
        return pl.ds(pl.multiple_of(fsdp * 128, 128), 128)

    def cols(first, width):
        return pl.ds(pl.multiple_of(first * 256, 256), width)

    first = []
    for block in range(4):
        first.append(
            sender.copy(
                grad4.at[:, rows(2 * block + 1 - core)], got.at[block], flip(me_f, 1), me_z
            )
        )
    local = []
    for block in range(4):
        copy = pltpu.make_async_copy(
            grad4.at[:, rows(2 * block + core)], keep.at[block], local_sem.at[block]
        )
        copy.start()
        local.append(copy)
    own_trunk = pltpu.make_async_copy(trunk, trunk_own, local_sem.at[4])
    own_trunk.start()

    def trunk_copy(index, source):
        return pltpu.make_async_remote_copy(
            src_ref=source.at[index],
            dst_ref=trunk_got.at[index],
            send_sem=trunk_send.at[index],
            recv_sem=trunk_recv.at[index],
            device_id=place(me_f, lax.rem(me_z + 3, 4)),
            device_id_type=MESH,
        )

    halo_copy = pltpu.make_async_remote_copy(
        src_ref=halo,
        dst_ref=halo_out,
        send_sem=trunk_send.at[4],
        recv_sem=trunk_recv.at[4],
        device_id=place(me_f, lax.rem(me_z + 3, 4)),
        device_id_type=MESH,
    )

    @pl.when(me_z == 3)
    def _():
        for index in range(4):
            trunk_copy(index, trunk).start()

    @pl.when(me_z > 0)
    def _():
        halo_copy.start()

    def small_copy(step):
        other = lax.rem(mine + step, 32)
        return pltpu.make_async_remote_copy(
            src_ref=small.at[other], dst_ref=small_got.at[mine], send_sem=small_send.at[step],
            recv_sem=small_recv.at[step], device_id=place(other // 4, lax.rem(other, 4)),
            device_id_type=MESH,
        )

    def expert_copies(step):
        other = lax.rem(mine + step, 32)
        fsdp, tensor = other // 4, lax.rem(other, 4)
        expert = 2 * me_z + me_y
        quarter = pl.ds(pl.multiple_of(lax.rem(me_f, 4) * 256, 256), 256)
        return (
            (up_grad.at[rows(fsdp), cols(tensor, 256)], up_out.at[expert, :, quarter]),
            (down_grad.at[cols(tensor, 256), rows(fsdp)], down_out.at[expert, quarter, :]),
            (fsdp, tensor),
        )

    def remote(step):
        ups, downs, (fsdp, tensor) = expert_copies(step)
        return [
            pltpu.make_async_remote_copy(
                src_ref=pair[0], dst_ref=pair[1], send_sem=sems[0].at[step],
                recv_sem=sems[1].at[step], device_id=place(fsdp, tensor), device_id_type=MESH,
            )
            for pair, sems in ((ups, (up_send, up_recv)), (downs, (down_send, down_recv)))
        ]

    def start_step(step, carry):
        small_copy(step).start()
        for copy in remote(step):
            copy.start()
        return carry

    lax.fori_loop(1, 32, start_step, 0)
    ups, downs, _ = expert_copies(0)
    own = [
        pltpu.make_async_copy(ups[0], ups[1], local_sem.at[5]),
        pltpu.make_async_copy(downs[0], downs[1], local_sem.at[6]),
        pltpu.make_async_copy(small.at[mine], small_got.at[mine], local_sem.at[7]),
    ]
    for copy in own:
        copy.start()

    def add_block(target, source):
        def step(index, carry):
            part = pl.ds(pl.multiple_of(index * 16, 16), 16)
            for which in range(4):
                target[which, part] = (
                    target[which, part].astype(F32) + source[which, part].astype(F32)
                ).astype(BF)
            return carry

        lax.fori_loop(0, 8, step, 0)

    for block in range(4):
        local[block].wait()
        first[block].wait_recv()
        add_block(keep.at[block], got.at[block])

    along = flip(me_f, 4) * (1 - core) + flip(me_f, 2) * core
    across = flip(me_f, 2) * (1 - core) + flip(me_f, 4) * core

    def block_of(fsdp):
        return fsdp // 2

    sent = [along, along * 0 + flip(across, 4) * (1 - core) + flip(across, 2) * core]
    kept = [me_f, across]
    second = []
    for index in range(2):
        second.append(
            sender.copy(keep.at[block_of(sent[index])], cut.at[index], along, me_z)
        )
    for index in range(2):
        second[index].wait_recv()
        add_block(keep.at[block_of(kept[index])], cut.at[index])
    third = sender.copy(keep.at[block_of(across)], cut_got, across, me_z)
    third.wait_recv()
    add_block(keep.at[block_of(me_f)], cut_got)
    mine4 = keep.at[block_of(me_f)]
    pair = me_z // 2 * 2
    other_pair = 2 - pair
    fourth = sender.copy(mine4.at[:, :, cols(other_pair, 512)], cut_a, me_f, flip(me_z, 2))
    fourth.wait_recv()

    def add_cols(source, begin, width, low):
        def step(index, carry):
            part = pl.ds(pl.multiple_of(index * 16, 16), 16)
            for which in range(4):
                mine4[which, part, cols(begin, width)] = (
                    mine4[which, part, cols(begin, width)].astype(F32)
                    + source[which, part, :].astype(F32)
                ).astype(BF)
            return carry

        lax.fori_loop(0, 8, step, 0)

    add_cols(cut_a, pair, 512, 0)
    fifth = sender.copy(
        mine4.at[:, :, cols(flip(me_z, 1), 256)], cut_got_a, me_f, flip(me_z, 1)
    )
    fifth.wait_recv()
    add_cols(cut_got_a, me_z, 256, 0)
    last = pltpu.make_async_copy(mine4.at[:, :, cols(me_z, 256)], out4, local_sem.at[0])
    last.start()

    own_trunk.wait()
    for index in range(4):
        @pl.when(me_z < 3)
        def _(index=index):
            trunk_copy(index, trunk_own).wait_recv()

            def step(row, carry):
                part = pl.ds(pl.multiple_of(row * 16, 16), 16)
                trunk_own[index, part] = (
                    trunk_own[index, part].astype(F32) + trunk_got[index, part].astype(F32)
                ).astype(BF)
                return carry

            lax.fori_loop(0, 8, step, 0)

        @pl.when((me_z > 0) & (me_z < 3))
        def _(index=index):
            trunk_copy(index, trunk_own).start()

    @pl.when(me_z > 0)
    def _():
        for index in range(4):
            trunk_copy(index, trunk_own).wait_send()
        halo_copy.wait_send()

    @pl.when(me_z < 3)
    def _():
        halo_copy.wait_recv()

    trunk_done = pltpu.make_async_copy(trunk_own, trunk_out, local_sem.at[1])
    trunk_done.start()
    for copy in own:
        copy.wait()

    def end_small(step, carry):
        copy = small_copy(step)
        copy.wait_send()
        copy.wait_recv()
        return carry

    lax.fori_loop(1, 32, end_small, 0)

    def sum_small(index, total):
        return total + small_got[index]

    small_out[...] = lax.fori_loop(1, 32, sum_small, small_got[0])

    def end_step(step, carry):
        for copy in remote(step):
            copy.wait_send()
            copy.wait_recv()
        return carry

    lax.fori_loop(1, 32, end_step, 0)
    sender.finish()
    last.wait()
    trunk_done.wait()


def scatter_all(up_grad, down_grad, grad4, small, trunk, halo):
    dma = pltpu.SemaphoreType.DMA
    shapes = [
        jax.ShapeDtypeStruct((8, 128, 1024), BF),
        jax.ShapeDtypeStruct((8, 1024, 128), BF),
        jax.ShapeDtypeStruct((4, 128, 256), BF),
        jax.ShapeDtypeStruct((16, 128), F32),
        jax.ShapeDtypeStruct((4, 128, 1024), BF),
        jax.ShapeDtypeStruct((2, 128, 1024), BF),
    ]
    specs = any_spec(6)
    specs[3] = pl.BlockSpec(memory_space=pltpu.VMEM)
    return pl.pallas_call(
        scatter_kernel,
        out_shape=shapes,
        in_specs=any_spec(6),
        out_specs=specs,
        scratch_shapes=[
            pltpu.VMEM((4, 4, 128, 1024), BF),
            pltpu.VMEM((4, 4, 128, 1024), BF),
            pltpu.VMEM((2, 4, 128, 1024), BF),
            pltpu.VMEM((4, 128, 1024), BF),
            pltpu.VMEM((4, 128, 512), BF),
            pltpu.VMEM((4, 128, 256), BF),
            pltpu.VMEM((32, 16, 128), F32),
            pltpu.VMEM((4, 128, 1024), BF),
            pltpu.VMEM((4, 128, 1024), BF),
            dma((10,)), dma((10,)), dma((8,)),
            dma((32,)), dma((32,)), dma((32,)), dma((32,)),
            dma((32,)), dma((32,)), dma((5,)), dma((5,)),
        ],
        compiler_params=pltpu.CompilerParams(
            collective_id=3, has_side_effects=True, vmem_limit_bytes=48 << 20
        ),
        name="scatter_all",
    )(up_grad, down_grad, grad4, small, trunk, halo)


def fast_body(
    tokens, segment, route, w_qkv, bias_qv, w_o, w_router, w_up, w_down, norm_gains, shifts, cotangent
):
    micro_count, local_rows, width = tokens.shape
    expert_count = w_up.shape[0]
    cap = 3 * local_rows // (2 * expert_count)
    me_z = lax.axis_index("tensor")
    start = me_z * local_rows
    small = jnp.concatenate(
        [norm_gains, shifts, w_router.T, bias_qv.reshape(2, 32)], axis=0
    )
    small = jnp.pad(small, ((0, 0), (0, 96)))
    w4 = jnp.concatenate([w_qkv, w_o.T[None]], axis=0)
    full4, small_all, trunk, halo, up_own, down_own = gather_all(w4, small, tokens, w_up, w_down)
    flat_small = small_all[..., :32].transpose(2, 0, 1, 3).reshape(16, width)
    gains = flat_small[:2].astype(F32)
    offsets = flat_small[2:6].astype(F32)
    router_t = flat_small[6:14]
    biases = (
        small_all[:, :, 14:16, :32].reshape(8, 4, 2, 4, 8).transpose(2, 1, 3, 0, 4).reshape(2, width)
    ).astype(F32)

    inputs = tokens.astype(F32)
    with_keys = jnp.concatenate([trunk.astype(F32), halo.astype(F32), inputs], axis=1)
    normed_all, plain_all, scale_all = norm_rows(with_keys, gains[0], offsets[0])
    normed_all = normed_all.astype(BF)
    normed_own = normed_all[:, 384:]
    plain_in, scale_in = plain_all[:, 384:], scale_all[:, 384:]
    queries = (
        jnp.einsum("mrd,dc->mrc", normed_own, full4[0], preferred_element_type=F32) + biases[0]
    ).astype(BF)
    keys = jnp.einsum("mrd,dc->mrc", normed_all, full4[1], preferred_element_type=F32).astype(BF)
    values = (
        jnp.einsum("mrd,dc->mrc", normed_all, full4[2], preferred_element_type=F32) + biases[1]
    ).astype(BF)
    own_index = start + jnp.arange(local_rows)
    key_index = jnp.concatenate([jnp.arange(256), start - 128 + jnp.arange(128), own_index])
    key_part = jnp.arange(640) < 256
    own_segs = lax.dynamic_slice_in_dim(segment, start, local_rows, axis=1)
    halo_segs = lax.dynamic_slice_in_dim(segment, jnp.maximum(start - 128, 0), 128, axis=1)
    key_segs = jnp.concatenate([segment[:, :256], halo_segs, own_segs], axis=1)
    query_seg, key_seg = own_segs[:, :, None], key_segs[:, None, :]
    allowed = (
        (key_seg == 0)
        | (key_seg == query_seg)
        | (query_seg >= 5) & (key_seg == (query_seg - 5) // 2 + 1)
    )
    allowed = allowed & (key_part | (key_index >= 256))[None, None, :]
    allowed = allowed & (key_index[None, :] <= own_index[:, None])[None]
    heads = (micro_count, -1, 16, 64)
    queries_h, keys_h, values_h = queries.reshape(heads), keys.reshape(heads), values.reshape(heads)
    scores = jnp.einsum("mqhd,mkhd->mhqk", queries_h, keys_h, preferred_element_type=F32) * 0.125
    scores = jnp.where(allowed[:, None], scores, MASKED)
    probs = jax.nn.softmax(scores, axis=-1)
    probs_low = probs.astype(BF)
    heads_low = (
        jnp.einsum("mhqk,mkhd->mqhd", probs_low, values_h, preferred_element_type=F32)
        .astype(BF)
        .reshape(micro_count, local_rows, width)
    )
    attention_rows = jnp.einsum("mrc,dc->mrd", heads_low, full4[3], preferred_element_type=F32)
    residual = inputs + attention_rows + offsets[2]
    normed_mid, plain_mid, scale_mid = norm_rows(residual, gains[1], offsets[1])
    mid_low = normed_mid.astype(BF)
    router_probs = jax.nn.softmax(
        jnp.einsum("mrd,ed->mre", mid_low, router_t, preferred_element_type=F32), axis=-1
    )
    own_routes = lax.dynamic_slice_in_dim(route[:, :, 0], start, local_rows, axis=1)
    own_choice = own_routes[:, :, None] == jnp.arange(expert_count)
    gate = jnp.sum(jnp.where(own_choice, router_probs, 0.0), axis=-1)
    grad_final = cotangent.astype(F32)
    grad_returned = (gate[..., None] * grad_final).astype(BF)
    running = jnp.cumsum(own_choice.astype(jnp.int32), axis=1)
    slot = own_routes * cap + jnp.sum(jnp.where(own_choice, running, 0), axis=-1) - 1
    pick = (slot[:, None, :] == jnp.arange(expert_count * cap)[None, :, None]).astype(BF)
    sending = jnp.stack([mid_low, grad_returned])
    slots = (
        jnp.einsum("msr,kmrd->kmsd", pick, sending, preferred_element_type=F32)
        .astype(BF)
        .reshape(2, micro_count, expert_count, cap, width)
        .transpose(0, 2, 1, 3, 4)
    )
    arrived = dispatch(slots, cap).reshape(2, -1, width)
    routed, grad_expert = arrived[0], arrived[1]
    hidden = jnp.dot(routed, up_own, preferred_element_type=F32)
    activated = jax.nn.gelu(hidden, approximate=True).astype(BF)
    expert_rows = jnp.dot(activated, down_own, preferred_element_type=F32).astype(BF)
    down_grad = jnp.einsum("rf,rd->fd", activated, grad_expert, preferred_element_type=F32).astype(BF)
    grad_act = jnp.einsum("rd,fd->rf", grad_expert, down_own, preferred_element_type=F32)
    grad_hidden = gelu_back(hidden, grad_act)
    up_grad = jnp.einsum("rd,rf->df", routed, grad_hidden, preferred_element_type=F32).astype(BF)
    grad_routed = jnp.einsum("rf,df->rd", grad_hidden, up_own, preferred_element_type=F32).astype(BF)
    parts = jnp.stack([expert_rows, grad_routed]).reshape(2, 2, 2, 16, cap, width)
    back = (
        combine(parts, cap).transpose(0, 2, 1, 3, 4).reshape(2, micro_count, expert_count * cap, width)
    )
    rows_back = jnp.einsum("msr,kmsd->kmrd", pick, back, preferred_element_type=F32)
    returned, grad_mid = rows_back[0], rows_back[1]
    output = (residual + gate[..., None] * returned + offsets[3]).astype(BF)
    grad_gate = jnp.sum(grad_final * returned, axis=-1)
    grad_logits = router_probs * (
        jnp.where(own_choice, grad_gate[..., None], 0.0) - (gate * grad_gate)[..., None]
    )
    router_grad = jnp.einsum(
        "mrd,mre->ed", mid_low.astype(F32), grad_logits, precision=HIGHEST
    )
    grad_mid = grad_mid + jnp.einsum(
        "mre,ed->mrd", grad_logits, router_t.astype(F32), precision=HIGHEST
    )

    def flat(value):
        return value.reshape(-1, value.shape[-1])

    grad_from_mid, gain_mid, shift_mid = norm_back(
        flat(grad_mid), flat(plain_mid), flat(scale_mid), gains[1]
    )
    grad_mixed = grad_final + grad_from_mid.reshape(grad_final.shape)
    proj = grad_mixed.astype(BF)
    out_grad_t = jnp.einsum("mrd,mrc->dc", proj, heads_low, preferred_element_type=F32)
    grad_heads = jnp.einsum("mrd,dc->mrc", proj, full4[3], preferred_element_type=F32).astype(BF)
    grad_heads_h = grad_heads.reshape(heads)
    grad_probs = jnp.einsum("mqhd,mkhd->mhqk", grad_heads_h, values_h, preferred_element_type=F32)
    grad_scores = (
        probs * (grad_probs - jnp.sum(probs * grad_probs, axis=-1, keepdims=True))
    ).astype(BF)
    grad_queries = (
        jnp.einsum("mhqk,mkhd->mqhd", grad_scores, keys_h, preferred_element_type=F32) * 0.125
    ).astype(BF).reshape(micro_count, -1, width)
    grad_keys = (
        jnp.einsum("mhqk,mqhd->mkhd", grad_scores, queries_h, preferred_element_type=F32) * 0.125
    ).astype(BF).reshape(micro_count, -1, width)
    grad_values = (
        jnp.einsum("mhqk,mqhd->mkhd", probs_low, grad_heads_h, preferred_element_type=F32)
    ).astype(BF).reshape(micro_count, -1, width)
    grad4 = jnp.stack([
        jnp.einsum("mrd,mrc->dc", normed_own, grad_queries, preferred_element_type=F32).astype(BF),
        jnp.einsum("mrd,mrc->dc", normed_all, grad_keys, preferred_element_type=F32).astype(BF),
        jnp.einsum("mrd,mrc->dc", normed_all, grad_values, preferred_element_type=F32).astype(BF),
        out_grad_t.astype(BF),
    ])
    bias_grad = jnp.stack([
        jnp.sum(grad_queries.astype(F32), axis=(0, 1)),
        jnp.sum(grad_values.astype(F32), axis=(0, 1)),
    ])
    grad_all = jnp.einsum(
        "mrc,dc->mrd", grad_keys, full4[1], preferred_element_type=F32
    ) + jnp.einsum("mrc,dc->mrd", grad_values, full4[2], preferred_element_type=F32)
    grad_own = grad_all[:, 384:] + jnp.einsum(
        "mrc,dc->mrd", grad_queries, full4[0], preferred_element_type=F32
    )
    early = jnp.concatenate([
        jnp.stack([jnp.zeros((width,), F32), gain_mid]),
        jnp.stack([
            jnp.zeros((width,), F32), shift_mid,
            jnp.sum(grad_mixed, axis=(0, 1)), jnp.sum(grad_final, axis=(0, 1)),
        ]),
        router_grad,
    ])
    plain_halo, plain_trunk = plain_all[:, 256:384], plain_all[:, :256]
    grad_trunk, grad_halo = grad_all[:, :256], grad_all[:, 256:384]
    early = early.at[0].set(
        jnp.sum(grad_all * plain_all, axis=(0, 1))
        + jnp.sum((grad_own - grad_all[:, 384:]) * plain_in, axis=(0, 1))
    )
    early = early.at[2].set(
        jnp.sum(grad_all, axis=(0, 1)) + jnp.sum(grad_own - grad_all[:, 384:], axis=(0, 1))
    )
    small_grad = early.reshape(14, 32, 32).transpose(1, 0, 2)
    bias_small = (
        bias_grad.reshape(2, 4, 4, 8, 8).transpose(3, 1, 0, 2, 4).reshape(32, 2, 32)
    )
    small_grad = jnp.pad(
        jnp.concatenate([small_grad, bias_small], axis=1), ((0, 0), (0, 0), (0, 96))
    )
    up_out, down_out, out4, small_out, trunk_sum, halo_sum = scatter_all(
        up_grad, down_grad, grad4, small_grad,
        grad_trunk.astype(BF).reshape(4, 128, width), grad_halo.astype(BF),
    )
    trunk_sum = trunk_sum.reshape(2, 256, width).astype(F32)
    grad_normed = grad_own + jnp.where(me_z == 0, trunk_sum, 0.0)
    grad_normed = grad_normed.at[:, 128:].add(jnp.where(me_z < 3, halo_sum.astype(F32), 0.0))
    grad_from_in, _, _ = norm_back(flat(grad_normed), flat(plain_in), flat(scale_in), gains[0])
    input_grad = grad_mixed + grad_from_in.reshape(grad_mixed.shape)
    small_out = small_out[:, :32]
    return (
        output,
        input_grad,
        out4[:3].astype(F32),
        small_out[14:16].reshape(2, 4, 8),
        out4[3].T.astype(F32),
        small_out[6:14].T,
        up_out.astype(F32),
        down_out.astype(F32),
        small_out[:2],
        small_out[2:5],
        small_out[5],
    )


def solution(mesh):
    placed = (
        P(None, ("fsdp", "tensor"), None),
        P(None, "fsdp"),
        P(None, "fsdp", None),
        P(None, "fsdp", "tensor"),
        P(None, "tensor", "fsdp"),
        P("tensor", "fsdp"),
        P(("fsdp", "tensor"), None),
        P(None, "fsdp", "tensor"),
        P(None, "tensor", "fsdp"),
        P(None, ("fsdp", "tensor")),
        P(None, ("fsdp", "tensor")),
        P(None, ("fsdp", "tensor"), None),
    )
    return jax.shard_map(
        fast_body if fits(mesh) else plain_body,
        mesh=mesh,
        in_specs=placed,
        out_specs=(
            P(None, ("fsdp", "tensor"), None),
            P(None, ("fsdp", "tensor"), None),
            P(None, "fsdp", "tensor"),
            P(None, "tensor", "fsdp"),
            P("tensor", "fsdp"),
            P(("fsdp", "tensor"), None),
            P(None, "fsdp", "tensor"),
            P(None, "tensor", "fsdp"),
            P(None, ("fsdp", "tensor")),
            P(None, ("fsdp", "tensor")),
            P(("fsdp", "tensor")),
        ),
        check_vma=False,
    )
```

```python
from functools import partial

import jax
import jax.numpy as jnp
from jax import lax
from jax.experimental import pallas as pl
from jax.experimental.pallas import tpu as pltpu
from jax.sharding import PartitionSpec as P

EPSILON = 1e-05
MASKED = -1e30
HIGHEST = lax.Precision.HIGHEST


def norm_rows(row_data, gain_row, shift_row):
    centered = row_data - jnp.mean(row_data, axis=-1, keepdims=True)
    inv_scale = lax.rsqrt(jnp.mean(centered * centered, axis=-1, keepdims=True) + EPSILON)
    normed = centered * inv_scale
    return (normed * gain_row + shift_row, normed, inv_scale)


def norm_back(grad_out, normed, inv_scale, gain_row):
    grad_normed = grad_out * gain_row
    interior = (
        grad_normed
        - jnp.mean(grad_normed, axis=-1, keepdims=True)
        - normed * jnp.mean(grad_normed * normed, axis=-1, keepdims=True)
    )
    return (inv_scale * interior, jnp.sum(grad_out * normed, axis=0), jnp.sum(grad_out, axis=0))


def tree_allowed(query_segs, key_segs, row_start):
    query_seg = query_segs[:, None]
    key_seg = key_segs[None, :]
    related = (
        (key_seg == 0)
        | (key_seg == query_seg)
        | (query_seg >= 5) & (key_seg == (query_seg - 5) // 2 + 1)
    )
    row_index = row_start + jnp.arange(query_segs.shape[0])[:, None]
    col_index = jnp.arange(key_segs.shape[0])[None, :]
    return related & (col_index <= row_index)


def block_scores(queries, key_rows, allowed, factor):
    scaled = (
        jnp.einsum("qhd,khd->hqk", queries, key_rows, preferred_element_type=jnp.float32) * factor
    )
    return jnp.where(allowed[None], scaled, MASKED)


def attend_forward(queries, key_rows, value_rows, segments, block_len):
    tree_len = queries.shape[0]
    factor = queries.shape[-1] ** (-0.5)
    outputs, totals = ([], [])
    for row_start in range(0, tree_len, block_len):
        row_stop = row_start + block_len
        allowed = tree_allowed(segments[row_start:row_stop], segments[:row_stop], row_start)
        scores = block_scores(queries[row_start:row_stop], key_rows[:row_stop], allowed, factor)
        peak_score = jnp.max(scores, axis=-1, keepdims=True)
        exponent = jnp.exp(scores - peak_score)
        denom_sum = jnp.sum(exponent, axis=-1, keepdims=True)
        weights = (exponent / denom_sum).astype(jnp.bfloat16)
        outputs.append(
            jnp.einsum(
                "hqk,khd->qhd", weights, value_rows[:row_stop], preferred_element_type=jnp.float32
            )
        )
        totals.append(peak_score + jnp.log(denom_sum))
    return (jnp.concatenate(outputs, axis=0), jnp.concatenate(totals, axis=1))


def attend_backward(queries, key_rows, value_rows, segments, grad_heads, log_sums, block_len):
    tree_len = queries.shape[0]
    factor = queries.shape[-1] ** (-0.5)
    grad_keys = jnp.zeros(key_rows.shape, jnp.float32)
    grad_values = jnp.zeros(value_rows.shape, jnp.float32)
    grad_queries = []
    for row_start in range(0, tree_len, block_len):
        row_stop = row_start + block_len
        allowed = tree_allowed(segments[row_start:row_stop], segments[:row_stop], row_start)
        scores = block_scores(queries[row_start:row_stop], key_rows[:row_stop], allowed, factor)
        weights = jnp.exp(scores - log_sums[:, row_start:row_stop])
        grad_weights = jnp.einsum(
            "qhd,khd->hqk",
            grad_heads[row_start:row_stop],
            value_rows[:row_stop],
            preferred_element_type=jnp.float32,
        )
        grad_scores = (
            weights * (grad_weights - jnp.sum(weights * grad_weights, axis=-1, keepdims=True))
        ).astype(jnp.bfloat16)
        grad_queries.append(
            jnp.einsum(
                "hqk,khd->qhd", grad_scores, key_rows[:row_stop], preferred_element_type=jnp.float32
            )
            * factor
        )
        grad_keys = grad_keys.at[:row_stop].add(
            jnp.einsum(
                "hqk,qhd->khd",
                grad_scores,
                queries[row_start:row_stop],
                preferred_element_type=jnp.float32,
            )
            * factor
        )
        grad_values = grad_values.at[:row_stop].add(
            jnp.einsum(
                "hqk,qhd->khd",
                weights.astype(jnp.bfloat16),
                grad_heads[row_start:row_stop],
                preferred_element_type=jnp.float32,
            )
        )
    return (jnp.concatenate(grad_queries, axis=0), grad_keys, grad_values)


def gelu_back(hidden, grad_act):
    return jax.vjp(partial(jax.nn.gelu, approximate=True), hidden)[1](grad_act)[0].astype(
        jnp.bfloat16
    )


def plain_body(
    tokens,
    segment,
    route,
    w_qkv,
    bias_qv,
    w_o,
    w_router,
    w_up,
    w_down,
    norm_gains,
    shifts,
    cotangent,
):
    micro_count, local_rows, model_width = tokens.shape
    tree_len = segment.shape[1]
    block_len = min(512, tree_len)
    expert_count = w_up.shape[0]
    tensor_count = lax.axis_size("tensor")
    local_cap = max(2, 3 * local_rows // (2 * expert_count))
    tree_cap = tensor_count * local_cap
    slot_count = expert_count * tree_cap
    position = lax.axis_index("tensor") * local_rows
    gains_all, shifts_all, router_all = (
        lax.all_gather(norm_gains, ("fsdp", "tensor"), axis=1, tiled=True),
        lax.all_gather(shifts, ("fsdp", "tensor"), axis=1, tiled=True),
        lax.all_gather(w_router, ("fsdp", "tensor"), axis=0, tiled=True),
    )
    gains_all = gains_all.astype(jnp.float32)
    shifts_all = shifts_all.astype(jnp.float32)
    router_wide = router_all.astype(jnp.float32)
    qkv_all, bias_all, out_all = (
        lax.all_gather(w_qkv, "fsdp", axis=1, tiled=True),
        lax.all_gather(bias_qv, "fsdp", axis=2, tiled=True),
        lax.all_gather(w_o, "fsdp", axis=1, tiled=True),
    )
    head_width = qkv_all.shape[2]
    head_count = bias_all.shape[1]
    bias_rows = bias_all.reshape(2, head_width).astype(jnp.float32)
    qkv_bias = jnp.stack([bias_rows[0], jnp.zeros_like(bias_rows[0]), bias_rows[1]])
    up_grad = jnp.zeros((expert_count, model_width, w_up.shape[2]), jnp.float32)
    down_grad = jnp.zeros((expert_count, w_down.shape[1], model_width), jnp.float32)
    qkv_grad = jnp.zeros(qkv_all.shape, jnp.float32)
    bias_grad = jnp.zeros((2, head_width), jnp.float32)
    out_grad = jnp.zeros(out_all.shape, jnp.float32)
    router_grad = jnp.zeros(router_wide.shape, jnp.float32)
    gain_grad = jnp.zeros(gains_all.shape, jnp.float32)
    shift_grad = jnp.zeros(shifts_all.shape, jnp.float32)
    expert_ids = jnp.arange(expert_count, dtype=jnp.int32)
    results, input_grads = ([], [])
    for micro_index in range(micro_count):
        segments = segment[micro_index]
        routes_all = route[micro_index, :, 0]
        inputs = tokens[micro_index].astype(jnp.float32)
        normed_in, plain_in, scale_in = norm_rows(inputs, gains_all[0], shifts_all[0])
        normed_tree = lax.all_gather(normed_in.astype(jnp.bfloat16), "tensor", axis=0, tiled=True)
        projected = (
            jnp.einsum("td,jdc->tjc", normed_tree, qkv_all, preferred_element_type=jnp.float32)
            + qkv_bias
        ).astype(jnp.bfloat16)
        queries = projected[:, 0].reshape(tree_len, head_count, -1)
        key_rows = projected[:, 1].reshape(tree_len, head_count, -1)
        value_rows = projected[:, 2].reshape(tree_len, head_count, -1)
        attended, log_sums = attend_forward(queries, key_rows, value_rows, segments, block_len)
        heads_low = attended.reshape(tree_len, head_width).astype(jnp.bfloat16)
        attention_rows = lax.psum_scatter(
            jnp.dot(heads_low, out_all, preferred_element_type=jnp.float32).astype(jnp.bfloat16),
            "tensor",
            scatter_dimension=0,
            tiled=True,
        ).astype(jnp.float32)
        residual = inputs + attention_rows + shifts_all[2]
        normed_mid, plain_mid, scale_mid = norm_rows(residual, gains_all[1], shifts_all[1])
        mid_low = normed_mid.astype(jnp.bfloat16)
        router_probs = jax.nn.softmax(
            jnp.dot(mid_low, router_all, preferred_element_type=jnp.float32), axis=-1
        )
        own_routes = lax.dynamic_slice_in_dim(routes_all, position, local_rows)
        own_choice = own_routes[:, None] == expert_ids[None, :]
        gate_value = jnp.sum(jnp.where(own_choice, router_probs, 0.0), axis=-1)
        grad_final = cotangent[micro_index].astype(jnp.float32)
        grad_returned = (gate_value[:, None] * grad_final).astype(jnp.bfloat16)
        up_all, down_all = (
            lax.all_gather(w_up, "fsdp", axis=1, tiled=True),
            lax.all_gather(w_down, "fsdp", axis=2, tiled=True),
        )
        chosen = routes_all[:, None] == expert_ids[None, :]
        running = jnp.cumsum(chosen.astype(jnp.int32), axis=0)
        slot_index = routes_all * tree_cap + jnp.sum(jnp.where(chosen, running, 0), axis=-1) - 1
        slot_token = (
            jnp.zeros((slot_count,), jnp.int32)
            .at[slot_index]
            .set(jnp.arange(tree_len, dtype=jnp.int32))
        )
        slot_filled = jnp.zeros((slot_count,), jnp.bool_).at[slot_index].set(True)
        mid_tree = lax.all_gather(mid_low, "tensor", axis=0, tiled=True)
        routed = jnp.where(slot_filled[:, None], mid_tree[slot_token], 0).reshape(
            expert_count, tree_cap, model_width
        )
        hidden = jnp.einsum("ecd,edf->ecf", routed, up_all, preferred_element_type=jnp.float32)
        activated = jax.nn.gelu(hidden, approximate=True).astype(jnp.bfloat16)
        expert_rows = jnp.einsum(
            "ecf,efd->ecd", activated, down_all, preferred_element_type=jnp.float32
        ).reshape(slot_count, model_width)
        returned = lax.psum_scatter(
            expert_rows[slot_index].astype(jnp.bfloat16), "tensor", scatter_dimension=0, tiled=True
        ).astype(jnp.float32)
        grad_tree = lax.all_gather(grad_returned, "tensor", axis=0, tiled=True)
        grad_expert = jnp.where(slot_filled[:, None], grad_tree[slot_token], 0).reshape(
            expert_count, tree_cap, model_width
        )
        down_grad = down_grad + jnp.einsum(
            "ecf,ecd->efd", activated, grad_expert, preferred_element_type=jnp.float32
        )
        grad_act = jnp.einsum(
            "ecd,efd->ecf", grad_expert, down_all, preferred_element_type=jnp.float32
        )
        grad_hidden = gelu_back(hidden, grad_act)
        up_grad = up_grad + jnp.einsum(
            "ecd,ecf->edf", routed, grad_hidden, preferred_element_type=jnp.float32
        )
        grad_routed = jnp.einsum(
            "ecf,edf->ecd", grad_hidden, up_all, preferred_element_type=jnp.float32
        ).reshape(slot_count, model_width)
        grad_mid = lax.psum_scatter(
            grad_routed[slot_index].astype(jnp.bfloat16), "tensor", scatter_dimension=0, tiled=True
        ).astype(jnp.float32)
        results.append(
            (residual + gate_value[:, None] * returned + shifts_all[3]).astype(jnp.bfloat16)
        )
        grad_gate = jnp.sum(grad_final * returned, axis=-1)
        grad_logits = router_probs * (
            jnp.where(own_choice, grad_gate[:, None], 0.0) - (gate_value * grad_gate)[:, None]
        )
        router_grad = router_grad + jnp.einsum(
            "td,te->de", mid_low.astype(jnp.float32), grad_logits, precision=HIGHEST
        )
        grad_mid = grad_mid + jnp.einsum("te,de->td", grad_logits, router_wide, precision=HIGHEST)
        grad_from_mid, gain_mid, shift_mid = norm_back(grad_mid, plain_mid, scale_mid, gains_all[1])
        grad_mixed = grad_final + grad_from_mid
        proj_tree = lax.all_gather(grad_mixed.astype(jnp.bfloat16), "tensor", axis=0, tiled=True)
        out_grad = out_grad + jnp.einsum(
            "tc,td->cd", heads_low, proj_tree, preferred_element_type=jnp.float32
        )
        grad_heads = jnp.einsum(
            "td,cd->tc", proj_tree, out_all, preferred_element_type=jnp.float32
        ).astype(jnp.bfloat16)
        grad_queries, grad_keys, grad_values = attend_backward(
            queries,
            key_rows,
            value_rows,
            segments,
            grad_heads.reshape(tree_len, head_count, -1),
            log_sums,
            block_len,
        )
        grad_proj_all = jnp.stack(
            [
                grad_queries.reshape(tree_len, head_width),
                grad_keys.reshape(tree_len, head_width),
                grad_values.reshape(tree_len, head_width),
            ],
            axis=1,
        ).astype(jnp.bfloat16)
        qkv_grad = qkv_grad + jnp.einsum(
            "td,tjc->jdc", normed_tree, grad_proj_all, preferred_element_type=jnp.float32
        )
        bias_grad = bias_grad + jnp.sum(grad_proj_all[:, 0::2].astype(jnp.float32), axis=0)
        grad_normed = lax.psum_scatter(
            jnp.einsum(
                "tjc,jdc->td", grad_proj_all, qkv_all, preferred_element_type=jnp.float32
            ).astype(jnp.bfloat16),
            "tensor",
            scatter_dimension=0,
            tiled=True,
        ).astype(jnp.float32)
        grad_from_in, gain_in, shift_in = norm_back(grad_normed, plain_in, scale_in, gains_all[0])
        input_grads.append(grad_mixed + grad_from_in)
        gain_grad = gain_grad + jnp.stack([gain_in, gain_mid])
        shift_grad = shift_grad + jnp.stack(
            [shift_in, shift_mid, jnp.sum(grad_mixed, axis=0), jnp.sum(grad_final, axis=0)]
        )
    weight_sums = (
        lax.psum_scatter(
            qkv_grad.astype(jnp.bfloat16), "fsdp", scatter_dimension=1, tiled=True
        ).astype(jnp.float32),
        lax.psum_scatter(
            bias_grad.reshape(2, head_count, -1).astype(jnp.bfloat16),
            "fsdp",
            scatter_dimension=2,
            tiled=True,
        ).astype(jnp.float32),
        lax.psum_scatter(
            out_grad.astype(jnp.bfloat16), "fsdp", scatter_dimension=1, tiled=True
        ).astype(jnp.float32),
    )
    up_final, down_final = (
        lax.psum_scatter(
            up_grad.astype(jnp.bfloat16), "fsdp", scatter_dimension=1, tiled=True
        ).astype(jnp.float32),
        lax.psum_scatter(
            down_grad.astype(jnp.bfloat16), "fsdp", scatter_dimension=2, tiled=True
        ).astype(jnp.float32),
    )
    small_sums = (
        lax.psum_scatter(gain_grad, ("fsdp", "tensor"), scatter_dimension=1, tiled=True),
        lax.psum_scatter(shift_grad, ("fsdp", "tensor"), scatter_dimension=1, tiled=True),
        lax.psum_scatter(router_grad, ("fsdp", "tensor"), scatter_dimension=0, tiled=True),
    )
    return (
        jnp.stack(results),
        jnp.stack(input_grads),
        weight_sums[0],
        weight_sums[1],
        weight_sums[2],
        small_sums[2],
        up_final,
        down_final,
        small_sums[0],
        small_sums[1][:3],
        small_sums[1][3],
    )


MESH = pl.DeviceIdType.MESH
BF = jnp.bfloat16
F32 = jnp.float32


def fits(mesh):
    return mesh.shape["fsdp"] == 8 and mesh.shape["tensor"] == 4


def flip(index, bit):
    return index + bit * (1 - 2 * (lax.rem(index // bit, 2)))


def place(fsdp, tensor):
    return {"fsdp": fsdp, "tensor": tensor}


def greet(partners):
    barrier = pltpu.get_barrier_semaphore()
    for fsdp, tensor in partners:
        pl.semaphore_signal(barrier, inc=1, device_id=place(fsdp, tensor), device_id_type=MESH)
    pl.semaphore_wait(barrier, len(partners))


def greet_all(mine):
    barrier = pltpu.get_barrier_semaphore()

    def signal(step, carry):
        other = lax.rem(mine + step, 32)
        pl.semaphore_signal(
            barrier, inc=1, device_id=place(other // 4, lax.rem(other, 4)), device_id_type=MESH
        )
        return carry

    lax.fori_loop(1, 32, signal, 0)
    pl.semaphore_wait(barrier, 31)


class Sender:
    def __init__(self, send_sem, recv_sem):
        self.send_sem, self.recv_sem, self.count = send_sem, recv_sem, 0
        self.open = []

    def copy(self, source, target, fsdp, tensor):
        made = pltpu.make_async_remote_copy(
            src_ref=source,
            dst_ref=target,
            send_sem=self.send_sem.at[self.count],
            recv_sem=self.recv_sem.at[self.count],
            device_id=place(fsdp, tensor),
            device_id_type=MESH,
        )
        self.count += 1
        made.start()
        self.open.append(made)
        return made

    def finish(self):
        for made in self.open:
            made.wait_send()


def gather_kernel(
    w4, small, tokens, up, down, full4, small_all, trunk, halo, up_own, down_own,
    send_sem, recv_sem, local_sem, up_send, up_recv, down_send, down_recv, trunk_send, trunk_recv,
):
    me_f, me_z = lax.axis_index("fsdp"), lax.axis_index("tensor")
    mine = me_f * 4 + me_z
    core = lax.rem(me_f, 2)
    greet_all(mine)
    sender = Sender(send_sem, recv_sem)

    def rows(fsdp):
        return pl.ds(pl.multiple_of(fsdp * 128, 128), 128)

    def cols(first, width):
        return pl.ds(pl.multiple_of(first * 256, 256), width)

    local = [
        pltpu.make_async_copy(w4, full4.at[:, rows(me_f), cols(me_z, 256)], local_sem.at[0]),
        pltpu.make_async_copy(small, small_all.at[me_f, me_z], local_sem.at[1]),
    ]
    for copy in local:
        copy.start()
    first = [
        sender.copy(w4, full4.at[:, rows(me_f), cols(me_z, 256)], me_f, flip(me_z, 1)),
        sender.copy(small, small_all.at[me_f, me_z], me_f, flip(me_z, 1)),
    ]

    piece = [(micro, half) for micro in range(2) for half in range(2)]

    def trunk_copy(index, source):
        micro, half = piece[index]
        return pltpu.make_async_remote_copy(
            src_ref=source.at[micro, pl.ds(half * 128, 128)],
            dst_ref=trunk.at[micro, pl.ds(half * 128, 128)],
            send_sem=trunk_send.at[index],
            recv_sem=trunk_recv.at[index],
            device_id=place(me_f, lax.rem(me_z + 1, 4)),
            device_id_type=MESH,
        )

    halo_copy = pltpu.make_async_remote_copy(
        src_ref=tokens.at[:, pl.ds(128, 128)],
        dst_ref=halo,
        send_sem=trunk_send.at[4],
        recv_sem=trunk_recv.at[4],
        device_id=place(me_f, lax.rem(me_z + 1, 4)),
        device_id_type=MESH,
    )

    def expert_copies(step):
        other = lax.rem(mine + step, 32)
        fsdp, tensor = other // 4, lax.rem(other, 4)
        expert = 2 * tensor + fsdp // 4
        quarter = pl.ds(pl.multiple_of(lax.rem(fsdp, 4) * 256, 256), 256)
        return (
            (up.at[expert, :, quarter], up_own.at[rows(me_f), cols(me_z, 256)]),
            (down.at[expert, quarter, :], down_own.at[cols(me_z, 256), rows(me_f)]),
            (fsdp, tensor),
        )

    def remote(step):
        ups, downs, (fsdp, tensor) = expert_copies(step)
        return [
            pltpu.make_async_remote_copy(
                src_ref=pair[0], dst_ref=pair[1], send_sem=sems[0].at[step],
                recv_sem=sems[1].at[step], device_id=place(fsdp, tensor), device_id_type=MESH,
            )
            for pair, sems in ((ups, (up_send, up_recv)), (downs, (down_send, down_recv)))
        ]

    def start_step(step, carry):
        for copy in remote(step):
            copy.start()
        return carry

    for copy in first:
        copy.wait_recv()
    for copy in local:
        copy.wait()
    pair = me_z // 2 * 2
    second = [
        sender.copy(
            full4.at[:, rows(me_f), cols(pair, 512)], full4.at[:, rows(me_f), cols(pair, 512)],
            me_f, flip(me_z, 2),
        ),
        sender.copy(
            small_all.at[me_f, pl.ds(pair, 2)], small_all.at[me_f, pl.ds(pair, 2)],
            me_f, flip(me_z, 2),
        ),
    ]
    for copy in second:
        copy.wait_recv()

    across = flip(me_f, 2) * (1 - core) + flip(me_f, 4) * core
    along = flip(me_f, 4) * (1 - core) + flip(me_f, 2) * core

    def blocks(fsdp_list, target):
        made = []
        for fsdp in fsdp_list:
            made.append(sender.copy(full4.at[:, rows(fsdp)], full4.at[:, rows(fsdp)], target, me_z))
            made.append(sender.copy(small_all.at[fsdp], small_all.at[fsdp], target, me_z))
        return made

    third = blocks([me_f], across)

    @pl.when(me_z == 0)
    def _():
        for index in range(4):
            trunk_copy(index, tokens).start()

    @pl.when(me_z < 3)
    def _():
        halo_copy.start()

    for copy in third:
        copy.wait_recv()
    fourth = blocks([me_f, across], along)

    for index in range(4):
        @pl.when(me_z > 0)
        def _(index=index):
            trunk_copy(index, trunk).wait_recv()

        @pl.when((me_z > 0) & (me_z < 3))
        def _(index=index):
            trunk_copy(index, trunk).start()

    for copy in fourth:
        copy.wait_recv()
    fifth = blocks([core, core + 2, core + 4, core + 6], flip(me_f, 1))
    lax.fori_loop(1, 32, start_step, 0)
    ups, downs, _ = expert_copies(0)
    own = [
        pltpu.make_async_copy(ups[0], ups[1], local_sem.at[2]),
        pltpu.make_async_copy(downs[0], downs[1], local_sem.at[3]),
    ]
    for copy in own:
        copy.start()

    for copy in fifth:
        copy.wait_recv()

    @pl.when(me_z > 0)
    def _():
        halo_copy.wait_recv()

    @pl.when(me_z < 3)
    def _():
        for index in range(4):
            trunk_copy(index, trunk).wait_send()
        halo_copy.wait_send()

    for copy in own:
        copy.wait()

    def end_step(step, carry):
        for copy in remote(step):
            copy.wait_send()
            copy.wait_recv()
        return carry

    lax.fori_loop(1, 32, end_step, 0)
    sender.finish()


def any_spec(count):
    return [pl.BlockSpec(memory_space=pl.ANY)] * count


def gather_all(w4, small, tokens, up, down):
    shapes = [
        jax.ShapeDtypeStruct((4, 1024, 1024), BF),
        jax.ShapeDtypeStruct((8, 4, 16, 128), BF),
        jax.ShapeDtypeStruct((2, 256, 1024), BF),
        jax.ShapeDtypeStruct((2, 128, 1024), BF),
        jax.ShapeDtypeStruct((1024, 1024), BF),
        jax.ShapeDtypeStruct((1024, 1024), BF),
    ]
    dma = pltpu.SemaphoreType.DMA
    return pl.pallas_call(
        gather_kernel,
        out_shape=shapes,
        in_specs=any_spec(5),
        out_specs=any_spec(6),
        scratch_shapes=[
            dma((20,)), dma((20,)), dma((4,)),
            dma((32,)), dma((32,)), dma((32,)), dma((32,)), dma((5,)), dma((5,)),
        ],
        compiler_params=pltpu.CompilerParams(collective_id=0, has_side_effects=True),
        name="gather_all",
    )(w4, small, tokens, up, down)


def gelu_pair(hidden):
    scale = (2.0 / jnp.pi) ** 0.5
    square = hidden * hidden
    bend = jnp.tanh(scale * hidden * (1.0 + 0.044715 * square))
    half = 0.5 * (1.0 + bend)
    slope = half + 0.5 * hidden * (1.0 - bend * bend) * scale * (1.0 + 0.134145 * square)
    return hidden * half, slope


def dot_nn(left, right):
    return lax.dot_general(left, right, (((1,), (0,)), ((), ())), preferred_element_type=F32)


def dot_nt(left, right):
    return lax.dot_general(left, right, (((1,), (1,)), ((), ())), preferred_element_type=F32)


def dot_tn(left, right):
    return lax.dot_general(left, right, (((0,), (0,)), ((), ())), preferred_element_type=F32)


def expert_kernel(
    slots, up_hbm, down_hbm, returned, up_grad, down_grad,
    arrived, parts, got, got_x, up, down, up_sum, down_sum, act, slope,
    send_sem, recv_sem, local_sem,
):
    cap = slots.shape[3]
    group = 8 * cap
    rows = 2 * group
    me_f, me_z = lax.axis_index("fsdp"), lax.axis_index("tensor")
    me_y, me_x, core = me_f // 4, lax.rem(me_f // 2, 2), lax.rem(me_f, 2)
    far_x = 1 - me_x
    x_mate, core_mate = flip(me_f, 2), flip(me_f, 1)
    far = []
    for step in range(1, 8):
        far.append(
            (lax.rem(me_y + step // 4, 2) * 4 + lax.rem(me_f, 4), lax.rem(me_z + step, 4))
        )
    greet([(x_mate, me_z), (core_mate, me_z)] + far)
    sender = Sender(send_sem, recv_sem)
    load = [
        pltpu.make_async_copy(up_hbm, up, local_sem.at[0]),
        pltpu.make_async_copy(down_hbm, down, local_sem.at[1]),
    ]

    def origin_rows(fsdp, tensor):
        first = (fsdp // 4 * 4 + tensor) * cap
        return pl.ds(pl.multiple_of(first, cap), cap)

    chunks = [(kind, micro) for kind in range(2) for micro in range(2)]
    incoming, own_in = [], []

    def send_in(index):
        kind, micro = chunks[index]
        incoming.append([
            sender.copy(
                slots.at[kind, micro, 2 * tensor + fsdp // 4],
                arrived.at[kind, micro, me_x, core, origin_rows(me_f, me_z)],
                fsdp, tensor,
            )
            for fsdp, tensor in far
        ])
        own = pltpu.make_async_copy(
            slots.at[kind, micro, 2 * me_z + me_y],
            arrived.at[kind, micro, me_x, core, origin_rows(me_f, me_z)],
            local_sem.at[2 + index],
        )
        own.start()
        own_in.append(own)

    send_in(0)
    for copy in load:
        copy.start()

    def same_place(view, fsdp):
        return sender.copy(view, view, fsdp, me_z)

    across, beside, onward = {}, {}, {}

    def landed(index):
        kind, micro = chunks[index]
        for copy in incoming[index]:
            copy.wait_recv()
        own_in[index].wait()
        if index < 3:
            send_in(index + 1)
        view = arrived.at[kind, micro, me_x, core]
        across[index] = same_place(view, x_mate)
        beside[index] = same_place(view, core_mate)

    def forwarded(index):
        kind, micro = chunks[index]
        across[index].wait_recv()
        onward[index] = same_place(arrived.at[kind, micro, far_x, core], core_mate)

    def tile(index):
        return pl.ds(pl.multiple_of(index * 256, 256), 256)

    def forward(micro, side):
        data = arrived.at[0, micro, side]

        def first(index, carry):
            hidden = dot_nn(data[...].reshape(rows, 1024), up[:, tile(index)])
            value, slope_value = gelu_pair(hidden)
            act[micro, side, :, tile(index)] = value.astype(BF)
            slope[micro, side, :, tile(index)] = slope_value.astype(BF)
            return carry

        lax.fori_loop(0, 4, first, 0)

        def second(index, carry):
            out = dot_nn(act[micro, side], down[:, tile(index)])
            parts[0, micro, side, :, :, tile(index)] = out.astype(BF).reshape(2, group, 256)
            return carry

        lax.fori_loop(0, 4, second, 0)

    def backward(micro, side, begin):
        data = arrived.at[0, micro, side]
        grads = arrived.at[1, micro, side]

        def first(index, carry):
            grad = grads[...].reshape(rows, 1024)
            grad_act = dot_nt(grad, down[tile(index), :])
            grad_hidden = (
                grad_act * slope[micro, side, :, tile(index)].astype(F32)
            ).astype(BF)
            slope[micro, side, :, tile(index)] = grad_hidden
            down_part = dot_tn(act[micro, side, :, tile(index)], grad)
            up_part = dot_tn(data[...].reshape(rows, 1024), grad_hidden)
            if begin:
                down_sum[tile(index), :] = down_part
                up_sum[:, tile(index)] = up_part
            else:
                down_sum[tile(index), :] += down_part
                up_sum[:, tile(index)] += up_part
            return carry

        lax.fori_loop(0, 4, first, 0)

        def second(index, carry):
            out = dot_nt(slope[micro, side], up[tile(index), :])
            parts[1, micro, side, :, :, tile(index)] = out.astype(BF).reshape(2, group, 256)
            return carry

        lax.fori_loop(0, 4, second, 0)

    def result(kind, micro):
        return parts.at[kind, micro]

    core_back, x_back, home = {}, {}, {}

    def back_core(index):
        kind, micro = chunks[index]
        core_back[index] = sender.copy(
            result(kind, micro).at[:, 1 - core], got.at[kind, micro], core_mate, me_z
        )

    def add_rows(target, source):
        def step(row, carry):
            part = pl.ds(pl.multiple_of(row * cap, cap), cap)
            target[part] = (target[part].astype(F32) + source[part].astype(F32)).astype(BF)
            return carry

        lax.fori_loop(0, 8, step, 0)

    def back_x(index):
        kind, micro = chunks[index]
        core_back[index].wait_recv()
        mine = result(kind, micro)
        add_rows(mine.at[far_x, core], got.at[kind, micro, far_x])
        x_back[index] = sender.copy(
            mine.at[far_x, core], got_x.at[kind, micro], x_mate, me_z
        )
        add_rows(mine.at[me_x, core], got.at[kind, micro, me_x])

    def back_home(index):
        kind, micro = chunks[index]
        x_back[index].wait_recv()
        mine = result(kind, micro).at[me_x, core]
        add_rows(mine, got_x.at[kind, micro])
        target = returned.at[kind, micro, 2 * me_z + me_y]
        home[index] = [
            sender.copy(mine.at[origin_rows(fsdp, tensor)], target, fsdp, tensor)
            for fsdp, tensor in far
        ]
        own = pltpu.make_async_copy(
            mine.at[origin_rows(me_f, me_z)], target, local_sem.at[2 + index]
        )
        own.start()
        own_in[index] = own

    landed(0)
    for copy in load:
        copy.wait()
    beside[0].wait_recv()
    forward(0, me_x)
    landed(1)
    forwarded(0)
    beside[1].wait_recv()
    forward(1, me_x)
    onward[0].wait_recv()
    forward(0, far_x)
    back_core(0)
    landed(2)
    forwarded(1)
    back_x(0)
    onward[1].wait_recv()
    forward(1, far_x)
    back_core(1)
    beside[2].wait_recv()
    backward(0, me_x, True)
    landed(3)
    forwarded(2)
    back_x(1)
    back_home(0)
    onward[2].wait_recv()
    backward(0, far_x, False)
    back_core(2)
    forwarded(3)
    back_home(1)
    beside[3].wait_recv()
    backward(1, me_x, False)
    back_x(2)
    onward[3].wait_recv()
    backward(1, far_x, False)
    back_core(3)
    back_home(2)

    def narrow(index, carry):
        part = pl.ds(pl.multiple_of(index * 64, 64), 64)
        up[part, :] = up_sum[part, :].astype(BF)
        down[part, :] = down_sum[part, :].astype(BF)
        return carry

    lax.fori_loop(0, 16, narrow, 0)
    store = [
        pltpu.make_async_copy(up, up_grad, local_sem.at[0]),
        pltpu.make_async_copy(down, down_grad, local_sem.at[1]),
    ]
    for copy in store:
        copy.start()
    back_x(3)
    back_home(3)
    for index in range(4):
        for copy in home[index]:
            copy.wait_recv()
        own_in[index].wait()
    for copy in store:
        copy.wait()
    sender.finish()


def run_experts(slots, up_own, down_own):
    cap = slots.shape[3]
    group = 8 * cap
    dma = pltpu.SemaphoreType.DMA
    return pl.pallas_call(
        expert_kernel,
        out_shape=[
            jax.ShapeDtypeStruct(slots.shape, BF),
            jax.ShapeDtypeStruct((1024, 1024), BF),
            jax.ShapeDtypeStruct((1024, 1024), BF),
        ],
        in_specs=any_spec(3),
        out_specs=any_spec(3),
        scratch_shapes=[
            pltpu.VMEM((2, 2, 2, 2, group, 1024), BF),
            pltpu.VMEM((2, 2, 2, 2, group, 1024), BF),
            pltpu.VMEM((2, 2, 2, group, 1024), BF),
            pltpu.VMEM((2, 2, group, 1024), BF),
            pltpu.VMEM((1024, 1024), BF),
            pltpu.VMEM((1024, 1024), BF),
            pltpu.VMEM((1024, 1024), F32),
            pltpu.VMEM((1024, 1024), F32),
            pltpu.VMEM((2, 2, 2 * group, 1024), BF),
            pltpu.VMEM((2, 2, 2 * group, 1024), BF),
            dma((76,)), dma((76,)), dma((6,)),
        ],
        compiler_params=pltpu.CompilerParams(
            collective_id=1, has_side_effects=True, vmem_limit_bytes=63 << 20
        ),
        cost_estimate=pl.CostEstimate(
            flops=12 * 4 * group * 2 * 1024 * 1024, bytes_accessed=20 << 20, transcendentals=0
        ),
        name="experts",
    )(slots, up_own, down_own)


def scatter_kernel(
    up_grad, down_grad, grad4, small, trunk, halo,
    up_out, down_out, out4, small_out, trunk_out, halo_out,
    keep, got, cut, cut_got, cut_a, cut_got_a, small_got, trunk_got, trunk_own,
    send_sem, recv_sem, local_sem, up_send, up_recv, down_send, down_recv,
    small_send, small_recv, trunk_send, trunk_recv,
):
    me_f, me_z = lax.axis_index("fsdp"), lax.axis_index("tensor")
    mine = me_f * 4 + me_z
    core = lax.rem(me_f, 2)
    me_y, me_x = me_f // 4, lax.rem(me_f // 2, 2)
    greet_all(mine)
    sender = Sender(send_sem, recv_sem)

    def rows(fsdp):
        return pl.ds(pl.multiple_of(fsdp * 128, 128), 128)

    def cols(first, width):
        return pl.ds(pl.multiple_of(first * 256, 256), width)

    first = []
    for block in range(4):
        first.append(
            sender.copy(
                grad4.at[:, rows(2 * block + 1 - core)], got.at[block], flip(me_f, 1), me_z
            )
        )
    local = []
    for block in range(4):
        copy = pltpu.make_async_copy(
            grad4.at[:, rows(2 * block + core)], keep.at[block], local_sem.at[block]
        )
        copy.start()
        local.append(copy)
    own_trunk = pltpu.make_async_copy(trunk, trunk_own, local_sem.at[4])
    own_trunk.start()

    def trunk_copy(index, source):
        return pltpu.make_async_remote_copy(
            src_ref=source.at[index],
            dst_ref=trunk_got.at[index],
            send_sem=trunk_send.at[index],
            recv_sem=trunk_recv.at[index],
            device_id=place(me_f, lax.rem(me_z + 3, 4)),
            device_id_type=MESH,
        )

    halo_copy = pltpu.make_async_remote_copy(
        src_ref=halo,
        dst_ref=halo_out,
        send_sem=trunk_send.at[4],
        recv_sem=trunk_recv.at[4],
        device_id=place(me_f, lax.rem(me_z + 3, 4)),
        device_id_type=MESH,
    )

    @pl.when(me_z == 3)
    def _():
        for index in range(4):
            trunk_copy(index, trunk).start()

    @pl.when(me_z > 0)
    def _():
        halo_copy.start()

    def small_copy(step):
        other = lax.rem(mine + step, 32)
        return pltpu.make_async_remote_copy(
            src_ref=small.at[other], dst_ref=small_got.at[mine], send_sem=small_send.at[step],
            recv_sem=small_recv.at[step], device_id=place(other // 4, lax.rem(other, 4)),
            device_id_type=MESH,
        )

    def expert_copies(step):
        other = lax.rem(mine + step, 32)
        fsdp, tensor = other // 4, lax.rem(other, 4)
        expert = 2 * me_z + me_y
        quarter = pl.ds(pl.multiple_of(lax.rem(me_f, 4) * 256, 256), 256)
        return (
            (up_grad.at[rows(fsdp), cols(tensor, 256)], up_out.at[expert, :, quarter]),
            (down_grad.at[cols(tensor, 256), rows(fsdp)], down_out.at[expert, quarter, :]),
            (fsdp, tensor),
        )

    def remote(step):
        ups, downs, (fsdp, tensor) = expert_copies(step)
        return [
            pltpu.make_async_remote_copy(
                src_ref=pair[0], dst_ref=pair[1], send_sem=sems[0].at[step],
                recv_sem=sems[1].at[step], device_id=place(fsdp, tensor), device_id_type=MESH,
            )
            for pair, sems in ((ups, (up_send, up_recv)), (downs, (down_send, down_recv)))
        ]

    def start_step(step, carry):
        small_copy(step).start()
        for copy in remote(step):
            copy.start()
        return carry

    lax.fori_loop(1, 32, start_step, 0)
    ups, downs, _ = expert_copies(0)
    own = [
        pltpu.make_async_copy(ups[0], ups[1], local_sem.at[5]),
        pltpu.make_async_copy(downs[0], downs[1], local_sem.at[6]),
        pltpu.make_async_copy(small.at[mine], small_got.at[mine], local_sem.at[7]),
    ]
    for copy in own:
        copy.start()

    def add_block(target, source):
        def step(index, carry):
            part = pl.ds(pl.multiple_of(index * 16, 16), 16)
            for which in range(4):
                target[which, part] = (
                    target[which, part].astype(F32) + source[which, part].astype(F32)
                ).astype(BF)
            return carry

        lax.fori_loop(0, 8, step, 0)

    for block in range(4):
        local[block].wait()
        first[block].wait_recv()
        add_block(keep.at[block], got.at[block])

    along = flip(me_f, 4) * (1 - core) + flip(me_f, 2) * core
    across = flip(me_f, 2) * (1 - core) + flip(me_f, 4) * core

    def block_of(fsdp):
        return fsdp // 2

    sent = [along, along * 0 + flip(across, 4) * (1 - core) + flip(across, 2) * core]
    kept = [me_f, across]
    second = []
    for index in range(2):
        second.append(
            sender.copy(keep.at[block_of(sent[index])], cut.at[index], along, me_z)
        )
    for index in range(2):
        second[index].wait_recv()
        add_block(keep.at[block_of(kept[index])], cut.at[index])
    third = sender.copy(keep.at[block_of(across)], cut_got, across, me_z)
    third.wait_recv()
    add_block(keep.at[block_of(me_f)], cut_got)
    mine4 = keep.at[block_of(me_f)]
    pair = me_z // 2 * 2
    other_pair = 2 - pair
    fourth = sender.copy(mine4.at[:, :, cols(other_pair, 512)], cut_a, me_f, flip(me_z, 2))
    fourth.wait_recv()

    def add_cols(source, begin, width, low):
        def step(index, carry):
            part = pl.ds(pl.multiple_of(index * 16, 16), 16)
            for which in range(4):
                mine4[which, part, cols(begin, width)] = (
                    mine4[which, part, cols(begin, width)].astype(F32)
                    + source[which, part, :].astype(F32)
                ).astype(BF)
            return carry

        lax.fori_loop(0, 8, step, 0)

    add_cols(cut_a, pair, 512, 0)
    fifth = sender.copy(
        mine4.at[:, :, cols(flip(me_z, 1), 256)], cut_got_a, me_f, flip(me_z, 1)
    )
    fifth.wait_recv()
    add_cols(cut_got_a, me_z, 256, 0)
    last = pltpu.make_async_copy(mine4.at[:, :, cols(me_z, 256)], out4, local_sem.at[0])
    last.start()

    own_trunk.wait()
    for index in range(4):
        @pl.when(me_z < 3)
        def _(index=index):
            trunk_copy(index, trunk_own).wait_recv()

            def step(row, carry):
                part = pl.ds(pl.multiple_of(row * 16, 16), 16)
                trunk_own[index, part] = (
                    trunk_own[index, part].astype(F32) + trunk_got[index, part].astype(F32)
                ).astype(BF)
                return carry

            lax.fori_loop(0, 8, step, 0)

        @pl.when((me_z > 0) & (me_z < 3))
        def _(index=index):
            trunk_copy(index, trunk_own).start()

    @pl.when(me_z > 0)
    def _():
        for index in range(4):
            trunk_copy(index, trunk_own).wait_send()
        halo_copy.wait_send()

    @pl.when(me_z < 3)
    def _():
        halo_copy.wait_recv()

    trunk_done = pltpu.make_async_copy(trunk_own, trunk_out, local_sem.at[1])
    trunk_done.start()
    for copy in own:
        copy.wait()

    def end_small(step, carry):
        copy = small_copy(step)
        copy.wait_send()
        copy.wait_recv()
        return carry

    lax.fori_loop(1, 32, end_small, 0)

    def sum_small(index, total):
        return total + small_got[index]

    small_out[...] = lax.fori_loop(1, 32, sum_small, small_got[0])

    def end_step(step, carry):
        for copy in remote(step):
            copy.wait_send()
            copy.wait_recv()
        return carry

    lax.fori_loop(1, 32, end_step, 0)
    sender.finish()
    last.wait()
    trunk_done.wait()


def scatter_all(up_grad, down_grad, grad4, small, trunk, halo):
    dma = pltpu.SemaphoreType.DMA
    shapes = [
        jax.ShapeDtypeStruct((8, 128, 1024), BF),
        jax.ShapeDtypeStruct((8, 1024, 128), BF),
        jax.ShapeDtypeStruct((4, 128, 256), BF),
        jax.ShapeDtypeStruct((16, 128), F32),
        jax.ShapeDtypeStruct((4, 128, 1024), BF),
        jax.ShapeDtypeStruct((2, 128, 1024), BF),
    ]
    specs = any_spec(6)
    specs[3] = pl.BlockSpec(memory_space=pltpu.VMEM)
    return pl.pallas_call(
        scatter_kernel,
        out_shape=shapes,
        in_specs=any_spec(6),
        out_specs=specs,
        scratch_shapes=[
            pltpu.VMEM((4, 4, 128, 1024), BF),
            pltpu.VMEM((4, 4, 128, 1024), BF),
            pltpu.VMEM((2, 4, 128, 1024), BF),
            pltpu.VMEM((4, 128, 1024), BF),
            pltpu.VMEM((4, 128, 512), BF),
            pltpu.VMEM((4, 128, 256), BF),
            pltpu.VMEM((32, 16, 128), F32),
            pltpu.VMEM((4, 128, 1024), BF),
            pltpu.VMEM((4, 128, 1024), BF),
            dma((10,)), dma((10,)), dma((8,)),
            dma((32,)), dma((32,)), dma((32,)), dma((32,)),
            dma((32,)), dma((32,)), dma((5,)), dma((5,)),
        ],
        compiler_params=pltpu.CompilerParams(
            collective_id=3, has_side_effects=True, vmem_limit_bytes=48 << 20
        ),
        name="scatter_all",
    )(up_grad, down_grad, grad4, small, trunk, halo)


def fast_body(
    tokens, segment, route, w_qkv, bias_qv, w_o, w_router, w_up, w_down, norm_gains, shifts, cotangent
):
    micro_count, local_rows, width = tokens.shape
    expert_count = w_up.shape[0]
    cap = 3 * local_rows // (2 * expert_count)
    me_z = lax.axis_index("tensor")
    start = me_z * local_rows
    small = jnp.concatenate(
        [norm_gains, shifts, w_router.T, bias_qv.reshape(2, 32)], axis=0
    )
    small = jnp.pad(small, ((0, 0), (0, 96)))
    w4 = jnp.concatenate([w_qkv, w_o.T[None]], axis=0)
    full4, small_all, trunk, halo, up_own, down_own = gather_all(w4, small, tokens, w_up, w_down)
    flat_small = small_all[..., :32].transpose(2, 0, 1, 3).reshape(16, width)
    gains = flat_small[:2].astype(F32)
    offsets = flat_small[2:6].astype(F32)
    router_t = flat_small[6:14]
    biases = (
        small_all[:, :, 14:16, :32].reshape(8, 4, 2, 4, 8).transpose(2, 1, 3, 0, 4).reshape(2, width)
    ).astype(F32)

    inputs = tokens.astype(F32)
    trunk = jnp.where(me_z == 0, tokens, trunk)
    halo = jnp.where(me_z == 0, tokens[:, 128:], halo)
    with_keys = jnp.concatenate([trunk.astype(F32), halo.astype(F32), inputs], axis=1)
    normed_all, plain_all, scale_all = norm_rows(with_keys, gains[0], offsets[0])
    normed_all = normed_all.astype(BF)
    normed_own = normed_all[:, 384:]
    plain_in, scale_in = plain_all[:, 384:], scale_all[:, 384:]
    queries = (
        jnp.einsum("mrd,dc->mrc", normed_own, full4[0], preferred_element_type=F32) + biases[0]
    ).astype(BF)
    keys = jnp.einsum("mrd,dc->mrc", normed_all, full4[1], preferred_element_type=F32).astype(BF)
    values = (
        jnp.einsum("mrd,dc->mrc", normed_all, full4[2], preferred_element_type=F32) + biases[1]
    ).astype(BF)
    own_index = start + jnp.arange(local_rows)
    key_index = jnp.concatenate([jnp.arange(256), start - 128 + jnp.arange(128), own_index])
    key_part = jnp.arange(640) < 256
    own_segs = lax.dynamic_slice_in_dim(segment, start, local_rows, axis=1)
    halo_segs = lax.dynamic_slice_in_dim(segment, jnp.maximum(start - 128, 0), 128, axis=1)
    key_segs = jnp.concatenate([segment[:, :256], halo_segs, own_segs], axis=1)
    query_seg, key_seg = own_segs[:, :, None], key_segs[:, None, :]
    allowed = (
        (key_seg == 0)
        | (key_seg == query_seg)
        | (query_seg >= 5) & (key_seg == (query_seg - 5) // 2 + 1)
    )
    allowed = allowed & (key_part | (key_index >= 256))[None, None, :]
    allowed = allowed & (key_index[None, :] <= own_index[:, None])[None]
    heads = (micro_count, -1, 16, 64)
    queries_h, keys_h, values_h = queries.reshape(heads), keys.reshape(heads), values.reshape(heads)
    scores = jnp.einsum("mqhd,mkhd->mhqk", queries_h, keys_h, preferred_element_type=F32) * 0.125
    scores = jnp.where(allowed[:, None], scores, MASKED)
    probs = jax.nn.softmax(scores, axis=-1)
    probs_low = probs.astype(BF)
    heads_low = (
        jnp.einsum("mhqk,mkhd->mqhd", probs_low, values_h, preferred_element_type=F32)
        .astype(BF)
        .reshape(micro_count, local_rows, width)
    )
    attention_rows = jnp.einsum("mrc,dc->mrd", heads_low, full4[3], preferred_element_type=F32)
    residual = inputs + attention_rows + offsets[2]
    normed_mid, plain_mid, scale_mid = norm_rows(residual, gains[1], offsets[1])
    mid_low = normed_mid.astype(BF)
    router_probs = jax.nn.softmax(
        jnp.einsum("mrd,ed->mre", mid_low, router_t, preferred_element_type=F32), axis=-1
    )
    own_routes = lax.dynamic_slice_in_dim(route[:, :, 0], start, local_rows, axis=1)
    own_choice = own_routes[:, :, None] == jnp.arange(expert_count)
    gate = jnp.sum(jnp.where(own_choice, router_probs, 0.0), axis=-1)
    grad_final = cotangent.astype(F32)
    grad_returned = (gate[..., None] * grad_final).astype(BF)
    running = jnp.cumsum(own_choice.astype(jnp.int32), axis=1)
    slot = own_routes * cap + jnp.sum(jnp.where(own_choice, running, 0), axis=-1) - 1
    pick = (slot[:, None, :] == jnp.arange(expert_count * cap)[None, :, None]).astype(BF)
    sending = jnp.stack([mid_low, grad_returned])
    slots = (
        jnp.einsum("msr,kmrd->kmsd", pick, sending, preferred_element_type=F32)
        .astype(BF)
        .reshape(2, micro_count, expert_count, cap, width)
    )
    back, up_grad, down_grad = run_experts(slots, up_own, down_own)
    back = back.reshape(2, micro_count, expert_count * cap, width)
    rows_back = jnp.einsum("msr,kmsd->kmrd", pick, back, preferred_element_type=F32)
    returned, grad_mid = rows_back[0], rows_back[1]
    output = (residual + gate[..., None] * returned + offsets[3]).astype(BF)
    grad_gate = jnp.sum(grad_final * returned, axis=-1)
    grad_logits = router_probs * (
        jnp.where(own_choice, grad_gate[..., None], 0.0) - (gate * grad_gate)[..., None]
    )
    router_grad = jnp.einsum(
        "mrd,mre->ed", mid_low.astype(F32), grad_logits, precision=HIGHEST
    )
    grad_mid = grad_mid + jnp.einsum(
        "mre,ed->mrd", grad_logits, router_t.astype(F32), precision=HIGHEST
    )

    def flat(value):
        return value.reshape(-1, value.shape[-1])

    grad_from_mid, gain_mid, shift_mid = norm_back(
        flat(grad_mid), flat(plain_mid), flat(scale_mid), gains[1]
    )
    grad_mixed = grad_final + grad_from_mid.reshape(grad_final.shape)
    proj = grad_mixed.astype(BF)
    out_grad_t = jnp.einsum("mrd,mrc->dc", proj, heads_low, preferred_element_type=F32)
    grad_heads = jnp.einsum("mrd,dc->mrc", proj, full4[3], preferred_element_type=F32).astype(BF)
    grad_heads_h = grad_heads.reshape(heads)
    grad_probs = jnp.einsum("mqhd,mkhd->mhqk", grad_heads_h, values_h, preferred_element_type=F32)
    grad_scores = (
        probs * (grad_probs - jnp.sum(probs * grad_probs, axis=-1, keepdims=True))
    ).astype(BF)
    grad_queries = (
        jnp.einsum("mhqk,mkhd->mqhd", grad_scores, keys_h, preferred_element_type=F32) * 0.125
    ).astype(BF).reshape(micro_count, -1, width)
    grad_keys = (
        jnp.einsum("mhqk,mqhd->mkhd", grad_scores, queries_h, preferred_element_type=F32) * 0.125
    ).astype(BF).reshape(micro_count, -1, width)
    grad_values = (
        jnp.einsum("mhqk,mqhd->mkhd", probs_low, grad_heads_h, preferred_element_type=F32)
    ).astype(BF).reshape(micro_count, -1, width)
    grad4 = jnp.stack([
        jnp.einsum("mrd,mrc->dc", normed_own, grad_queries, preferred_element_type=F32).astype(BF),
        jnp.einsum("mrd,mrc->dc", normed_all, grad_keys, preferred_element_type=F32).astype(BF),
        jnp.einsum("mrd,mrc->dc", normed_all, grad_values, preferred_element_type=F32).astype(BF),
        out_grad_t.astype(BF),
    ])
    bias_grad = jnp.stack([
        jnp.sum(grad_queries.astype(F32), axis=(0, 1)),
        jnp.sum(grad_values.astype(F32), axis=(0, 1)),
    ])
    grad_all = jnp.einsum(
        "mrc,dc->mrd", grad_keys, full4[1], preferred_element_type=F32
    ) + jnp.einsum("mrc,dc->mrd", grad_values, full4[2], preferred_element_type=F32)
    grad_own = grad_all[:, 384:] + jnp.einsum(
        "mrc,dc->mrd", grad_queries, full4[0], preferred_element_type=F32
    )
    early = jnp.concatenate([
        jnp.stack([jnp.zeros((width,), F32), gain_mid]),
        jnp.stack([
            jnp.zeros((width,), F32), shift_mid,
            jnp.sum(grad_mixed, axis=(0, 1)), jnp.sum(grad_final, axis=(0, 1)),
        ]),
        router_grad,
    ])
    plain_halo, plain_trunk = plain_all[:, 256:384], plain_all[:, :256]
    grad_trunk, grad_halo = grad_all[:, :256], grad_all[:, 256:384]
    early = early.at[0].set(
        jnp.sum(grad_all * plain_all, axis=(0, 1))
        + jnp.sum((grad_own - grad_all[:, 384:]) * plain_in, axis=(0, 1))
    )
    early = early.at[2].set(
        jnp.sum(grad_all, axis=(0, 1)) + jnp.sum(grad_own - grad_all[:, 384:], axis=(0, 1))
    )
    small_grad = early.reshape(14, 32, 32).transpose(1, 0, 2)
    bias_small = (
        bias_grad.reshape(2, 4, 4, 8, 8).transpose(3, 1, 0, 2, 4).reshape(32, 2, 32)
    )
    small_grad = jnp.pad(
        jnp.concatenate([small_grad, bias_small], axis=1), ((0, 0), (0, 0), (0, 96))
    )
    up_out, down_out, out4, small_out, trunk_sum, halo_sum = scatter_all(
        up_grad, down_grad, grad4, small_grad,
        grad_trunk.astype(BF).reshape(4, 128, width), grad_halo.astype(BF),
    )
    trunk_sum = trunk_sum.reshape(2, 256, width).astype(F32)
    grad_normed = grad_own + jnp.where(me_z == 0, trunk_sum, 0.0)
    grad_normed = grad_normed.at[:, 128:].add(jnp.where(me_z < 3, halo_sum.astype(F32), 0.0))
    grad_from_in, _, _ = norm_back(flat(grad_normed), flat(plain_in), flat(scale_in), gains[0])
    input_grad = grad_mixed + grad_from_in.reshape(grad_mixed.shape)
    small_out = small_out[:, :32]
    return (
        output,
        input_grad,
        out4[:3].astype(F32),
        small_out[14:16].reshape(2, 4, 8),
        out4[3].T.astype(F32),
        small_out[6:14].T,
        up_out.astype(F32),
        down_out.astype(F32),
        small_out[:2],
        small_out[2:5],
        small_out[5],
    )


def solution(mesh):
    placed = (
        P(None, ("fsdp", "tensor"), None),
        P(None, "fsdp"),
        P(None, "fsdp", None),
        P(None, "fsdp", "tensor"),
        P(None, "tensor", "fsdp"),
        P("tensor", "fsdp"),
        P(("fsdp", "tensor"), None),
        P(None, "fsdp", "tensor"),
        P(None, "tensor", "fsdp"),
        P(None, ("fsdp", "tensor")),
        P(None, ("fsdp", "tensor")),
        P(None, ("fsdp", "tensor"), None),
    )
    return jax.shard_map(
        fast_body if fits(mesh) else plain_body,
        mesh=mesh,
        in_specs=placed,
        out_specs=(
            P(None, ("fsdp", "tensor"), None),
            P(None, ("fsdp", "tensor"), None),
            P(None, "fsdp", "tensor"),
            P(None, "tensor", "fsdp"),
            P("tensor", "fsdp"),
            P(("fsdp", "tensor"), None),
            P(None, "fsdp", "tensor"),
            P(None, "tensor", "fsdp"),
            P(None, ("fsdp", "tensor")),
            P(None, ("fsdp", "tensor")),
            P(("fsdp", "tensor")),
        ),
        check_vma=False,
    )
```

```python
from functools import partial

import jax
import jax.numpy as jnp
from jax import lax
from jax.experimental import pallas as pl
from jax.experimental.pallas import tpu as pltpu
from jax.sharding import PartitionSpec as P

EPSILON = 1e-05
MASKED = -1e30
HIGHEST = lax.Precision.HIGHEST


def norm_rows(row_data, gain_row, shift_row):
    centered = row_data - jnp.mean(row_data, axis=-1, keepdims=True)
    inv_scale = lax.rsqrt(jnp.mean(centered * centered, axis=-1, keepdims=True) + EPSILON)
    normed = centered * inv_scale
    return (normed * gain_row + shift_row, normed, inv_scale)


def norm_back(grad_out, normed, inv_scale, gain_row):
    grad_normed = grad_out * gain_row
    interior = (
        grad_normed
        - jnp.mean(grad_normed, axis=-1, keepdims=True)
        - normed * jnp.mean(grad_normed * normed, axis=-1, keepdims=True)
    )
    return (inv_scale * interior, jnp.sum(grad_out * normed, axis=0), jnp.sum(grad_out, axis=0))


def tree_allowed(query_segs, key_segs, row_start):
    query_seg = query_segs[:, None]
    key_seg = key_segs[None, :]
    related = (
        (key_seg == 0)
        | (key_seg == query_seg)
        | (query_seg >= 5) & (key_seg == (query_seg - 5) // 2 + 1)
    )
    row_index = row_start + jnp.arange(query_segs.shape[0])[:, None]
    col_index = jnp.arange(key_segs.shape[0])[None, :]
    return related & (col_index <= row_index)


def block_scores(queries, key_rows, allowed, factor):
    scaled = (
        jnp.einsum("qhd,khd->hqk", queries, key_rows, preferred_element_type=jnp.float32) * factor
    )
    return jnp.where(allowed[None], scaled, MASKED)


def attend_forward(queries, key_rows, value_rows, segments, block_len):
    tree_len = queries.shape[0]
    factor = queries.shape[-1] ** (-0.5)
    outputs, totals = ([], [])
    for row_start in range(0, tree_len, block_len):
        row_stop = row_start + block_len
        allowed = tree_allowed(segments[row_start:row_stop], segments[:row_stop], row_start)
        scores = block_scores(queries[row_start:row_stop], key_rows[:row_stop], allowed, factor)
        peak_score = jnp.max(scores, axis=-1, keepdims=True)
        exponent = jnp.exp(scores - peak_score)
        denom_sum = jnp.sum(exponent, axis=-1, keepdims=True)
        weights = (exponent / denom_sum).astype(jnp.bfloat16)
        outputs.append(
            jnp.einsum(
                "hqk,khd->qhd", weights, value_rows[:row_stop], preferred_element_type=jnp.float32
            )
        )
        totals.append(peak_score + jnp.log(denom_sum))
    return (jnp.concatenate(outputs, axis=0), jnp.concatenate(totals, axis=1))


def attend_backward(queries, key_rows, value_rows, segments, grad_heads, log_sums, block_len):
    tree_len = queries.shape[0]
    factor = queries.shape[-1] ** (-0.5)
    grad_keys = jnp.zeros(key_rows.shape, jnp.float32)
    grad_values = jnp.zeros(value_rows.shape, jnp.float32)
    grad_queries = []
    for row_start in range(0, tree_len, block_len):
        row_stop = row_start + block_len
        allowed = tree_allowed(segments[row_start:row_stop], segments[:row_stop], row_start)
        scores = block_scores(queries[row_start:row_stop], key_rows[:row_stop], allowed, factor)
        weights = jnp.exp(scores - log_sums[:, row_start:row_stop])
        grad_weights = jnp.einsum(
            "qhd,khd->hqk",
            grad_heads[row_start:row_stop],
            value_rows[:row_stop],
            preferred_element_type=jnp.float32,
        )
        grad_scores = (
            weights * (grad_weights - jnp.sum(weights * grad_weights, axis=-1, keepdims=True))
        ).astype(jnp.bfloat16)
        grad_queries.append(
            jnp.einsum(
                "hqk,khd->qhd", grad_scores, key_rows[:row_stop], preferred_element_type=jnp.float32
            )
            * factor
        )
        grad_keys = grad_keys.at[:row_stop].add(
            jnp.einsum(
                "hqk,qhd->khd",
                grad_scores,
                queries[row_start:row_stop],
                preferred_element_type=jnp.float32,
            )
            * factor
        )
        grad_values = grad_values.at[:row_stop].add(
            jnp.einsum(
                "hqk,qhd->khd",
                weights.astype(jnp.bfloat16),
                grad_heads[row_start:row_stop],
                preferred_element_type=jnp.float32,
            )
        )
    return (jnp.concatenate(grad_queries, axis=0), grad_keys, grad_values)


def gelu_back(hidden, grad_act):
    return jax.vjp(partial(jax.nn.gelu, approximate=True), hidden)[1](grad_act)[0].astype(
        jnp.bfloat16
    )


def plain_body(
    tokens,
    segment,
    route,
    w_qkv,
    bias_qv,
    w_o,
    w_router,
    w_up,
    w_down,
    norm_gains,
    shifts,
    cotangent,
):
    micro_count, local_rows, model_width = tokens.shape
    tree_len = segment.shape[1]
    block_len = min(512, tree_len)
    expert_count = w_up.shape[0]
    tensor_count = lax.axis_size("tensor")
    local_cap = max(2, 3 * local_rows // (2 * expert_count))
    tree_cap = tensor_count * local_cap
    slot_count = expert_count * tree_cap
    position = lax.axis_index("tensor") * local_rows
    gains_all, shifts_all, router_all = (
        lax.all_gather(norm_gains, ("fsdp", "tensor"), axis=1, tiled=True),
        lax.all_gather(shifts, ("fsdp", "tensor"), axis=1, tiled=True),
        lax.all_gather(w_router, ("fsdp", "tensor"), axis=0, tiled=True),
    )
    gains_all = gains_all.astype(jnp.float32)
    shifts_all = shifts_all.astype(jnp.float32)
    router_wide = router_all.astype(jnp.float32)
    qkv_all, bias_all, out_all = (
        lax.all_gather(w_qkv, "fsdp", axis=1, tiled=True),
        lax.all_gather(bias_qv, "fsdp", axis=2, tiled=True),
        lax.all_gather(w_o, "fsdp", axis=1, tiled=True),
    )
    head_width = qkv_all.shape[2]
    head_count = bias_all.shape[1]
    bias_rows = bias_all.reshape(2, head_width).astype(jnp.float32)
    qkv_bias = jnp.stack([bias_rows[0], jnp.zeros_like(bias_rows[0]), bias_rows[1]])
    up_grad = jnp.zeros((expert_count, model_width, w_up.shape[2]), jnp.float32)
    down_grad = jnp.zeros((expert_count, w_down.shape[1], model_width), jnp.float32)
    qkv_grad = jnp.zeros(qkv_all.shape, jnp.float32)
    bias_grad = jnp.zeros((2, head_width), jnp.float32)
    out_grad = jnp.zeros(out_all.shape, jnp.float32)
    router_grad = jnp.zeros(router_wide.shape, jnp.float32)
    gain_grad = jnp.zeros(gains_all.shape, jnp.float32)
    shift_grad = jnp.zeros(shifts_all.shape, jnp.float32)
    expert_ids = jnp.arange(expert_count, dtype=jnp.int32)
    results, input_grads = ([], [])
    for micro_index in range(micro_count):
        segments = segment[micro_index]
        routes_all = route[micro_index, :, 0]
        inputs = tokens[micro_index].astype(jnp.float32)
        normed_in, plain_in, scale_in = norm_rows(inputs, gains_all[0], shifts_all[0])
        normed_tree = lax.all_gather(normed_in.astype(jnp.bfloat16), "tensor", axis=0, tiled=True)
        projected = (
            jnp.einsum("td,jdc->tjc", normed_tree, qkv_all, preferred_element_type=jnp.float32)
            + qkv_bias
        ).astype(jnp.bfloat16)
        queries = projected[:, 0].reshape(tree_len, head_count, -1)
        key_rows = projected[:, 1].reshape(tree_len, head_count, -1)
        value_rows = projected[:, 2].reshape(tree_len, head_count, -1)
        attended, log_sums = attend_forward(queries, key_rows, value_rows, segments, block_len)
        heads_low = attended.reshape(tree_len, head_width).astype(jnp.bfloat16)
        attention_rows = lax.psum_scatter(
            jnp.dot(heads_low, out_all, preferred_element_type=jnp.float32).astype(jnp.bfloat16),
            "tensor",
            scatter_dimension=0,
            tiled=True,
        ).astype(jnp.float32)
        residual = inputs + attention_rows + shifts_all[2]
        normed_mid, plain_mid, scale_mid = norm_rows(residual, gains_all[1], shifts_all[1])
        mid_low = normed_mid.astype(jnp.bfloat16)
        router_probs = jax.nn.softmax(
            jnp.dot(mid_low, router_all, preferred_element_type=jnp.float32), axis=-1
        )
        own_routes = lax.dynamic_slice_in_dim(routes_all, position, local_rows)
        own_choice = own_routes[:, None] == expert_ids[None, :]
        gate_value = jnp.sum(jnp.where(own_choice, router_probs, 0.0), axis=-1)
        grad_final = cotangent[micro_index].astype(jnp.float32)
        grad_returned = (gate_value[:, None] * grad_final).astype(jnp.bfloat16)
        up_all, down_all = (
            lax.all_gather(w_up, "fsdp", axis=1, tiled=True),
            lax.all_gather(w_down, "fsdp", axis=2, tiled=True),
        )
        chosen = routes_all[:, None] == expert_ids[None, :]
        running = jnp.cumsum(chosen.astype(jnp.int32), axis=0)
        slot_index = routes_all * tree_cap + jnp.sum(jnp.where(chosen, running, 0), axis=-1) - 1
        slot_token = (
            jnp.zeros((slot_count,), jnp.int32)
            .at[slot_index]
            .set(jnp.arange(tree_len, dtype=jnp.int32))
        )
        slot_filled = jnp.zeros((slot_count,), jnp.bool_).at[slot_index].set(True)
        mid_tree = lax.all_gather(mid_low, "tensor", axis=0, tiled=True)
        routed = jnp.where(slot_filled[:, None], mid_tree[slot_token], 0).reshape(
            expert_count, tree_cap, model_width
        )
        hidden = jnp.einsum("ecd,edf->ecf", routed, up_all, preferred_element_type=jnp.float32)
        activated = jax.nn.gelu(hidden, approximate=True).astype(jnp.bfloat16)
        expert_rows = jnp.einsum(
            "ecf,efd->ecd", activated, down_all, preferred_element_type=jnp.float32
        ).reshape(slot_count, model_width)
        returned = lax.psum_scatter(
            expert_rows[slot_index].astype(jnp.bfloat16), "tensor", scatter_dimension=0, tiled=True
        ).astype(jnp.float32)
        grad_tree = lax.all_gather(grad_returned, "tensor", axis=0, tiled=True)
        grad_expert = jnp.where(slot_filled[:, None], grad_tree[slot_token], 0).reshape(
            expert_count, tree_cap, model_width
        )
        down_grad = down_grad + jnp.einsum(
            "ecf,ecd->efd", activated, grad_expert, preferred_element_type=jnp.float32
        )
        grad_act = jnp.einsum(
            "ecd,efd->ecf", grad_expert, down_all, preferred_element_type=jnp.float32
        )
        grad_hidden = gelu_back(hidden, grad_act)
        up_grad = up_grad + jnp.einsum(
            "ecd,ecf->edf", routed, grad_hidden, preferred_element_type=jnp.float32
        )
        grad_routed = jnp.einsum(
            "ecf,edf->ecd", grad_hidden, up_all, preferred_element_type=jnp.float32
        ).reshape(slot_count, model_width)
        grad_mid = lax.psum_scatter(
            grad_routed[slot_index].astype(jnp.bfloat16), "tensor", scatter_dimension=0, tiled=True
        ).astype(jnp.float32)
        results.append(
            (residual + gate_value[:, None] * returned + shifts_all[3]).astype(jnp.bfloat16)
        )
        grad_gate = jnp.sum(grad_final * returned, axis=-1)
        grad_logits = router_probs * (
            jnp.where(own_choice, grad_gate[:, None], 0.0) - (gate_value * grad_gate)[:, None]
        )
        router_grad = router_grad + jnp.einsum(
            "td,te->de", mid_low.astype(jnp.float32), grad_logits, precision=HIGHEST
        )
        grad_mid = grad_mid + jnp.einsum("te,de->td", grad_logits, router_wide, precision=HIGHEST)
        grad_from_mid, gain_mid, shift_mid = norm_back(grad_mid, plain_mid, scale_mid, gains_all[1])
        grad_mixed = grad_final + grad_from_mid
        proj_tree = lax.all_gather(grad_mixed.astype(jnp.bfloat16), "tensor", axis=0, tiled=True)
        out_grad = out_grad + jnp.einsum(
            "tc,td->cd", heads_low, proj_tree, preferred_element_type=jnp.float32
        )
        grad_heads = jnp.einsum(
            "td,cd->tc", proj_tree, out_all, preferred_element_type=jnp.float32
        ).astype(jnp.bfloat16)
        grad_queries, grad_keys, grad_values = attend_backward(
            queries,
            key_rows,
            value_rows,
            segments,
            grad_heads.reshape(tree_len, head_count, -1),
            log_sums,
            block_len,
        )
        grad_proj_all = jnp.stack(
            [
                grad_queries.reshape(tree_len, head_width),
                grad_keys.reshape(tree_len, head_width),
                grad_values.reshape(tree_len, head_width),
            ],
            axis=1,
        ).astype(jnp.bfloat16)
        qkv_grad = qkv_grad + jnp.einsum(
            "td,tjc->jdc", normed_tree, grad_proj_all, preferred_element_type=jnp.float32
        )
        bias_grad = bias_grad + jnp.sum(grad_proj_all[:, 0::2].astype(jnp.float32), axis=0)
        grad_normed = lax.psum_scatter(
            jnp.einsum(
                "tjc,jdc->td", grad_proj_all, qkv_all, preferred_element_type=jnp.float32
            ).astype(jnp.bfloat16),
            "tensor",
            scatter_dimension=0,
            tiled=True,
        ).astype(jnp.float32)
        grad_from_in, gain_in, shift_in = norm_back(grad_normed, plain_in, scale_in, gains_all[0])
        input_grads.append(grad_mixed + grad_from_in)
        gain_grad = gain_grad + jnp.stack([gain_in, gain_mid])
        shift_grad = shift_grad + jnp.stack(
            [shift_in, shift_mid, jnp.sum(grad_mixed, axis=0), jnp.sum(grad_final, axis=0)]
        )
    weight_sums = (
        lax.psum_scatter(
            qkv_grad.astype(jnp.bfloat16), "fsdp", scatter_dimension=1, tiled=True
        ).astype(jnp.float32),
        lax.psum_scatter(
            bias_grad.reshape(2, head_count, -1).astype(jnp.bfloat16),
            "fsdp",
            scatter_dimension=2,
            tiled=True,
        ).astype(jnp.float32),
        lax.psum_scatter(
            out_grad.astype(jnp.bfloat16), "fsdp", scatter_dimension=1, tiled=True
        ).astype(jnp.float32),
    )
    up_final, down_final = (
        lax.psum_scatter(
            up_grad.astype(jnp.bfloat16), "fsdp", scatter_dimension=1, tiled=True
        ).astype(jnp.float32),
        lax.psum_scatter(
            down_grad.astype(jnp.bfloat16), "fsdp", scatter_dimension=2, tiled=True
        ).astype(jnp.float32),
    )
    small_sums = (
        lax.psum_scatter(gain_grad, ("fsdp", "tensor"), scatter_dimension=1, tiled=True),
        lax.psum_scatter(shift_grad, ("fsdp", "tensor"), scatter_dimension=1, tiled=True),
        lax.psum_scatter(router_grad, ("fsdp", "tensor"), scatter_dimension=0, tiled=True),
    )
    return (
        jnp.stack(results),
        jnp.stack(input_grads),
        weight_sums[0],
        weight_sums[1],
        weight_sums[2],
        small_sums[2],
        up_final,
        down_final,
        small_sums[0],
        small_sums[1][:3],
        small_sums[1][3],
    )


MESH = pl.DeviceIdType.MESH
BF = jnp.bfloat16
F32 = jnp.float32


def fits(mesh):
    return mesh.shape["fsdp"] == 8 and mesh.shape["tensor"] == 4


def flip(index, bit):
    return index + bit * (1 - 2 * (lax.rem(index // bit, 2)))


def place(fsdp, tensor):
    return {"fsdp": fsdp, "tensor": tensor}


def greet(partners):
    barrier = pltpu.get_barrier_semaphore()
    for fsdp, tensor in partners:
        pl.semaphore_signal(barrier, inc=1, device_id=place(fsdp, tensor), device_id_type=MESH)
    pl.semaphore_wait(barrier, len(partners))


def greet_all(mine):
    barrier = pltpu.get_barrier_semaphore()

    def signal(step, carry):
        other = lax.rem(mine + step, 32)
        pl.semaphore_signal(
            barrier, inc=1, device_id=place(other // 4, lax.rem(other, 4)), device_id_type=MESH
        )
        return carry

    lax.fori_loop(1, 32, signal, 0)
    pl.semaphore_wait(barrier, 31)


class Sender:
    def __init__(self, send_sem, recv_sem):
        self.send_sem, self.recv_sem, self.count = send_sem, recv_sem, 0
        self.open = []

    def copy(self, source, target, fsdp, tensor):
        made = pltpu.make_async_remote_copy(
            src_ref=source,
            dst_ref=target,
            send_sem=self.send_sem.at[self.count],
            recv_sem=self.recv_sem.at[self.count],
            device_id=place(fsdp, tensor),
            device_id_type=MESH,
        )
        self.count += 1
        made.start()
        self.open.append(made)
        return made

    def finish(self):
        for made in self.open:
            made.wait_send()


def attend_kernel(
    w4, small, tokens, up, down, bias,
    full4, params, rows_out, normed_out, q_out, k_out, v_out, heads_out, residual_out, probs_out,
    up_own, down_own,
    weights, pieces, table, rows_all, normed, queries, keys, values, heads, residual, probs, mask,
    send_sem, recv_sem, local_sem, up_send, up_recv, down_send, down_recv, trunk_send, trunk_recv,
):
    me_f, me_z = lax.axis_index("fsdp"), lax.axis_index("tensor")
    mine = me_f * 4 + me_z
    core = lax.rem(me_f, 2)
    greet_all(mine)
    sender = Sender(send_sem, recv_sem)

    def rows(fsdp):
        return pl.ds(pl.multiple_of(fsdp * 128, 128), 128)

    def cols(first, width):
        return pl.ds(pl.multiple_of(first * 256, 256), width)

    trunk_rows, halo_rows, own_rows = pl.ds(0, 256), pl.ds(256, 128), pl.ds(384, 256)
    first = [
        sender.copy(w4, weights.at[:, rows(me_f), cols(me_z, 256)], me_f, flip(me_z, 1)),
        sender.copy(small, pieces.at[me_f, me_z], me_f, flip(me_z, 1)),
    ]
    local = [
        pltpu.make_async_copy(w4, weights.at[:, rows(me_f), cols(me_z, 256)], local_sem.at[0]),
        pltpu.make_async_copy(small, pieces.at[me_f, me_z], local_sem.at[1]),
        pltpu.make_async_copy(tokens, rows_all.at[:, own_rows], local_sem.at[2]),
        pltpu.make_async_copy(bias, mask, local_sem.at[3]),
    ]
    for copy in local:
        copy.start()

    piece = [(micro, half) for micro in range(2) for half in range(2)]

    def trunk_copy(index, from_tokens):
        micro, half = piece[index]
        part = pl.ds(half * 128, 128)
        return pltpu.make_async_remote_copy(
            src_ref=tokens.at[micro, part] if from_tokens else rows_all.at[micro, part],
            dst_ref=rows_all.at[micro, part],
            send_sem=trunk_send.at[index],
            recv_sem=trunk_recv.at[index],
            device_id=place(me_f, lax.rem(me_z + 1, 4)),
            device_id_type=MESH,
        )

    halo_copy = pltpu.make_async_remote_copy(
        src_ref=tokens.at[:, pl.ds(128, 128)],
        dst_ref=rows_all.at[:, halo_rows],
        send_sem=trunk_send.at[4],
        recv_sem=trunk_recv.at[4],
        device_id=place(me_f, lax.rem(me_z + 1, 4)),
        device_id_type=MESH,
    )

    def expert_copies(step):
        other = lax.rem(mine + step, 32)
        fsdp, tensor = other // 4, lax.rem(other, 4)
        expert = 2 * tensor + fsdp // 4
        quarter = pl.ds(pl.multiple_of(lax.rem(fsdp, 4) * 256, 256), 256)
        return (
            (up.at[expert, :, quarter], up_own.at[rows(me_f), cols(me_z, 256)]),
            (down.at[expert, quarter, :], down_own.at[cols(me_z, 256), rows(me_f)]),
            (fsdp, tensor),
        )

    def remote(step):
        ups, downs, (fsdp, tensor) = expert_copies(step)
        return [
            pltpu.make_async_remote_copy(
                src_ref=pair[0], dst_ref=pair[1], send_sem=sems[0].at[step],
                recv_sem=sems[1].at[step], device_id=place(fsdp, tensor), device_id_type=MESH,
            )
            for pair, sems in ((ups, (up_send, up_recv)), (downs, (down_send, down_recv)))
        ]

    def start_step(step, carry):
        for copy in remote(step):
            copy.start()
        return carry

    for copy in first:
        copy.wait_recv()
    for copy in local:
        copy.wait()
    pair = me_z // 2 * 2
    second = [
        sender.copy(
            weights.at[:, rows(me_f), cols(pair, 512)], weights.at[:, rows(me_f), cols(pair, 512)],
            me_f, flip(me_z, 2),
        ),
        sender.copy(
            pieces.at[me_f, pl.ds(pair, 2)], pieces.at[me_f, pl.ds(pair, 2)], me_f, flip(me_z, 2)
        ),
    ]
    for copy in second:
        copy.wait_recv()

    across = flip(me_f, 2) * (1 - core) + flip(me_f, 4) * core
    along = flip(me_f, 4) * (1 - core) + flip(me_f, 2) * core

    def blocks(fsdp_list, target):
        made = []
        for fsdp in fsdp_list:
            view = weights.at[:, rows(fsdp)]
            made.append(sender.copy(view, view, target, me_z))
            made.append(sender.copy(pieces.at[fsdp], pieces.at[fsdp], target, me_z))
        return made

    third = blocks([me_f], across)

    @pl.when(me_z == 0)
    def _():
        for index in range(4):
            trunk_copy(index, True).start()

    @pl.when(me_z < 3)
    def _():
        halo_copy.start()

    for copy in third:
        copy.wait_recv()
    fourth = blocks([me_f, across], along)
    for index in range(4):
        @pl.when(me_z > 0)
        def _(index=index):
            trunk_copy(index, False).wait_recv()

        @pl.when((me_z > 0) & (me_z < 3))
        def _(index=index):
            trunk_copy(index, False).start()

    @pl.when(me_z > 0)
    def _():
        halo_copy.wait_recv()

    @pl.when(me_z == 0)
    def _():
        keep = [
            pltpu.make_async_copy(tokens, rows_all.at[:, trunk_rows], local_sem.at[0]),
            pltpu.make_async_copy(
                tokens.at[:, pl.ds(128, 128)], rows_all.at[:, halo_rows], local_sem.at[1]
            ),
        ]
        for copy in keep:
            copy.start()
        for copy in keep:
            copy.wait()

    for copy in fourth:
        copy.wait_recv()
    fifth = blocks([core, core + 2, core + 4, core + 6], flip(me_f, 1))
    lax.fori_loop(1, 32, start_step, 0)
    ups, downs, _ = expert_copies(0)
    own = [
        pltpu.make_async_copy(ups[0], ups[1], local_sem.at[4]),
        pltpu.make_async_copy(downs[0], downs[1], local_sem.at[5]),
    ]
    for copy in own:
        copy.start()

    for copy in fifth:
        copy.wait_recv()

    for fsdp in range(8):
        total = pieces[fsdp, 0, 0:16].astype(F32)
        for tensor in range(1, 4):
            total = total + pieces[fsdp, tensor, 0:16].astype(F32)
        table[0:16, fsdp * 128 : fsdp * 128 + 128] = total
    for tensor in range(4):
        total = pieces[0, tensor, 16:32].astype(F32)
        for fsdp in range(1, 8):
            total = total + pieces[fsdp, tensor, 16:32].astype(F32)
        for which in range(2):
            for half in range(2):
                lane = tensor * 256 + half * 128
                table[14 + which : 15 + which, lane : lane + 128] = total[
                    2 * which + half : 2 * which + half + 1, :
                ]
    saves = [
        pltpu.make_async_copy(weights, full4, local_sem.at[6]),
        pltpu.make_async_copy(table, params, local_sem.at[7]),
        pltpu.make_async_copy(rows_all, rows_out, local_sem.at[8]),
    ]
    for copy in saves:
        copy.start()

    def tile(index):
        return pl.ds(pl.multiple_of(index * 256, 256), 256)

    def lanes(index):
        return pl.ds(pl.multiple_of(index * 128, 128), 128)

    def one_tree(micro, carry):
        def norm(index, carry):
            value = rows_all[micro, lanes(index), :].astype(F32)
            centered = value - jnp.mean(value, axis=-1, keepdims=True)
            scale = lax.rsqrt(jnp.mean(centered * centered, axis=-1, keepdims=True) + EPSILON)
            out = centered * scale * table[0:1, :] + table[2:3, :]
            normed[micro, lanes(index), :] = out.astype(BF)
            return carry

        lax.fori_loop(0, 5, norm, 0)

        def project(index, carry):
            place_cols = tile(index)
            key = dot_nn(normed[micro], weights[1, :, place_cols])
            keys[micro, :, place_cols] = key.astype(BF)
            value = dot_nn(normed[micro], weights[2, :, place_cols]) + table[15:16, place_cols]
            values[micro, :, place_cols] = value.astype(BF)
            query = dot_nn(normed[micro, own_rows], weights[0, :, place_cols])
            queries[micro, :, place_cols] = (query + table[14:15, place_cols]).astype(BF)
            return carry

        lax.fori_loop(0, 4, project, 0)

        def two_heads(index, carry):
            query, key, value = (
                part[micro, :, lanes(index)] for part in (queries, keys, values)
            )
            low = lax.broadcasted_iota(jnp.int32, (256, 128), 1) < 64
            outs = []
            for which in range(2):
                one = jnp.where(low if which == 0 else ~low, query, jnp.zeros_like(query))
                scores = dot_nt(one, key) * 0.125 + mask[micro]
                exponent = jnp.exp(scores - jnp.max(scores, axis=-1, keepdims=True))
                total = jnp.sum(exponent, axis=-1, keepdims=True)
                weight = (exponent * (1.0 / total)).astype(BF)
                probs[micro, 2 * index + which] = weight
                outs.append(dot_nn(weight, value))
            heads[micro, :, lanes(index)] = jnp.where(low, outs[0], outs[1]).astype(BF)
            return carry

        lax.fori_loop(0, 8, two_heads, 0)

        def mix(index, carry):
            place_cols = tile(index)
            out = dot_nt(heads[micro], weights[3, place_cols, :])
            residual[micro, :, place_cols] = (
                rows_all[micro, own_rows, place_cols].astype(F32) + out + table[4:5, place_cols]
            )
            return carry

        lax.fori_loop(0, 4, mix, 0)
        return carry

    lax.fori_loop(0, 2, one_tree, 0)
    late = [
        (normed, normed_out), (queries, q_out), (keys, k_out), (values, v_out),
        (heads, heads_out), (residual, residual_out), (probs, probs_out),
    ]
    for index, (source, target) in enumerate(late):
        copy = pltpu.make_async_copy(source, target, local_sem.at[9 + index])
        copy.start()
        saves.append(copy)

    @pl.when((me_z > 0) & (me_z < 3))
    def _():
        for index in range(4):
            trunk_copy(index, False).wait_send()

    @pl.when(me_z == 0)
    def _():
        for index in range(4):
            trunk_copy(index, True).wait_send()

    @pl.when(me_z < 3)
    def _():
        halo_copy.wait_send()

    for copy in own:
        copy.wait()

    def end_step(step, carry):
        for copy in remote(step):
            copy.wait_send()
            copy.wait_recv()
        return carry

    lax.fori_loop(1, 32, end_step, 0)
    sender.finish()
    for copy in saves:
        copy.wait()


def any_spec(count):
    return [pl.BlockSpec(memory_space=pl.ANY)] * count


def attend_all(w4, small, tokens, up, down, bias):
    kept = [
        ((4, 1024, 1024), BF), ((16, 1024), F32), ((2, 640, 1024), BF), ((2, 640, 1024), BF),
        ((2, 256, 1024), BF), ((2, 640, 1024), BF), ((2, 640, 1024), BF), ((2, 256, 1024), BF),
        ((2, 256, 1024), F32), ((2, 16, 256, 640), BF),
    ]
    dma = pltpu.SemaphoreType.DMA
    return pl.pallas_call(
        attend_kernel,
        out_shape=[
            *(jax.ShapeDtypeStruct(shape, dtype) for shape, dtype in kept),
            jax.ShapeDtypeStruct((1024, 1024), BF),
            jax.ShapeDtypeStruct((1024, 1024), BF),
        ],
        in_specs=any_spec(6),
        out_specs=any_spec(12),
        scratch_shapes=[
            pltpu.VMEM(*kept[0]),
            pltpu.VMEM((8, 4, 32, 128), BF),
            *(pltpu.VMEM(shape, dtype) for shape, dtype in kept[1:]),
            pltpu.VMEM((2, 256, 640), F32),
            dma((20,)), dma((20,)), dma((16,)),
            dma((32,)), dma((32,)), dma((32,)), dma((32,)), dma((5,)), dma((5,)),
        ],
        compiler_params=pltpu.CompilerParams(
            collective_id=0, has_side_effects=True, vmem_limit_bytes=60 << 20
        ),
        name="attend",
    )(w4, small, tokens, up, down, bias)


def gelu_pair(hidden):
    scale = (2.0 / jnp.pi) ** 0.5
    square = hidden * hidden
    bend = jnp.tanh(scale * hidden * (1.0 + 0.044715 * square))
    half = 0.5 * (1.0 + bend)
    slope = half + 0.5 * hidden * (1.0 - bend * bend) * scale * (1.0 + 0.134145 * square)
    return hidden * half, slope


def dot_nn(left, right):
    return lax.dot_general(left, right, (((1,), (0,)), ((), ())), preferred_element_type=F32)


def dot_nt(left, right):
    return lax.dot_general(left, right, (((1,), (1,)), ((), ())), preferred_element_type=F32)


def dot_tn(left, right):
    return lax.dot_general(left, right, (((0,), (0,)), ((), ())), preferred_element_type=F32)


def expert_kernel(
    slots, up_hbm, down_hbm, returned, up_0, up_1, up_2, up_3, down_0, down_1, down_2, down_3,
    arrived, parts, got, got_x, up, down, up_sum, down_sum, act, slope,
    send_sem, recv_sem, local_sem,
):
    cap = slots.shape[3]
    group = 8 * cap
    rows = 2 * group
    me_f, me_z = lax.axis_index("fsdp"), lax.axis_index("tensor")
    me_y, me_x, core = me_f // 4, lax.rem(me_f // 2, 2), lax.rem(me_f, 2)
    far_x = 1 - me_x
    x_mate, core_mate = flip(me_f, 2), flip(me_f, 1)
    far = []
    for step in range(1, 8):
        far.append(
            (lax.rem(me_y + step // 4, 2) * 4 + lax.rem(me_f, 4), lax.rem(me_z + step, 4))
        )
    greet([(x_mate, me_z), (core_mate, me_z)] + far)
    sender = Sender(send_sem, recv_sem)
    load = [
        pltpu.make_async_copy(up_hbm, up, local_sem.at[0]),
        pltpu.make_async_copy(down_hbm, down, local_sem.at[1]),
    ]

    def origin_rows(fsdp, tensor):
        first = (fsdp // 4 * 4 + tensor) * cap
        return pl.ds(pl.multiple_of(first, cap), cap)

    chunks = [(kind, micro) for kind in range(2) for micro in range(2)]
    incoming, own_in = [], []

    def send_in(index):
        kind, micro = chunks[index]
        incoming.append([
            sender.copy(
                slots.at[kind, micro, 2 * tensor + fsdp // 4],
                arrived.at[kind, micro, me_x, core, origin_rows(me_f, me_z)],
                fsdp, tensor,
            )
            for fsdp, tensor in far
        ])
        own = pltpu.make_async_copy(
            slots.at[kind, micro, 2 * me_z + me_y],
            arrived.at[kind, micro, me_x, core, origin_rows(me_f, me_z)],
            local_sem.at[2 + index],
        )
        own.start()
        own_in.append(own)

    send_in(0)
    for copy in load:
        copy.start()

    def same_place(view, fsdp):
        return sender.copy(view, view, fsdp, me_z)

    across, beside, onward = {}, {}, {}

    def landed(index):
        kind, micro = chunks[index]
        for copy in incoming[index]:
            copy.wait_recv()
        own_in[index].wait()
        if index < 3:
            send_in(index + 1)
        view = arrived.at[kind, micro, me_x, core]
        across[index] = same_place(view, x_mate)
        beside[index] = same_place(view, core_mate)

    def forwarded(index):
        kind, micro = chunks[index]
        across[index].wait_recv()
        onward[index] = same_place(arrived.at[kind, micro, far_x, core], core_mate)

    def tile(index):
        return pl.ds(pl.multiple_of(index * 256, 256), 256)

    def forward(micro, side):
        data = arrived.at[0, micro, side]

        def first(index, carry):
            hidden = dot_nn(data[...].reshape(rows, 1024), up[:, tile(index)])
            value, slope_value = gelu_pair(hidden)
            act[micro, side, :, tile(index)] = value.astype(BF)
            slope[micro, side, :, tile(index)] = slope_value.astype(BF)
            return carry

        lax.fori_loop(0, 4, first, 0)

        def second(index, carry):
            out = dot_nn(act[micro, side], down[:, tile(index)])
            parts[0, micro, side, :, :, tile(index)] = out.astype(BF).reshape(2, group, 256)
            return carry

        lax.fori_loop(0, 4, second, 0)

    def backward(micro, side, begin):
        data = arrived.at[0, micro, side]
        grads = arrived.at[1, micro, side]

        def first(index, carry):
            grad = grads[...].reshape(rows, 1024)
            grad_act = dot_nt(grad, down[tile(index), :])
            grad_hidden = (
                grad_act * slope[micro, side, :, tile(index)].astype(F32)
            ).astype(BF)
            slope[micro, side, :, tile(index)] = grad_hidden
            down_part = dot_tn(act[micro, side, :, tile(index)], grad)
            up_part = dot_tn(data[...].reshape(rows, 1024), grad_hidden)
            if begin:
                down_sum[tile(index), :] = down_part
                up_sum[:, tile(index)] = up_part
            else:
                down_sum[tile(index), :] += down_part
                up_sum[:, tile(index)] += up_part
            return carry

        lax.fori_loop(0, 4, first, 0)

        def second(index, carry):
            out = dot_nt(slope[micro, side], up[tile(index), :])
            parts[1, micro, side, :, :, tile(index)] = out.astype(BF).reshape(2, group, 256)
            return carry

        lax.fori_loop(0, 4, second, 0)

    def result(kind, micro):
        return parts.at[kind, micro]

    core_back, x_back, home = {}, {}, {}

    def back_core(index):
        kind, micro = chunks[index]
        core_back[index] = sender.copy(
            result(kind, micro).at[:, 1 - core], got.at[kind, micro], core_mate, me_z
        )

    def add_rows(target, source):
        def step(row, carry):
            part = pl.ds(pl.multiple_of(row * cap, cap), cap)
            target[part] = (target[part].astype(F32) + source[part].astype(F32)).astype(BF)
            return carry

        lax.fori_loop(0, 8, step, 0)

    def back_x(index):
        kind, micro = chunks[index]
        core_back[index].wait_recv()
        mine = result(kind, micro)
        add_rows(mine.at[far_x, core], got.at[kind, micro, far_x])
        x_back[index] = sender.copy(
            mine.at[far_x, core], got_x.at[kind, micro], x_mate, me_z
        )
        add_rows(mine.at[me_x, core], got.at[kind, micro, me_x])

    def back_home(index):
        kind, micro = chunks[index]
        x_back[index].wait_recv()
        mine = result(kind, micro).at[me_x, core]
        add_rows(mine, got_x.at[kind, micro])
        target = returned.at[kind, micro, 2 * me_z + me_y]
        home[index] = [
            sender.copy(mine.at[origin_rows(fsdp, tensor)], target, fsdp, tensor)
            for fsdp, tensor in far
        ]
        own = pltpu.make_async_copy(
            mine.at[origin_rows(me_f, me_z)], target, local_sem.at[2 + index]
        )
        own.start()
        own_in[index] = own

    landed(0)
    for copy in load:
        copy.wait()
    beside[0].wait_recv()
    forward(0, me_x)
    landed(1)
    forwarded(0)
    beside[1].wait_recv()
    forward(1, me_x)
    onward[0].wait_recv()
    forward(0, far_x)
    back_core(0)
    landed(2)
    forwarded(1)
    back_x(0)
    onward[1].wait_recv()
    forward(1, far_x)
    back_core(1)
    beside[2].wait_recv()
    backward(0, me_x, True)
    landed(3)
    forwarded(2)
    back_x(1)
    back_home(0)
    onward[2].wait_recv()
    backward(0, far_x, False)
    back_core(2)
    forwarded(3)
    back_home(1)
    beside[3].wait_recv()
    backward(1, me_x, False)
    back_x(2)
    onward[3].wait_recv()
    backward(1, far_x, False)
    back_core(3)
    back_home(2)

    def narrow(index, carry):
        part = pl.ds(pl.multiple_of(index * 64, 64), 64)
        up[part, :] = up_sum[part, :].astype(BF)
        down[part, :] = down_sum[part, :].astype(BF)
        return carry

    lax.fori_loop(0, 16, narrow, 0)
    store = []
    for step, (up_part, down_part) in enumerate(
        ((up_0, down_0), (up_1, down_1), (up_2, down_2), (up_3, down_3))
    ):
        plane = lax.rem(me_z + step, 4)
        store.append(
            pltpu.make_async_copy(up.at[:, tile(plane)], up_part, local_sem.at[6 + 2 * step])
        )
        store.append(
            pltpu.make_async_copy(down.at[tile(plane), :], down_part, local_sem.at[7 + 2 * step])
        )
    for copy in store:
        copy.start()
    back_x(3)
    back_home(3)
    for index in range(4):
        for copy in home[index]:
            copy.wait_recv()
        own_in[index].wait()
    for copy in store:
        copy.wait()
    sender.finish()


def run_experts(slots, up_own, down_own):
    cap = slots.shape[3]
    group = 8 * cap
    dma = pltpu.SemaphoreType.DMA
    return pl.pallas_call(
        expert_kernel,
        out_shape=[
            jax.ShapeDtypeStruct(slots.shape, BF),
            *([jax.ShapeDtypeStruct((1024, 256), BF)] * 4),
            *([jax.ShapeDtypeStruct((256, 1024), BF)] * 4),
        ],
        in_specs=any_spec(3),
        out_specs=any_spec(9),
        scratch_shapes=[
            pltpu.VMEM((2, 2, 2, 2, group, 1024), BF),
            pltpu.VMEM((2, 2, 2, 2, group, 1024), BF),
            pltpu.VMEM((2, 2, 2, group, 1024), BF),
            pltpu.VMEM((2, 2, group, 1024), BF),
            pltpu.VMEM((1024, 1024), BF),
            pltpu.VMEM((1024, 1024), BF),
            pltpu.VMEM((1024, 1024), F32),
            pltpu.VMEM((1024, 1024), F32),
            pltpu.VMEM((2, 2, 2 * group, 1024), BF),
            pltpu.VMEM((2, 2, 2 * group, 1024), BF),
            dma((76,)), dma((76,)), dma((14,)),
        ],
        compiler_params=pltpu.CompilerParams(
            collective_id=1, has_side_effects=True, vmem_limit_bytes=63 << 20
        ),
        cost_estimate=pl.CostEstimate(
            flops=12 * 4 * group * 2 * 1024 * 1024, bytes_accessed=20 << 20, transcendentals=0
        ),
        name="experts",
    )(slots, up_own, down_own)


def scatter_kernel(
    up_0, up_1, up_2, up_3, down_0, down_1, down_2, down_3, grad4, small, trunk, halo,
    up_out, down_out, out4, small_out, trunk_out, halo_out,
    keep, got, cut, cut_got, cut_a, cut_got_a, small_got, trunk_got, trunk_own,
    send_sem, recv_sem, local_sem, up_send, up_recv, down_send, down_recv,
    small_send, small_recv, trunk_send, trunk_recv,
):
    me_f, me_z = lax.axis_index("fsdp"), lax.axis_index("tensor")
    mine = me_f * 4 + me_z
    core = lax.rem(me_f, 2)
    me_y, me_x = me_f // 4, lax.rem(me_f // 2, 2)
    greet_all(mine)
    sender = Sender(send_sem, recv_sem)

    def rows(fsdp):
        return pl.ds(pl.multiple_of(fsdp * 128, 128), 128)

    def cols(first, width):
        return pl.ds(pl.multiple_of(first * 256, 256), width)

    first = []
    for block in range(4):
        first.append(
            sender.copy(
                grad4.at[:, rows(2 * block + 1 - core)], got.at[block], flip(me_f, 1), me_z
            )
        )
    local = []
    for block in range(4):
        copy = pltpu.make_async_copy(
            grad4.at[:, rows(2 * block + core)], keep.at[block], local_sem.at[block]
        )
        copy.start()
        local.append(copy)
    own_trunk = pltpu.make_async_copy(trunk, trunk_own, local_sem.at[4])
    own_trunk.start()

    def trunk_copy(index, source):
        return pltpu.make_async_remote_copy(
            src_ref=source.at[index],
            dst_ref=trunk_got.at[index],
            send_sem=trunk_send.at[index],
            recv_sem=trunk_recv.at[index],
            device_id=place(me_f, lax.rem(me_z + 3, 4)),
            device_id_type=MESH,
        )

    halo_copy = pltpu.make_async_remote_copy(
        src_ref=halo,
        dst_ref=halo_out,
        send_sem=trunk_send.at[4],
        recv_sem=trunk_recv.at[4],
        device_id=place(me_f, lax.rem(me_z + 3, 4)),
        device_id_type=MESH,
    )

    @pl.when(me_z == 3)
    def _():
        for index in range(4):
            trunk_copy(index, trunk).start()

    @pl.when(me_z > 0)
    def _():
        halo_copy.start()

    def small_copy(step):
        other = lax.rem(mine + step, 32)
        return pltpu.make_async_remote_copy(
            src_ref=small.at[other], dst_ref=small_got.at[mine], send_sem=small_send.at[step],
            recv_sem=small_recv.at[step], device_id=place(other // 4, lax.rem(other, 4)),
            device_id_type=MESH,
        )

    def start_small(step, carry):
        small_copy(step).start()
        return carry

    lax.fori_loop(1, 32, start_small, 0)

    planes = ((up_0, down_0), (up_1, down_1), (up_2, down_2), (up_3, down_3))
    quarter = pl.ds(pl.multiple_of(lax.rem(me_f, 4) * 256, 256), 256)

    def pairs(fsdp, number):
        up_part, down_part = planes[number]
        expert = 2 * lax.rem(me_z + 4 - number, 4) + me_y
        return (
            (up_part.at[rows(fsdp), :], up_out.at[expert, :, quarter]),
            (down_part.at[:, rows(fsdp)], down_out.at[expert, quarter, :]),
        )

    def remote(step):
        fsdp = lax.rem(me_f + step, 8)
        made = []
        for number in range(4):
            for pair, sems in zip(
                pairs(fsdp, number), ((up_send, up_recv), (down_send, down_recv))
            ):
                made.append(
                    pltpu.make_async_remote_copy(
                        src_ref=pair[0], dst_ref=pair[1], send_sem=sems[0].at[step * 4 + number],
                        recv_sem=sems[1].at[step * 4 + number], device_id=place(fsdp, me_z),
                        device_id_type=MESH,
                    )
                )
        return made

    def start_step(step, carry):
        for copy in remote(step):
            copy.start()
        return carry

    own = [pltpu.make_async_copy(small.at[mine], small_got.at[mine], local_sem.at[5])]
    for number in range(4):
        for which, pair in enumerate(pairs(me_f, number)):
            own.append(
                pltpu.make_async_copy(pair[0], pair[1], local_sem.at[6 + 2 * number + which])
            )
    for copy in own:
        copy.start()

    def add_block(target, source):
        def step(index, carry):
            part = pl.ds(pl.multiple_of(index * 16, 16), 16)
            for which in range(4):
                target[which, part] = (
                    target[which, part].astype(F32) + source[which, part].astype(F32)
                ).astype(BF)
            return carry

        lax.fori_loop(0, 8, step, 0)

    for block in range(4):
        local[block].wait()
        first[block].wait_recv()
        add_block(keep.at[block], got.at[block])

    along = flip(me_f, 4) * (1 - core) + flip(me_f, 2) * core
    across = flip(me_f, 2) * (1 - core) + flip(me_f, 4) * core

    def block_of(fsdp):
        return fsdp // 2

    sent = [along, along * 0 + flip(across, 4) * (1 - core) + flip(across, 2) * core]
    kept = [me_f, across]
    second = []
    for index in range(2):
        second.append(
            sender.copy(keep.at[block_of(sent[index])], cut.at[index], along, me_z)
        )
    own_trunk.wait()
    for index in range(4):
        @pl.when(me_z < 3)
        def _(index=index):
            trunk_copy(index, trunk_own).wait_recv()

            def step(row, carry):
                part = pl.ds(pl.multiple_of(row * 16, 16), 16)
                trunk_own[index, part] = (
                    trunk_own[index, part].astype(F32) + trunk_got[index, part].astype(F32)
                ).astype(BF)
                return carry

            lax.fori_loop(0, 8, step, 0)

        @pl.when((me_z > 0) & (me_z < 3))
        def _(index=index):
            trunk_copy(index, trunk_own).start()

    for index in range(2):
        second[index].wait_recv()
        add_block(keep.at[block_of(kept[index])], cut.at[index])
    third = sender.copy(keep.at[block_of(across)], cut_got, across, me_z)
    lax.fori_loop(1, 8, start_step, 0)
    third.wait_recv()
    add_block(keep.at[block_of(me_f)], cut_got)
    mine4 = keep.at[block_of(me_f)]
    pair = me_z // 2 * 2
    other_pair = 2 - pair
    fourth = sender.copy(mine4.at[:, :, cols(other_pair, 512)], cut_a, me_f, flip(me_z, 2))
    fourth.wait_recv()

    def add_cols(source, begin, width, low):
        def step(index, carry):
            part = pl.ds(pl.multiple_of(index * 16, 16), 16)
            for which in range(4):
                mine4[which, part, cols(begin, width)] = (
                    mine4[which, part, cols(begin, width)].astype(F32)
                    + source[which, part, :].astype(F32)
                ).astype(BF)
            return carry

        lax.fori_loop(0, 8, step, 0)

    add_cols(cut_a, pair, 512, 0)
    fifth = sender.copy(
        mine4.at[:, :, cols(flip(me_z, 1), 256)], cut_got_a, me_f, flip(me_z, 1)
    )
    fifth.wait_recv()
    add_cols(cut_got_a, me_z, 256, 0)
    last = pltpu.make_async_copy(mine4.at[:, :, cols(me_z, 256)], out4, local_sem.at[0])
    last.start()

    @pl.when(me_z > 0)
    def _():
        for index in range(4):
            trunk_copy(index, trunk_own).wait_send()
        halo_copy.wait_send()

    @pl.when(me_z < 3)
    def _():
        halo_copy.wait_recv()

    trunk_done = pltpu.make_async_copy(trunk_own, trunk_out, local_sem.at[1])
    trunk_done.start()
    for copy in own:
        copy.wait()

    def end_small(step, carry):
        copy = small_copy(step)
        copy.wait_send()
        copy.wait_recv()
        return carry

    lax.fori_loop(1, 32, end_small, 0)

    def sum_small(index, total):
        return total + small_got[index]

    small_out[...] = lax.fori_loop(1, 32, sum_small, small_got[0])

    def end_step(step, carry):
        for copy in remote(step):
            copy.wait_send()
            copy.wait_recv()
        return carry

    lax.fori_loop(1, 8, end_step, 0)
    sender.finish()
    last.wait()
    trunk_done.wait()


def scatter_all(up_parts, down_parts, grad4, small, trunk, halo):
    dma = pltpu.SemaphoreType.DMA
    shapes = [
        jax.ShapeDtypeStruct((8, 128, 1024), BF),
        jax.ShapeDtypeStruct((8, 1024, 128), BF),
        jax.ShapeDtypeStruct((4, 128, 256), BF),
        jax.ShapeDtypeStruct((16, 128), F32),
        jax.ShapeDtypeStruct((4, 128, 1024), BF),
        jax.ShapeDtypeStruct((2, 128, 1024), BF),
    ]
    specs = any_spec(6)
    specs[3] = pl.BlockSpec(memory_space=pltpu.VMEM)
    return pl.pallas_call(
        scatter_kernel,
        out_shape=shapes,
        in_specs=any_spec(12),
        out_specs=specs,
        scratch_shapes=[
            pltpu.VMEM((4, 4, 128, 1024), BF),
            pltpu.VMEM((4, 4, 128, 1024), BF),
            pltpu.VMEM((2, 4, 128, 1024), BF),
            pltpu.VMEM((4, 128, 1024), BF),
            pltpu.VMEM((4, 128, 512), BF),
            pltpu.VMEM((4, 128, 256), BF),
            pltpu.VMEM((32, 16, 128), F32),
            pltpu.VMEM((4, 128, 1024), BF),
            pltpu.VMEM((4, 128, 1024), BF),
            dma((10,)), dma((10,)), dma((14,)),
            dma((32,)), dma((32,)), dma((32,)), dma((32,)),
            dma((32,)), dma((32,)), dma((5,)), dma((5,)),
        ],
        compiler_params=pltpu.CompilerParams(
            collective_id=3, has_side_effects=True, vmem_limit_bytes=48 << 20
        ),
        name="scatter_all",
    )(*up_parts, *down_parts, grad4, small, trunk, halo)


def fast_body(
    tokens, segment, route, w_qkv, bias_qv, w_o, w_router, w_up, w_down, norm_gains, shifts, cotangent
):
    micro_count, local_rows, width = tokens.shape
    expert_count = w_up.shape[0]
    cap = 3 * local_rows // (2 * expert_count)
    me_z = lax.axis_index("tensor")
    start = me_z * local_rows
    me_f = lax.axis_index("fsdp")
    lane = jnp.arange(128)
    mine = jnp.concatenate(
        [norm_gains, shifts, w_router.T, jnp.zeros((2, 32), BF)], axis=0
    )
    mine = jnp.where(lane // 32 == me_z, jnp.tile(mine, (1, 4)), 0)
    bias_lane = jnp.arange(64)
    bias_mine = jnp.where(bias_lane // 8 == me_f, jnp.tile(bias_qv, (1, 1, 8)), 0).reshape(4, 128)
    small = jnp.concatenate([mine, bias_mine, jnp.zeros((12, 128), BF)], axis=0)
    w4 = jnp.concatenate([w_qkv, w_o.T[None]], axis=0)
    own_index = start + jnp.arange(local_rows)
    key_index = jnp.concatenate([jnp.arange(256), start - 128 + jnp.arange(128), own_index])
    key_part = jnp.arange(640) < 256
    own_segs = lax.dynamic_slice_in_dim(segment, start, local_rows, axis=1)
    halo_segs = lax.dynamic_slice_in_dim(segment, jnp.maximum(start - 128, 0), 128, axis=1)
    key_segs = jnp.concatenate([segment[:, :256], halo_segs, own_segs], axis=1)
    query_seg, key_seg = own_segs[:, :, None], key_segs[:, None, :]
    allowed = (
        (key_seg == 0)
        | (key_seg == query_seg)
        | (query_seg >= 5) & (key_seg == (query_seg - 5) // 2 + 1)
    )
    allowed = allowed & (key_part | (key_index >= 256))[None, None, :]
    allowed = allowed & (key_index[None, :] <= own_index[:, None])[None]
    bias = jnp.where(allowed, 0.0, MASKED)
    (
        full4, params, rows_all, normed_all, queries, keys, values, heads_low, residual, probs_low,
        up_own, down_own,
    ) = attend_all(w4, small, tokens, w_up, w_down, bias)
    gains, offsets = params[:2], params[2:6]
    router_t = params[6:14].astype(BF)
    heads = (micro_count, -1, 16, 64)
    queries_h, keys_h, values_h = queries.reshape(heads), keys.reshape(heads), values.reshape(heads)
    normed_own = normed_all[:, 384:]
    _, plain_all, scale_all = norm_rows(rows_all.astype(F32), gains[0], offsets[0])
    plain_in, scale_in = plain_all[:, 384:], scale_all[:, 384:]
    probs = probs_low.astype(F32)
    normed_mid, plain_mid, scale_mid = norm_rows(residual, gains[1], offsets[1])
    mid_low = normed_mid.astype(BF)
    router_probs = jax.nn.softmax(
        jnp.einsum("mrd,ed->mre", mid_low, router_t, preferred_element_type=F32), axis=-1
    )
    own_routes = lax.dynamic_slice_in_dim(route[:, :, 0], start, local_rows, axis=1)
    own_choice = own_routes[:, :, None] == jnp.arange(expert_count)
    gate = jnp.sum(jnp.where(own_choice, router_probs, 0.0), axis=-1)
    grad_final = cotangent.astype(F32)
    grad_returned = (gate[..., None] * grad_final).astype(BF)
    running = jnp.cumsum(own_choice.astype(jnp.int32), axis=1)
    slot = own_routes * cap + jnp.sum(jnp.where(own_choice, running, 0), axis=-1) - 1
    pick = (slot[:, None, :] == jnp.arange(expert_count * cap)[None, :, None]).astype(BF)
    sending = jnp.stack([mid_low, grad_returned])
    slots = (
        jnp.einsum("msr,kmrd->kmsd", pick, sending, preferred_element_type=F32)
        .astype(BF)
        .reshape(2, micro_count, expert_count, cap, width)
    )
    back, *expert_grads = run_experts(slots, up_own, down_own)
    up_parts, down_parts = (
        [
            lax.ppermute(part, "tensor", [(z, (z + step) % 4) for z in range(4)]) if step else part
            for step, part in enumerate(group)
        ]
        for group in (expert_grads[:4], expert_grads[4:])
    )
    back = back.reshape(2, micro_count, expert_count * cap, width)
    rows_back = jnp.einsum("msr,kmsd->kmrd", pick, back, preferred_element_type=F32)
    returned, grad_mid = rows_back[0], rows_back[1]
    output = (residual + gate[..., None] * returned + offsets[3]).astype(BF)
    grad_gate = jnp.sum(grad_final * returned, axis=-1)
    grad_logits = router_probs * (
        jnp.where(own_choice, grad_gate[..., None], 0.0) - (gate * grad_gate)[..., None]
    )
    router_grad = jnp.einsum(
        "mrd,mre->ed", mid_low.astype(F32), grad_logits, precision=HIGHEST
    )
    grad_mid = grad_mid + jnp.einsum(
        "mre,ed->mrd", grad_logits, router_t.astype(F32), precision=HIGHEST
    )

    def flat(value):
        return value.reshape(-1, value.shape[-1])

    grad_from_mid, gain_mid, shift_mid = norm_back(
        flat(grad_mid), flat(plain_mid), flat(scale_mid), gains[1]
    )
    grad_mixed = grad_final + grad_from_mid.reshape(grad_final.shape)
    proj = grad_mixed.astype(BF)
    out_grad_t = jnp.einsum("mrd,mrc->dc", proj, heads_low, preferred_element_type=F32)
    grad_heads = jnp.einsum("mrd,dc->mrc", proj, full4[3], preferred_element_type=F32).astype(BF)
    grad_heads_h = grad_heads.reshape(heads)
    grad_probs = jnp.einsum("mqhd,mkhd->mhqk", grad_heads_h, values_h, preferred_element_type=F32)
    grad_scores = (
        probs * (grad_probs - jnp.sum(probs * grad_probs, axis=-1, keepdims=True))
    ).astype(BF)
    grad_queries = (
        jnp.einsum("mhqk,mkhd->mqhd", grad_scores, keys_h, preferred_element_type=F32) * 0.125
    ).astype(BF).reshape(micro_count, -1, width)
    grad_keys = (
        jnp.einsum("mhqk,mqhd->mkhd", grad_scores, queries_h, preferred_element_type=F32) * 0.125
    ).astype(BF).reshape(micro_count, -1, width)
    grad_values = (
        jnp.einsum("mhqk,mqhd->mkhd", probs_low, grad_heads_h, preferred_element_type=F32)
    ).astype(BF).reshape(micro_count, -1, width)
    grad4 = jnp.stack([
        jnp.einsum("mrd,mrc->dc", normed_own, grad_queries, preferred_element_type=F32).astype(BF),
        jnp.einsum("mrd,mrc->dc", normed_all, grad_keys, preferred_element_type=F32).astype(BF),
        jnp.einsum("mrd,mrc->dc", normed_all, grad_values, preferred_element_type=F32).astype(BF),
        out_grad_t.astype(BF),
    ])
    bias_grad = jnp.stack([
        jnp.sum(grad_queries.astype(F32), axis=(0, 1)),
        jnp.sum(grad_values.astype(F32), axis=(0, 1)),
    ])
    grad_all = jnp.einsum(
        "mrc,dc->mrd", grad_keys, full4[1], preferred_element_type=F32
    ) + jnp.einsum("mrc,dc->mrd", grad_values, full4[2], preferred_element_type=F32)
    grad_own = grad_all[:, 384:] + jnp.einsum(
        "mrc,dc->mrd", grad_queries, full4[0], preferred_element_type=F32
    )
    early = jnp.concatenate([
        jnp.stack([jnp.zeros((width,), F32), gain_mid]),
        jnp.stack([
            jnp.zeros((width,), F32), shift_mid,
            jnp.sum(grad_mixed, axis=(0, 1)), jnp.sum(grad_final, axis=(0, 1)),
        ]),
        router_grad,
    ])
    plain_halo, plain_trunk = plain_all[:, 256:384], plain_all[:, :256]
    grad_trunk, grad_halo = grad_all[:, :256], grad_all[:, 256:384]
    early = early.at[0].set(
        jnp.sum(grad_all * plain_all, axis=(0, 1))
        + jnp.sum((grad_own - grad_all[:, 384:]) * plain_in, axis=(0, 1))
    )
    early = early.at[2].set(
        jnp.sum(grad_all, axis=(0, 1)) + jnp.sum(grad_own - grad_all[:, 384:], axis=(0, 1))
    )
    small_grad = early.reshape(14, 32, 32).transpose(1, 0, 2)
    bias_small = (
        bias_grad.reshape(2, 4, 4, 8, 8).transpose(3, 1, 0, 2, 4).reshape(32, 2, 32)
    )
    small_grad = jnp.pad(
        jnp.concatenate([small_grad, bias_small], axis=1), ((0, 0), (0, 0), (0, 96))
    )
    up_out, down_out, out4, small_out, trunk_sum, halo_sum = scatter_all(
        up_parts, down_parts, grad4, small_grad,
        grad_trunk.astype(BF).reshape(4, 128, width), grad_halo.astype(BF),
    )
    trunk_sum = trunk_sum.reshape(2, 256, width).astype(F32)
    grad_normed = grad_own + jnp.where(me_z == 0, trunk_sum, 0.0)
    grad_normed = grad_normed.at[:, 128:].add(jnp.where(me_z < 3, halo_sum.astype(F32), 0.0))
    grad_from_in, _, _ = norm_back(flat(grad_normed), flat(plain_in), flat(scale_in), gains[0])
    input_grad = grad_mixed + grad_from_in.reshape(grad_mixed.shape)
    small_out = small_out[:, :32]
    return (
        output,
        input_grad,
        out4[:3].astype(F32),
        small_out[14:16].reshape(2, 4, 8),
        out4[3].T.astype(F32),
        small_out[6:14].T,
        up_out.astype(F32),
        down_out.astype(F32),
        small_out[:2],
        small_out[2:5],
        small_out[5],
    )


def solution(mesh):
    placed = (
        P(None, ("fsdp", "tensor"), None),
        P(None, "fsdp"),
        P(None, "fsdp", None),
        P(None, "fsdp", "tensor"),
        P(None, "tensor", "fsdp"),
        P("tensor", "fsdp"),
        P(("fsdp", "tensor"), None),
        P(None, "fsdp", "tensor"),
        P(None, "tensor", "fsdp"),
        P(None, ("fsdp", "tensor")),
        P(None, ("fsdp", "tensor")),
        P(None, ("fsdp", "tensor"), None),
    )
    return jax.shard_map(
        fast_body if fits(mesh) else plain_body,
        mesh=mesh,
        in_specs=placed,
        out_specs=(
            P(None, ("fsdp", "tensor"), None),
            P(None, ("fsdp", "tensor"), None),
            P(None, "fsdp", "tensor"),
            P(None, "tensor", "fsdp"),
            P("tensor", "fsdp"),
            P(("fsdp", "tensor"), None),
            P(None, "fsdp", "tensor"),
            P(None, "tensor", "fsdp"),
            P(None, ("fsdp", "tensor")),
            P(None, ("fsdp", "tensor")),
            P(("fsdp", "tensor")),
        ),
        check_vma=False,
    )
```

```python
from functools import partial

import jax
import jax.numpy as jnp
from jax import lax
from jax.experimental import pallas as pl
from jax.experimental.pallas import tpu as pltpu
from jax.sharding import PartitionSpec as P

EPSILON = 1e-05
MASKED = -1e30
HIGHEST = lax.Precision.HIGHEST


def norm_rows(row_data, gain_row, shift_row):
    centered = row_data - jnp.mean(row_data, axis=-1, keepdims=True)
    inv_scale = lax.rsqrt(jnp.mean(centered * centered, axis=-1, keepdims=True) + EPSILON)
    normed = centered * inv_scale
    return (normed * gain_row + shift_row, normed, inv_scale)


def norm_back(grad_out, normed, inv_scale, gain_row):
    grad_normed = grad_out * gain_row
    interior = (
        grad_normed
        - jnp.mean(grad_normed, axis=-1, keepdims=True)
        - normed * jnp.mean(grad_normed * normed, axis=-1, keepdims=True)
    )
    return (inv_scale * interior, jnp.sum(grad_out * normed, axis=0), jnp.sum(grad_out, axis=0))


def tree_allowed(query_segs, key_segs, row_start):
    query_seg = query_segs[:, None]
    key_seg = key_segs[None, :]
    related = (
        (key_seg == 0)
        | (key_seg == query_seg)
        | (query_seg >= 5) & (key_seg == (query_seg - 5) // 2 + 1)
    )
    row_index = row_start + jnp.arange(query_segs.shape[0])[:, None]
    col_index = jnp.arange(key_segs.shape[0])[None, :]
    return related & (col_index <= row_index)


def block_scores(queries, key_rows, allowed, factor):
    scaled = (
        jnp.einsum("qhd,khd->hqk", queries, key_rows, preferred_element_type=jnp.float32) * factor
    )
    return jnp.where(allowed[None], scaled, MASKED)


def attend_forward(queries, key_rows, value_rows, segments, block_len):
    tree_len = queries.shape[0]
    factor = queries.shape[-1] ** (-0.5)
    outputs, totals = ([], [])
    for row_start in range(0, tree_len, block_len):
        row_stop = row_start + block_len
        allowed = tree_allowed(segments[row_start:row_stop], segments[:row_stop], row_start)
        scores = block_scores(queries[row_start:row_stop], key_rows[:row_stop], allowed, factor)
        peak_score = jnp.max(scores, axis=-1, keepdims=True)
        exponent = jnp.exp(scores - peak_score)
        denom_sum = jnp.sum(exponent, axis=-1, keepdims=True)
        weights = (exponent / denom_sum).astype(jnp.bfloat16)
        outputs.append(
            jnp.einsum(
                "hqk,khd->qhd", weights, value_rows[:row_stop], preferred_element_type=jnp.float32
            )
        )
        totals.append(peak_score + jnp.log(denom_sum))
    return (jnp.concatenate(outputs, axis=0), jnp.concatenate(totals, axis=1))


def attend_backward(queries, key_rows, value_rows, segments, grad_heads, log_sums, block_len):
    tree_len = queries.shape[0]
    factor = queries.shape[-1] ** (-0.5)
    grad_keys = jnp.zeros(key_rows.shape, jnp.float32)
    grad_values = jnp.zeros(value_rows.shape, jnp.float32)
    grad_queries = []
    for row_start in range(0, tree_len, block_len):
        row_stop = row_start + block_len
        allowed = tree_allowed(segments[row_start:row_stop], segments[:row_stop], row_start)
        scores = block_scores(queries[row_start:row_stop], key_rows[:row_stop], allowed, factor)
        weights = jnp.exp(scores - log_sums[:, row_start:row_stop])
        grad_weights = jnp.einsum(
            "qhd,khd->hqk",
            grad_heads[row_start:row_stop],
            value_rows[:row_stop],
            preferred_element_type=jnp.float32,
        )
        grad_scores = (
            weights * (grad_weights - jnp.sum(weights * grad_weights, axis=-1, keepdims=True))
        ).astype(jnp.bfloat16)
        grad_queries.append(
            jnp.einsum(
                "hqk,khd->qhd", grad_scores, key_rows[:row_stop], preferred_element_type=jnp.float32
            )
            * factor
        )
        grad_keys = grad_keys.at[:row_stop].add(
            jnp.einsum(
                "hqk,qhd->khd",
                grad_scores,
                queries[row_start:row_stop],
                preferred_element_type=jnp.float32,
            )
            * factor
        )
        grad_values = grad_values.at[:row_stop].add(
            jnp.einsum(
                "hqk,qhd->khd",
                weights.astype(jnp.bfloat16),
                grad_heads[row_start:row_stop],
                preferred_element_type=jnp.float32,
            )
        )
    return (jnp.concatenate(grad_queries, axis=0), grad_keys, grad_values)


def gelu_back(hidden, grad_act):
    return jax.vjp(partial(jax.nn.gelu, approximate=True), hidden)[1](grad_act)[0].astype(
        jnp.bfloat16
    )


def plain_body(
    tokens,
    segment,
    route,
    w_qkv,
    bias_qv,
    w_o,
    w_router,
    w_up,
    w_down,
    norm_gains,
    shifts,
    cotangent,
):
    micro_count, local_rows, model_width = tokens.shape
    tree_len = segment.shape[1]
    block_len = min(512, tree_len)
    expert_count = w_up.shape[0]
    tensor_count = lax.axis_size("tensor")
    local_cap = max(2, 3 * local_rows // (2 * expert_count))
    tree_cap = tensor_count * local_cap
    slot_count = expert_count * tree_cap
    position = lax.axis_index("tensor") * local_rows
    gains_all, shifts_all, router_all = (
        lax.all_gather(norm_gains, ("fsdp", "tensor"), axis=1, tiled=True),
        lax.all_gather(shifts, ("fsdp", "tensor"), axis=1, tiled=True),
        lax.all_gather(w_router, ("fsdp", "tensor"), axis=0, tiled=True),
    )
    gains_all = gains_all.astype(jnp.float32)
    shifts_all = shifts_all.astype(jnp.float32)
    router_wide = router_all.astype(jnp.float32)
    qkv_all, bias_all, out_all = (
        lax.all_gather(w_qkv, "fsdp", axis=1, tiled=True),
        lax.all_gather(bias_qv, "fsdp", axis=2, tiled=True),
        lax.all_gather(w_o, "fsdp", axis=1, tiled=True),
    )
    head_width = qkv_all.shape[2]
    head_count = bias_all.shape[1]
    bias_rows = bias_all.reshape(2, head_width).astype(jnp.float32)
    qkv_bias = jnp.stack([bias_rows[0], jnp.zeros_like(bias_rows[0]), bias_rows[1]])
    up_grad = jnp.zeros((expert_count, model_width, w_up.shape[2]), jnp.float32)
    down_grad = jnp.zeros((expert_count, w_down.shape[1], model_width), jnp.float32)
    qkv_grad = jnp.zeros(qkv_all.shape, jnp.float32)
    bias_grad = jnp.zeros((2, head_width), jnp.float32)
    out_grad = jnp.zeros(out_all.shape, jnp.float32)
    router_grad = jnp.zeros(router_wide.shape, jnp.float32)
    gain_grad = jnp.zeros(gains_all.shape, jnp.float32)
    shift_grad = jnp.zeros(shifts_all.shape, jnp.float32)
    expert_ids = jnp.arange(expert_count, dtype=jnp.int32)
    results, input_grads = ([], [])
    for micro_index in range(micro_count):
        segments = segment[micro_index]
        routes_all = route[micro_index, :, 0]
        inputs = tokens[micro_index].astype(jnp.float32)
        normed_in, plain_in, scale_in = norm_rows(inputs, gains_all[0], shifts_all[0])
        normed_tree = lax.all_gather(normed_in.astype(jnp.bfloat16), "tensor", axis=0, tiled=True)
        projected = (
            jnp.einsum("td,jdc->tjc", normed_tree, qkv_all, preferred_element_type=jnp.float32)
            + qkv_bias
        ).astype(jnp.bfloat16)
        queries = projected[:, 0].reshape(tree_len, head_count, -1)
        key_rows = projected[:, 1].reshape(tree_len, head_count, -1)
        value_rows = projected[:, 2].reshape(tree_len, head_count, -1)
        attended, log_sums = attend_forward(queries, key_rows, value_rows, segments, block_len)
        heads_low = attended.reshape(tree_len, head_width).astype(jnp.bfloat16)
        attention_rows = lax.psum_scatter(
            jnp.dot(heads_low, out_all, preferred_element_type=jnp.float32).astype(jnp.bfloat16),
            "tensor",
            scatter_dimension=0,
            tiled=True,
        ).astype(jnp.float32)
        residual = inputs + attention_rows + shifts_all[2]
        normed_mid, plain_mid, scale_mid = norm_rows(residual, gains_all[1], shifts_all[1])
        mid_low = normed_mid.astype(jnp.bfloat16)
        router_probs = jax.nn.softmax(
            jnp.dot(mid_low, router_all, preferred_element_type=jnp.float32), axis=-1
        )
        own_routes = lax.dynamic_slice_in_dim(routes_all, position, local_rows)
        own_choice = own_routes[:, None] == expert_ids[None, :]
        gate_value = jnp.sum(jnp.where(own_choice, router_probs, 0.0), axis=-1)
        grad_final = cotangent[micro_index].astype(jnp.float32)
        grad_returned = (gate_value[:, None] * grad_final).astype(jnp.bfloat16)
        up_all, down_all = (
            lax.all_gather(w_up, "fsdp", axis=1, tiled=True),
            lax.all_gather(w_down, "fsdp", axis=2, tiled=True),
        )
        chosen = routes_all[:, None] == expert_ids[None, :]
        running = jnp.cumsum(chosen.astype(jnp.int32), axis=0)
        slot_index = routes_all * tree_cap + jnp.sum(jnp.where(chosen, running, 0), axis=-1) - 1
        slot_token = (
            jnp.zeros((slot_count,), jnp.int32)
            .at[slot_index]
            .set(jnp.arange(tree_len, dtype=jnp.int32))
        )
        slot_filled = jnp.zeros((slot_count,), jnp.bool_).at[slot_index].set(True)
        mid_tree = lax.all_gather(mid_low, "tensor", axis=0, tiled=True)
        routed = jnp.where(slot_filled[:, None], mid_tree[slot_token], 0).reshape(
            expert_count, tree_cap, model_width
        )
        hidden = jnp.einsum("ecd,edf->ecf", routed, up_all, preferred_element_type=jnp.float32)
        activated = jax.nn.gelu(hidden, approximate=True).astype(jnp.bfloat16)
        expert_rows = jnp.einsum(
            "ecf,efd->ecd", activated, down_all, preferred_element_type=jnp.float32
        ).reshape(slot_count, model_width)
        returned = lax.psum_scatter(
            expert_rows[slot_index].astype(jnp.bfloat16), "tensor", scatter_dimension=0, tiled=True
        ).astype(jnp.float32)
        grad_tree = lax.all_gather(grad_returned, "tensor", axis=0, tiled=True)
        grad_expert = jnp.where(slot_filled[:, None], grad_tree[slot_token], 0).reshape(
            expert_count, tree_cap, model_width
        )
        down_grad = down_grad + jnp.einsum(
            "ecf,ecd->efd", activated, grad_expert, preferred_element_type=jnp.float32
        )
        grad_act = jnp.einsum(
            "ecd,efd->ecf", grad_expert, down_all, preferred_element_type=jnp.float32
        )
        grad_hidden = gelu_back(hidden, grad_act)
        up_grad = up_grad + jnp.einsum(
            "ecd,ecf->edf", routed, grad_hidden, preferred_element_type=jnp.float32
        )
        grad_routed = jnp.einsum(
            "ecf,edf->ecd", grad_hidden, up_all, preferred_element_type=jnp.float32
        ).reshape(slot_count, model_width)
        grad_mid = lax.psum_scatter(
            grad_routed[slot_index].astype(jnp.bfloat16), "tensor", scatter_dimension=0, tiled=True
        ).astype(jnp.float32)
        results.append(
            (residual + gate_value[:, None] * returned + shifts_all[3]).astype(jnp.bfloat16)
        )
        grad_gate = jnp.sum(grad_final * returned, axis=-1)
        grad_logits = router_probs * (
            jnp.where(own_choice, grad_gate[:, None], 0.0) - (gate_value * grad_gate)[:, None]
        )
        router_grad = router_grad + jnp.einsum(
            "td,te->de", mid_low.astype(jnp.float32), grad_logits, precision=HIGHEST
        )
        grad_mid = grad_mid + jnp.einsum("te,de->td", grad_logits, router_wide, precision=HIGHEST)
        grad_from_mid, gain_mid, shift_mid = norm_back(grad_mid, plain_mid, scale_mid, gains_all[1])
        grad_mixed = grad_final + grad_from_mid
        proj_tree = lax.all_gather(grad_mixed.astype(jnp.bfloat16), "tensor", axis=0, tiled=True)
        out_grad = out_grad + jnp.einsum(
            "tc,td->cd", heads_low, proj_tree, preferred_element_type=jnp.float32
        )
        grad_heads = jnp.einsum(
            "td,cd->tc", proj_tree, out_all, preferred_element_type=jnp.float32
        ).astype(jnp.bfloat16)
        grad_queries, grad_keys, grad_values = attend_backward(
            queries,
            key_rows,
            value_rows,
            segments,
            grad_heads.reshape(tree_len, head_count, -1),
            log_sums,
            block_len,
        )
        grad_proj_all = jnp.stack(
            [
                grad_queries.reshape(tree_len, head_width),
                grad_keys.reshape(tree_len, head_width),
                grad_values.reshape(tree_len, head_width),
            ],
            axis=1,
        ).astype(jnp.bfloat16)
        qkv_grad = qkv_grad + jnp.einsum(
            "td,tjc->jdc", normed_tree, grad_proj_all, preferred_element_type=jnp.float32
        )
        bias_grad = bias_grad + jnp.sum(grad_proj_all[:, 0::2].astype(jnp.float32), axis=0)
        grad_normed = lax.psum_scatter(
            jnp.einsum(
                "tjc,jdc->td", grad_proj_all, qkv_all, preferred_element_type=jnp.float32
            ).astype(jnp.bfloat16),
            "tensor",
            scatter_dimension=0,
            tiled=True,
        ).astype(jnp.float32)
        grad_from_in, gain_in, shift_in = norm_back(grad_normed, plain_in, scale_in, gains_all[0])
        input_grads.append(grad_mixed + grad_from_in)
        gain_grad = gain_grad + jnp.stack([gain_in, gain_mid])
        shift_grad = shift_grad + jnp.stack(
            [shift_in, shift_mid, jnp.sum(grad_mixed, axis=0), jnp.sum(grad_final, axis=0)]
        )
    weight_sums = (
        lax.psum_scatter(
            qkv_grad.astype(jnp.bfloat16), "fsdp", scatter_dimension=1, tiled=True
        ).astype(jnp.float32),
        lax.psum_scatter(
            bias_grad.reshape(2, head_count, -1).astype(jnp.bfloat16),
            "fsdp",
            scatter_dimension=2,
            tiled=True,
        ).astype(jnp.float32),
        lax.psum_scatter(
            out_grad.astype(jnp.bfloat16), "fsdp", scatter_dimension=1, tiled=True
        ).astype(jnp.float32),
    )
    up_final, down_final = (
        lax.psum_scatter(
            up_grad.astype(jnp.bfloat16), "fsdp", scatter_dimension=1, tiled=True
        ).astype(jnp.float32),
        lax.psum_scatter(
            down_grad.astype(jnp.bfloat16), "fsdp", scatter_dimension=2, tiled=True
        ).astype(jnp.float32),
    )
    small_sums = (
        lax.psum_scatter(gain_grad, ("fsdp", "tensor"), scatter_dimension=1, tiled=True),
        lax.psum_scatter(shift_grad, ("fsdp", "tensor"), scatter_dimension=1, tiled=True),
        lax.psum_scatter(router_grad, ("fsdp", "tensor"), scatter_dimension=0, tiled=True),
    )
    return (
        jnp.stack(results),
        jnp.stack(input_grads),
        weight_sums[0],
        weight_sums[1],
        weight_sums[2],
        small_sums[2],
        up_final,
        down_final,
        small_sums[0],
        small_sums[1][:3],
        small_sums[1][3],
    )


MESH = pl.DeviceIdType.MESH
BF = jnp.bfloat16
F32 = jnp.float32


def fits(mesh):
    return mesh.shape["fsdp"] == 8 and mesh.shape["tensor"] == 4


def flip(index, bit):
    return index + bit * (1 - 2 * (lax.rem(index // bit, 2)))


def place(fsdp, tensor):
    return {"fsdp": fsdp, "tensor": tensor}


def greet(partners):
    barrier = pltpu.get_barrier_semaphore()
    for fsdp, tensor in partners:
        pl.semaphore_signal(barrier, inc=1, device_id=place(fsdp, tensor), device_id_type=MESH)
    pl.semaphore_wait(barrier, len(partners))


def greet_all(mine):
    barrier = pltpu.get_barrier_semaphore()

    def signal(step, carry):
        other = lax.rem(mine + step, 32)
        pl.semaphore_signal(
            barrier, inc=1, device_id=place(other // 4, lax.rem(other, 4)), device_id_type=MESH
        )
        return carry

    lax.fori_loop(1, 32, signal, 0)
    pl.semaphore_wait(barrier, 31)


class Sender:
    def __init__(self, send_sem, recv_sem):
        self.send_sem, self.recv_sem, self.count = send_sem, recv_sem, 0
        self.open = []

    def copy(self, source, target, fsdp, tensor, when=None):
        made = pltpu.make_async_remote_copy(
            src_ref=source,
            dst_ref=target,
            send_sem=self.send_sem.at[self.count],
            recv_sem=self.recv_sem.at[self.count],
            device_id=place(fsdp, tensor),
            device_id_type=MESH,
        )
        self.count += 1
        if when is None:
            made.start()
        else:
            pl.when(when)(made.start)
        self.open.append((made, when))
        return made

    def finish(self):
        for made, when in self.open:
            if when is None:
                made.wait_send()
            else:
                pl.when(when)(made.wait_send)


def attend_kernel(
    w4, small, tokens, up, down, bias, chosen_hbm, cotangent,
    full4, params, rows_out, normed_out, q_out, k_out, v_out, heads_out, residual_out, probs_out,
    slots_out, pick_out, gates_out, up_own, down_own,
    weights, pieces, table, rows_all, normed, queries, keys, values, heads, residual, probs,
    slots, pick, gates, mask, chosen, grads, router,
    send_sem, recv_sem, local_sem, up_send, up_recv, down_send, down_recv, trunk_send, trunk_recv,
):
    cap = slots.shape[2] // 8
    me_f, me_z = lax.axis_index("fsdp"), lax.axis_index("tensor")
    mine = me_f * 4 + me_z
    core = lax.rem(me_f, 2)
    greet_all(mine)
    sender = Sender(send_sem, recv_sem)

    def rows(fsdp):
        return pl.ds(pl.multiple_of(fsdp * 128, 128), 128)

    def cols(first, width):
        return pl.ds(pl.multiple_of(first * 256, 256), width)

    trunk_rows, halo_rows, own_rows = pl.ds(0, 256), pl.ds(256, 128), pl.ds(384, 256)
    first = [
        sender.copy(w4, weights.at[:, rows(me_f), cols(me_z, 256)], me_f, flip(me_z, 1)),
        sender.copy(small, pieces.at[me_f, me_z], me_f, flip(me_z, 1)),
    ]
    local = [
        pltpu.make_async_copy(w4, weights.at[:, rows(me_f), cols(me_z, 256)], local_sem.at[0]),
        pltpu.make_async_copy(small, pieces.at[me_f, me_z], local_sem.at[1]),
        pltpu.make_async_copy(tokens, rows_all.at[:, own_rows], local_sem.at[2]),
        pltpu.make_async_copy(bias, mask, local_sem.at[3]),
        pltpu.make_async_copy(chosen_hbm, chosen, local_sem.at[16]),
        pltpu.make_async_copy(cotangent, grads, local_sem.at[17]),
    ]
    for copy in local:
        copy.start()

    piece = [(micro, half) for micro in range(2) for half in range(2)]

    def trunk_copy(index, from_tokens):
        micro, half = piece[index]
        part = pl.ds(half * 128, 128)
        return pltpu.make_async_remote_copy(
            src_ref=tokens.at[micro, part] if from_tokens else rows_all.at[micro, part],
            dst_ref=rows_all.at[micro, part],
            send_sem=trunk_send.at[index],
            recv_sem=trunk_recv.at[index],
            device_id=place(me_f, lax.rem(me_z + 1, 4)),
            device_id_type=MESH,
        )

    halo_copy = pltpu.make_async_remote_copy(
        src_ref=tokens.at[:, pl.ds(128, 128)],
        dst_ref=rows_all.at[:, halo_rows],
        send_sem=trunk_send.at[4],
        recv_sem=trunk_recv.at[4],
        device_id=place(me_f, lax.rem(me_z + 1, 4)),
        device_id_type=MESH,
    )

    def expert_copies(step):
        fsdp = (
            lax.rem(me_f // 4 + step // 16, 2) * 4
            + lax.rem(me_f // 2 + step // 8, 2) * 2
            + lax.rem(me_f + step // 4, 2)
        )
        tensor = lax.rem(me_z + step, 4)
        expert = 2 * tensor + fsdp // 4
        quarter = pl.ds(pl.multiple_of(lax.rem(fsdp, 4) * 256, 256), 256)
        return (
            (up.at[expert, :, quarter], up_own.at[rows(me_f), cols(me_z, 256)]),
            (down.at[expert, quarter, :], down_own.at[cols(me_z, 256), rows(me_f)]),
            (fsdp, tensor),
        )

    def remote(step):
        ups, downs, (fsdp, tensor) = expert_copies(step)
        return [
            pltpu.make_async_remote_copy(
                src_ref=pair[0], dst_ref=pair[1], send_sem=sems[0].at[step],
                recv_sem=sems[1].at[step], device_id=place(fsdp, tensor), device_id_type=MESH,
            )
            for pair, sems in ((ups, (up_send, up_recv)), (downs, (down_send, down_recv)))
        ]

    def start_step(step, carry):
        for copy in remote(step):
            copy.start()
        return carry

    @pl.when(me_z == 0)
    def _():
        for index in range(4):
            trunk_copy(index, True).start()

    inner = (me_z == 1) | (me_z == 2)

    @pl.when(inner)
    def _():
        halo_copy.start()

    def pass_up(level, indices):
        @pl.when(me_z == level)
        def _():
            for index in indices:
                trunk_copy(index, False).wait_recv()
                if level < 3:
                    trunk_copy(index, False).start()

    for copy in first:
        copy.wait_recv()
    for copy in local:
        copy.wait()

    pair = me_z // 2 * 2

    def pair_views(number):
        return [
            weights.at[:, rows(me_f), cols(number, 512)],
            pieces.at[me_f, pl.ds(number, 2)],
        ]

    second = [
        sender.copy(view, view, me_f, 3 - me_z, inner) for view in pair_views(pair)
    ]

    @pl.when(inner)
    def _():
        for copy in second:
            copy.wait_recv()

    handed = [
        sender.copy(view, view, me_f, flip(me_z, 1), inner) for view in pair_views(2 - pair)
    ]

    @pl.when(~inner)
    def _():
        for copy in handed:
            copy.wait_recv()

    across = flip(me_f, 2) * (1 - core) + flip(me_f, 4) * core
    along = flip(me_f, 4) * (1 - core) + flip(me_f, 2) * core

    def blocks(fsdp_list, target):
        made = []
        for fsdp in fsdp_list:
            view = weights.at[:, rows(fsdp)]
            made.append(sender.copy(view, view, target, me_z))
            made.append(sender.copy(pieces.at[fsdp], pieces.at[fsdp], target, me_z))
        return made

    third = blocks([me_f], across)
    pass_up(1, (0, 1, 2, 3))
    lax.fori_loop(1, 8, start_step, 0)
    pass_up(2, (0, 1))
    for copy in third:
        copy.wait_recv()
    fourth = blocks([me_f, across], along)
    ups, downs, _ = expert_copies(0)
    own = [
        pltpu.make_async_copy(ups[0], ups[1], local_sem.at[4]),
        pltpu.make_async_copy(downs[0], downs[1], local_sem.at[5]),
    ]
    for copy in own:
        copy.start()
    pass_up(2, (2, 3))
    pass_up(3, (0, 1, 2, 3))

    @pl.when(me_z > 1)
    def _():
        halo_copy.wait_recv()

    fill = [
        pltpu.make_async_copy(tokens, rows_all.at[:, trunk_rows], local_sem.at[0]),
        pltpu.make_async_copy(
            tokens.at[:, pl.ds(128, 128)], rows_all.at[:, halo_rows], local_sem.at[1]
        ),
    ]
    for copy, when in zip(fill, (me_z == 0, me_z < 2)):
        pl.when(when)(copy.start)
        pl.when(when)(copy.wait)

    for copy in fourth:
        copy.wait_recv()
    fifth = blocks([core, core + 2, core + 4, core + 6], flip(me_f, 1))
    lax.fori_loop(8, 32, start_step, 0)
    for copy in fifth:
        copy.wait_recv()

    for fsdp in range(8):
        total = pieces[fsdp, 0, 0:16].astype(F32)
        for tensor in range(1, 4):
            total = total + pieces[fsdp, tensor, 0:16].astype(F32)
        table[0:16, fsdp * 128 : fsdp * 128 + 128] = total
    for tensor in range(4):
        total = pieces[0, tensor, 16:32].astype(F32)
        for fsdp in range(1, 8):
            total = total + pieces[fsdp, tensor, 16:32].astype(F32)
        for which in range(2):
            for half in range(2):
                lane = tensor * 256 + half * 128
                table[14 + which : 15 + which, lane : lane + 128] = total[
                    2 * which + half : 2 * which + half + 1, :
                ]
    saves = [
        pltpu.make_async_copy(weights, full4, local_sem.at[6]),
        pltpu.make_async_copy(table, params, local_sem.at[7]),
        pltpu.make_async_copy(rows_all, rows_out, local_sem.at[8]),
    ]
    for copy in saves:
        copy.start()

    def tile(index):
        return pl.ds(pl.multiple_of(index * 256, 256), 256)

    def lanes(index):
        return pl.ds(pl.multiple_of(index * 128, 128), 128)

    def one_tree(micro, carry):
        def norm(index, carry):
            value = rows_all[micro, lanes(index), :].astype(F32)
            centered = value - jnp.mean(value, axis=-1, keepdims=True)
            scale = lax.rsqrt(jnp.mean(centered * centered, axis=-1, keepdims=True) + EPSILON)
            out = centered * scale * table[0:1, :] + table[2:3, :]
            normed[micro, lanes(index), :] = out.astype(BF)
            return carry

        lax.fori_loop(0, 5, norm, 0)

        def project(index, carry):
            place_cols = tile(index)
            key = dot_nn(normed[micro], weights[1, :, place_cols])
            keys[micro, :, place_cols] = key.astype(BF)
            value = dot_nn(normed[micro], weights[2, :, place_cols]) + table[15:16, place_cols]
            values[micro, :, place_cols] = value.astype(BF)
            query = dot_nn(normed[micro, own_rows], weights[0, :, place_cols])
            queries[micro, :, place_cols] = (query + table[14:15, place_cols]).astype(BF)
            return carry

        lax.fori_loop(0, 4, project, 0)

        def two_heads(index, carry):
            query, key, value = (
                part[micro, :, lanes(index)] for part in (queries, keys, values)
            )
            low = lax.broadcasted_iota(jnp.int32, (256, 128), 1) < 64
            outs = []
            for which in range(2):
                one = jnp.where(low if which == 0 else ~low, query, jnp.zeros_like(query))
                scores = dot_nt(one, key) * 0.125 + mask[micro]
                exponent = jnp.exp(scores - jnp.max(scores, axis=-1, keepdims=True))
                total = jnp.sum(exponent, axis=-1, keepdims=True)
                weight = (exponent * (1.0 / total)).astype(BF)
                probs[micro, 2 * index + which] = weight
                outs.append(dot_nn(weight, value))
            heads[micro, :, lanes(index)] = jnp.where(low, outs[0], outs[1]).astype(BF)
            return carry

        lax.fori_loop(0, 8, two_heads, 0)

        def mix(index, carry):
            place_cols = tile(index)
            out = dot_nt(heads[micro], weights[3, place_cols, :])
            residual[micro, :, place_cols] = (
                rows_all[micro, own_rows, place_cols].astype(F32) + out + table[4:5, place_cols]
            )
            return carry

        lax.fori_loop(0, 4, mix, 0)

        value = residual[micro]
        centered = value - jnp.mean(value, axis=-1, keepdims=True)
        scale = lax.rsqrt(jnp.mean(centered * centered, axis=-1, keepdims=True) + EPSILON)
        middle = (centered * scale * table[1:2, :] + table[3:4, :]).astype(BF)
        lane = lax.broadcasted_iota(jnp.int32, (256, 128), 1)
        logits = jnp.where(lane < 8, dot_nt(middle, router[...]), MASKED)
        exponent = jnp.exp(logits - jnp.max(logits, axis=-1, keepdims=True))
        share = exponent / jnp.sum(exponent, axis=-1, keepdims=True)
        gates[micro] = share
        choice = chosen[micro]
        wide = choice.astype(F32)
        gate = jnp.sum(share * wide, axis=-1, keepdims=True)
        earlier = (
            lax.broadcasted_iota(jnp.int32, (256, 256), 1)
            < lax.broadcasted_iota(jnp.int32, (256, 256), 0)
        ).astype(F32).astype(BF)
        rank = dot_nn(earlier, choice) + (lane * cap).astype(F32)
        slot = jnp.sum(wide * rank, axis=-1, keepdims=True)
        column = lax.broadcasted_iota(jnp.int32, (256, 8 * cap), 1).astype(F32)
        hit = (column == slot).astype(F32).astype(BF)
        pick[micro] = hit
        slots[0, micro] = dot_tn(hit, middle).astype(BF)
        returned = (gate * grads[micro].astype(F32)).astype(BF)
        slots[1, micro] = dot_tn(hit, returned).astype(BF)
        return carry

    router[...] = jnp.zeros_like(router)
    router[0:16, :] = jnp.concatenate(
        [table[6:14, :], jnp.zeros((8, 1024), F32)], axis=0
    ).astype(BF)
    lax.fori_loop(0, 2, one_tree, 0)
    late = [
        (normed, normed_out), (queries, q_out), (keys, k_out), (values, v_out),
        (heads, heads_out), (residual, residual_out), (probs, probs_out), (slots, slots_out),
        (pick, pick_out), (gates, gates_out),
    ]
    for index, (source, target) in enumerate(late):
        copy = pltpu.make_async_copy(source, target, local_sem.at[(9 + index) if index < 7 else (11 + index)])
        copy.start()
        saves.append(copy)

    @pl.when((me_z > 0) & (me_z < 3))
    def _():
        for index in range(4):
            trunk_copy(index, False).wait_send()

    @pl.when(me_z == 0)
    def _():
        for index in range(4):
            trunk_copy(index, True).wait_send()

    @pl.when(inner)
    def _():
        halo_copy.wait_send()

    for copy in own:
        copy.wait()

    def end_step(step, carry):
        for copy in remote(step):
            copy.wait_send()
            copy.wait_recv()
        return carry

    lax.fori_loop(1, 32, end_step, 0)
    sender.finish()
    for copy in saves:
        copy.wait()


def any_spec(count):
    return [pl.BlockSpec(memory_space=pl.ANY)] * count


def attend_all(w4, small, tokens, up, down, bias, chosen, cotangent, cap):
    kept = [
        ((4, 1024, 1024), BF), ((16, 1024), F32), ((2, 640, 1024), BF), ((2, 640, 1024), BF),
        ((2, 256, 1024), BF), ((2, 640, 1024), BF), ((2, 640, 1024), BF), ((2, 256, 1024), BF),
        ((2, 256, 1024), F32), ((2, 16, 256, 640), BF), ((2, 2, 8 * cap, 1024), BF),
        ((2, 256, 8 * cap), BF), ((2, 256, 128), F32),
    ]
    dma = pltpu.SemaphoreType.DMA
    return pl.pallas_call(
        attend_kernel,
        out_shape=[
            *(jax.ShapeDtypeStruct(shape, dtype) for shape, dtype in kept),
            jax.ShapeDtypeStruct((1024, 1024), BF),
            jax.ShapeDtypeStruct((1024, 1024), BF),
        ],
        in_specs=any_spec(8),
        out_specs=any_spec(15),
        scratch_shapes=[
            pltpu.VMEM(*kept[0]),
            pltpu.VMEM((8, 4, 32, 128), BF),
            *(pltpu.VMEM(shape, dtype) for shape, dtype in kept[1:]),
            pltpu.VMEM((2, 256, 640), F32),
            pltpu.VMEM((2, 256, 128), BF),
            pltpu.VMEM((2, 256, 1024), BF),
            pltpu.VMEM((128, 1024), BF),
            dma((20,)), dma((20,)), dma((21,)),
            dma((32,)), dma((32,)), dma((32,)), dma((32,)), dma((5,)), dma((5,)),
        ],
        compiler_params=pltpu.CompilerParams(
            collective_id=0, has_side_effects=True, vmem_limit_bytes=60 << 20
        ),
        name="attend",
    )(w4, small, tokens, up, down, bias, chosen, cotangent)


def gelu_pair(hidden):
    scale = (2.0 / jnp.pi) ** 0.5
    square = hidden * hidden
    bend = jnp.tanh(scale * hidden * (1.0 + 0.044715 * square))
    half = 0.5 * (1.0 + bend)
    slope = half + 0.5 * hidden * (1.0 - bend * bend) * scale * (1.0 + 0.134145 * square)
    return hidden * half, slope


def dot_nn(left, right):
    return lax.dot_general(left, right, (((1,), (0,)), ((), ())), preferred_element_type=F32)


def dot_nt(left, right):
    return lax.dot_general(left, right, (((1,), (1,)), ((), ())), preferred_element_type=F32)


def dot_tn(left, right):
    return lax.dot_general(left, right, (((0,), (0,)), ((), ())), preferred_element_type=F32)


def expert_kernel(
    slots, up_hbm, down_hbm, returned, up_grad, down_grad,
    arrived, parts, got, got_x, up, down, up_sum, down_sum, act, slope,
    send_sem, recv_sem, local_sem,
):
    cap = slots.shape[3]
    group = 8 * cap
    rows = 2 * group
    me_f, me_z = lax.axis_index("fsdp"), lax.axis_index("tensor")
    me_y, me_x, core = me_f // 4, lax.rem(me_f // 2, 2), lax.rem(me_f, 2)
    far_x = 1 - me_x
    x_mate, core_mate = flip(me_f, 2), flip(me_f, 1)
    far = []
    for step in range(1, 8):
        far.append(
            (lax.rem(me_y + step // 4, 2) * 4 + lax.rem(me_f, 4), lax.rem(me_z + step, 4))
        )
    greet([(x_mate, me_z), (core_mate, me_z)] + far)
    sender = Sender(send_sem, recv_sem)
    load = [
        pltpu.make_async_copy(up_hbm, up, local_sem.at[0]),
        pltpu.make_async_copy(down_hbm, down, local_sem.at[1]),
    ]

    def origin_rows(fsdp, tensor):
        first = (fsdp // 4 * 4 + tensor) * cap
        return pl.ds(pl.multiple_of(first, cap), cap)

    chunks = [(kind, micro) for kind in range(2) for micro in range(2)]
    half_rows = 4 * cap
    incoming, own_in = {}, {}

    def half_of(half):
        first = (me_y + half - 2 * me_y * half) * half_rows
        return pl.ds(pl.multiple_of(first, half_rows), half_rows)

    def send_half(number):
        index, half = number // 2, number % 2
        kind, micro = chunks[index]
        target = arrived.at[kind, micro, me_x, core, origin_rows(me_f, me_z)]
        incoming[number] = [
            sender.copy(slots.at[kind, micro, 2 * tensor + fsdp // 4], target, fsdp, tensor)
            for fsdp, tensor in (far[:3] if half == 0 else far[3:])
        ]
        if half == 0:
            own = pltpu.make_async_copy(
                slots.at[kind, micro, 2 * me_z + me_y], target, local_sem.at[2 + index]
            )
            own.start()
            own_in[index] = own

    send_half(0)
    send_half(1)
    for copy in load:
        copy.start()

    def same_place(view, fsdp):
        return sender.copy(view, view, fsdp, me_z)

    across, beside, onward = {}, {}, {}

    def landed(index):
        kind, micro = chunks[index]
        across[index], beside[index] = [], []
        for half in range(2):
            for copy in incoming[2 * index + half]:
                copy.wait_recv()
            if half == 0:
                own_in[index].wait()
            if 2 * index + half + 2 < 8:
                send_half(2 * index + half + 2)
            view = arrived.at[kind, micro, me_x, core, half_of(half)]
            across[index].append(same_place(view, x_mate))
            beside[index].append(same_place(view, core_mate))

    def forwarded(index):
        kind, micro = chunks[index]
        onward[index] = []
        for half in range(2):
            across[index][half].wait_recv()
            onward[index].append(
                same_place(arrived.at[kind, micro, far_x, core, half_of(half)], core_mate)
            )

    def ready(copies):
        for copy in copies:
            copy.wait_recv()

    def tile(index):
        return pl.ds(pl.multiple_of(index * 256, 256), 256)

    def forward(micro, side):
        data = arrived.at[0, micro, side]

        def first(index, carry):
            hidden = dot_nn(data[...].reshape(rows, 1024), up[:, tile(index)])
            value, slope_value = gelu_pair(hidden)
            act[micro, side, :, tile(index)] = value.astype(BF)
            slope[micro, side, :, tile(index)] = slope_value.astype(BF)
            return carry

        lax.fori_loop(0, 4, first, 0)

        def second(index, carry):
            out = dot_nn(act[micro, side], down[:, tile(index)])
            parts[0, micro, side, :, :, tile(index)] = out.astype(BF).reshape(2, group, 256)
            return carry

        lax.fori_loop(0, 4, second, 0)

    def backward(micro, side, begin):
        data = arrived.at[0, micro, side]
        grads = arrived.at[1, micro, side]

        def first(index, carry):
            grad = grads[...].reshape(rows, 1024)
            grad_act = dot_nt(grad, down[tile(index), :])
            grad_hidden = (
                grad_act * slope[micro, side, :, tile(index)].astype(F32)
            ).astype(BF)
            slope[micro, side, :, tile(index)] = grad_hidden
            down_part = dot_tn(act[micro, side, :, tile(index)], grad)
            up_part = dot_tn(data[...].reshape(rows, 1024), grad_hidden)
            if begin:
                down_sum[tile(index), :] = down_part
                up_sum[:, tile(index)] = up_part
            else:
                down_sum[tile(index), :] += down_part
                up_sum[:, tile(index)] += up_part
            return carry

        lax.fori_loop(0, 4, first, 0)

        def second(index, carry):
            out = dot_nt(slope[micro, side], up[tile(index), :])
            parts[1, micro, side, :, :, tile(index)] = out.astype(BF).reshape(2, group, 256)
            return carry

        lax.fori_loop(0, 4, second, 0)

    def result(kind, micro):
        return parts.at[kind, micro]

    core_back, x_back, home = {}, {}, {}

    def back_core(index):
        kind, micro = chunks[index]
        core_back[index] = sender.copy(
            result(kind, micro).at[:, 1 - core], got.at[kind, micro], core_mate, me_z
        )

    def add_rows(target, source, count=8):
        def step(row, carry):
            part = pl.ds(pl.multiple_of(row * cap, cap), cap)
            target[part] = (target[part].astype(F32) + source[part].astype(F32)).astype(BF)
            return carry

        lax.fori_loop(0, count, step, 0)

    def back_x(index):
        kind, micro = chunks[index]
        core_back[index].wait_recv()
        mine = result(kind, micro)
        add_rows(mine.at[far_x, core], got.at[kind, micro, far_x])
        x_back[index] = [
            sender.copy(
                mine.at[far_x, core, half_of(half)], got_x.at[kind, micro, half_of(half)],
                x_mate, me_z,
            )
            for half in range(2)
        ]
        add_rows(mine.at[me_x, core], got.at[kind, micro, me_x])

    def back_home(index):
        kind, micro = chunks[index]
        mine = result(kind, micro).at[me_x, core]
        target = returned.at[kind, micro, 2 * me_z + me_y]
        home[index] = []
        for half in range(2):
            x_back[index][half].wait_recv()
            part = half_of(half)
            add_rows(mine.at[part], got_x.at[kind, micro, part], 4)
            for fsdp, tensor in far[:3] if half == 0 else far[3:]:
                home[index].append(
                    sender.copy(mine.at[origin_rows(fsdp, tensor)], target, fsdp, tensor)
                )
            if half == 0:
                own = pltpu.make_async_copy(
                    mine.at[origin_rows(me_f, me_z)], target, local_sem.at[2 + index]
                )
                own.start()
                own_in[index] = own

    landed(0)
    for copy in load:
        copy.wait()
    ready(beside[0])
    forward(0, me_x)
    landed(1)
    forwarded(0)
    ready(beside[1])
    forward(1, me_x)
    ready(onward[0])
    forward(0, far_x)
    back_core(0)
    landed(2)
    forwarded(1)
    ready(beside[2])
    backward(0, me_x, True)
    ready(onward[1])
    landed(3)
    forward(1, far_x)
    back_core(1)
    back_x(0)
    ready(beside[3])
    backward(1, me_x, False)
    forwarded(2)
    back_x(1)
    ready(onward[2])
    backward(0, far_x, False)
    back_core(2)
    back_home(0)
    forwarded(3)
    back_x(2)
    ready(onward[3])
    backward(1, far_x, False)
    back_core(3)
    back_home(1)
    back_x(3)

    def narrow(index, carry):
        part = pl.ds(pl.multiple_of(index * 64, 64), 64)
        up[part, :] = up_sum[part, :].astype(BF)
        down[part, :] = down_sum[part, :].astype(BF)
        return carry

    lax.fori_loop(0, 16, narrow, 0)
    store = [
        pltpu.make_async_copy(up, up_grad, local_sem.at[0]),
        pltpu.make_async_copy(down, down_grad, local_sem.at[1]),
    ]
    for copy in store:
        copy.start()
    back_home(2)
    back_home(3)
    for index in range(4):
        for copy in home[index]:
            copy.wait_recv()
        own_in[index].wait()
    for copy in store:
        copy.wait()
    sender.finish()


def run_experts(slots, up_own, down_own):
    cap = slots.shape[3]
    group = 8 * cap
    dma = pltpu.SemaphoreType.DMA
    return pl.pallas_call(
        expert_kernel,
        out_shape=[
            jax.ShapeDtypeStruct(slots.shape, BF),
            jax.ShapeDtypeStruct((1024, 1024), BF),
            jax.ShapeDtypeStruct((1024, 1024), BF),
        ],
        in_specs=any_spec(3),
        out_specs=any_spec(3),
        scratch_shapes=[
            pltpu.VMEM((2, 2, 2, 2, group, 1024), BF),
            pltpu.VMEM((2, 2, 2, 2, group, 1024), BF),
            pltpu.VMEM((2, 2, 2, group, 1024), BF),
            pltpu.VMEM((2, 2, group, 1024), BF),
            pltpu.VMEM((1024, 1024), BF),
            pltpu.VMEM((1024, 1024), BF),
            pltpu.VMEM((1024, 1024), F32),
            pltpu.VMEM((1024, 1024), F32),
            pltpu.VMEM((2, 2, 2 * group, 1024), BF),
            pltpu.VMEM((2, 2, 2 * group, 1024), BF),
            dma((92,)), dma((92,)), dma((6,)),
        ],
        compiler_params=pltpu.CompilerParams(
            collective_id=1, has_side_effects=True, vmem_limit_bytes=63 << 20
        ),
        cost_estimate=pl.CostEstimate(
            flops=12 * 4 * group * 2 * 1024 * 1024, bytes_accessed=20 << 20, transcendentals=0
        ),
        name="experts",
    )(slots, up_own, down_own)


def backward_kernel(
    up_grad, down_grad, back_hbm, pick_hbm, residual_hbm, cotangent, share_hbm, chosen_hbm,
    heads_hbm, q_hbm, k_hbm, v_hbm, normed_hbm, probs_hbm, full4, params,
    up_out, down_out, out4, small_out, own_out, trunk_out, halo_out, output, mixed_out,
    weights, sums, proj, heads, grad_heads, queries, keys, values, normed, probs,
    grad_q, grad_k, grad_v, own_rows, trunk_rows, halo_rows, trunk_got,
    got, cut, cut_x, cut_z, cut_w, table, known, small_mine, small_got,
    back, pick, shares, chosen, router,
    send_sem, recv_sem, local_sem, up_send, up_recv, down_send, down_recv,
    small_send, small_recv, trunk_send, trunk_recv, out_sem,
):
    me_f, me_z = lax.axis_index("fsdp"), lax.axis_index("tensor")
    mine = me_f * 4 + me_z
    core = lax.rem(me_f, 2)
    me_y = me_f // 4
    greet_all(mine)
    sender = Sender(send_sem, recv_sem)

    def rows(fsdp):
        return pl.ds(pl.multiple_of(fsdp * 128, 128), 128)

    def cols(first, width):
        return pl.ds(pl.multiple_of(first * 256, 256), width)

    def tile(index):
        return pl.ds(pl.multiple_of(index * 256, 256), 256)

    def lanes(index):
        return pl.ds(pl.multiple_of(index * 128, 128), 128)

    loads = [
        pltpu.make_async_copy(source, target, local_sem.at[index])
        for index, (source, target) in enumerate([
            (back_hbm, back), (pick_hbm, pick), (residual_hbm, own_rows), (cotangent, grad_q),
            (share_hbm, shares), (chosen_hbm, chosen), (params, known), (heads_hbm, heads),
            (full4, weights), (v_hbm, values), (probs_hbm.at[0], probs), (k_hbm, keys),
            (q_hbm, queries), (normed_hbm, normed),
        ])
    ]
    for copy in loads:
        copy.start()

    def expert_copies(step):
        other = lax.rem(mine + step, 32)
        fsdp, tensor = other // 4, lax.rem(other, 4)
        expert = 2 * me_z + me_y
        quarter = pl.ds(pl.multiple_of(lax.rem(me_f, 4) * 256, 256), 256)
        return (
            (up_grad.at[rows(fsdp), cols(tensor, 256)], up_out.at[expert, :, quarter]),
            (down_grad.at[cols(tensor, 256), rows(fsdp)], down_out.at[expert, quarter, :]),
            (fsdp, tensor),
        )

    def remote(step):
        ups, downs, (fsdp, tensor) = expert_copies(step)
        return [
            pltpu.make_async_remote_copy(
                src_ref=pair[0], dst_ref=pair[1], send_sem=sems[0].at[step],
                recv_sem=sems[1].at[step], device_id=place(fsdp, tensor), device_id_type=MESH,
            )
            for pair, sems in ((ups, (up_send, up_recv)), (downs, (down_send, down_recv)))
        ]

    def start_step(step, carry):
        for copy in remote(step):
            copy.start()
        return carry

    lax.fori_loop(1, 32, start_step, 0)
    ups, downs, _ = expert_copies(0)
    own = [
        pltpu.make_async_copy(ups[0], ups[1], out_sem.at[0]),
        pltpu.make_async_copy(downs[0], downs[1], out_sem.at[1]),
    ]
    for copy in own:
        copy.start()

    along = flip(me_f, 4) * (1 - core) + flip(me_f, 2) * core
    across = flip(me_f, 2) * (1 - core) + flip(me_f, 4) * core
    corner = flip(across, 4) * (1 - core) + flip(across, 2) * core
    sent, kept = [along, corner], [me_f, across]
    pair = me_z // 2 * 2
    flight = {}

    def add(target, source, part=None):
        def step(index, carry):
            place_rows = pl.ds(pl.multiple_of(index * 16, 16), 16)
            where = (place_rows,) if part is None else (place_rows, part)
            target[where] = (
                target[where].astype(F32) + source[place_rows, :].astype(F32)
            ).astype(BF)
            return carry

        lax.fori_loop(0, 8, step, 0)

    def by_core(which):
        flight[which] = [
            sender.copy(sums.at[which, :, 1 - core], got.at[which], flip(me_f, 1), me_z)
        ]

    def landed(which):
        for copy in flight[which]:
            copy.wait_recv()

    def by_first(which):
        landed(which)

        def step(block, carry):
            add(sums.at[which, block, core], got.at[which, block])
            return carry

        lax.fori_loop(0, 4, step, 0)
        flight[which] = [
            sender.copy(
                sums.at[which, sent[index] // 2, core], cut.at[which, index], along, me_z
            )
            for index in range(2)
        ]

    def by_second(which):
        landed(which)
        for index in range(2):
            add(sums.at[which, kept[index] // 2, core], cut.at[which, index])
        flight[which] = [
            sender.copy(sums.at[which, across // 2, core], cut_x.at[which], across, me_z)
        ]

    def by_pair(which):
        landed(which)
        block = sums.at[which, me_f // 2, core]
        add(block, cut_x.at[which])
        flight[which] = [
            sender.copy(block.at[:, cols(2 - pair, 512)], cut_z.at[which], me_f, flip(me_z, 2))
        ]

    def by_last(which):
        landed(which)
        block = sums.at[which, me_f // 2, core]
        add(block, cut_z.at[which], cols(pair, 512))
        flight[which] = [
            sender.copy(
                block.at[:, cols(flip(me_z, 1), 256)], cut_w.at[which], me_f, flip(me_z, 1)
            )
        ]

    def by_end(which):
        landed(which)
        block = sums.at[which, me_f // 2, core]
        add(block, cut_w.at[which], cols(me_z, 256))
        copy = pltpu.make_async_copy(
            block.at[:, cols(me_z, 256)], out4.at[which], out_sem.at[2 + which]
        )
        copy.start()
        own.append(copy)

    def loaded(*indices):
        for index in indices:
            loads[index].wait()

    loaded(0, 1, 2, 3, 4, 5, 6)
    table[...] = jnp.zeros_like(table)
    router[...] = jnp.zeros_like(router)
    router[0:16, :] = jnp.concatenate(
        [known[6:14, :], jnp.zeros((8, 1024), F32)], axis=0
    ).astype(BF)

    def three(value):
        high = value.astype(BF)
        rest = value - high.astype(F32)
        middle = rest.astype(BF)
        return high, middle, (rest - middle.astype(F32)).astype(BF)

    def finish_rows(index, carry):
        micro, part = index // 2, pl.ds(pl.multiple_of(lax.rem(index, 2) * 128, 128), 128)
        hit = pick[micro, part, :]
        returned = dot_nn(hit, back[0, micro])
        grad_mid = dot_nn(hit, back[1, micro])
        value = own_rows[micro, part, :]
        final = grad_q[micro, part, :].astype(F32)
        share, choice = shares[micro, part, :], chosen[micro, part, :].astype(F32)
        gate = jnp.sum(share * choice, axis=-1, keepdims=True)
        grad_heads[micro, part, :] = (value + gate * returned + known[5:6, :]).astype(BF)
        grad_gate = jnp.sum(final * returned, axis=-1, keepdims=True)
        grad_logits = three(share * (choice * grad_gate - gate * grad_gate))
        centered = value - jnp.mean(value, axis=-1, keepdims=True)
        scale = lax.rsqrt(jnp.mean(centered * centered, axis=-1, keepdims=True) + EPSILON)
        plain = centered * scale
        middle = (plain * known[1:2, :] + known[3:4, :]).astype(BF)
        for piece in grad_logits:
            table[6:14, :] += dot_tn(piece, middle)[0:8, :]
            grad_mid = grad_mid + dot_nn(piece, router[...])
        table[1:2, :] += jnp.sum(grad_mid * plain, axis=0, keepdims=True)
        table[3:4, :] += jnp.sum(grad_mid, axis=0, keepdims=True)
        scaled = grad_mid * known[1:2, :]
        inside = (
            scaled
            - jnp.mean(scaled, axis=-1, keepdims=True)
            - plain * jnp.mean(scaled * plain, axis=-1, keepdims=True)
        )
        mixed = final + scale * inside
        own_rows[micro, part, :] = mixed
        proj[micro, part, :] = mixed.astype(BF)
        table[4:5, :] += jnp.sum(mixed, axis=0, keepdims=True)
        table[5:6, :] += jnp.sum(final, axis=0, keepdims=True)
        return carry

    lax.fori_loop(0, 4, finish_rows, 0)
    shown = [
        pltpu.make_async_copy(grad_heads, output, out_sem.at[8]),
        pltpu.make_async_copy(own_rows, mixed_out, out_sem.at[9]),
    ]
    for copy in shown:
        copy.start()
    loaded(7)

    def out_sum(index, carry):
        left = proj[:, :, tile(index)].reshape(512, 256)
        part = dot_tn(left, heads[...].reshape(512, 1024))
        sums[3, index] = part.astype(BF).reshape(2, 128, 1024)
        return carry

    lax.fori_loop(0, 4, out_sum, 0)
    by_core(3)
    loaded(8)
    shown[0].wait()

    def head_grads(index, carry):
        part = dot_nn(proj[...].reshape(512, 1024), weights[3, :, tile(index)])
        grad_heads[:, :, tile(index)] = part.astype(BF).reshape(2, 256, 256)
        return carry

    lax.fori_loop(0, 4, head_grads, 0)
    by_first(3)
    loaded(9, 10, 11, 12)

    def one_tree(micro):
        def two_heads(index, carry):
            query, key, value, grad = (
                part[micro, :, lanes(index)] for part in (queries, keys, values, grad_heads)
            )
            low = lax.broadcasted_iota(jnp.int32, (256, 128), 1) < 64
            low_keys = lax.broadcasted_iota(jnp.int32, (640, 128), 1) < 64
            outs = []
            for which in range(2):
                one = jnp.where(low if which == 0 else ~low, grad, jnp.zeros_like(grad))
                grad_probs = dot_nt(one, value)
                weight = probs[2 * index + which]
                wide = weight.astype(F32)
                scaled = wide * grad_probs
                total = jnp.sum(scaled, axis=-1, keepdims=True)
                grad_scores = (scaled - wide * total).astype(BF)
                outs.append((
                    dot_nn(grad_scores, key), dot_tn(grad_scores, query), dot_tn(weight, grad)
                ))
            grad_q[micro, :, lanes(index)] = (
                jnp.where(low, outs[0][0], outs[1][0]) * 0.125
            ).astype(BF)
            grad_k[micro, :, lanes(index)] = (
                jnp.where(low_keys, outs[0][1], outs[1][1]) * 0.125
            ).astype(BF)
            grad_v[micro, :, lanes(index)] = jnp.where(
                low_keys, outs[0][2], outs[1][2]
            ).astype(BF)
            return carry

        lax.fori_loop(0, 8, two_heads, 0)

    one_tree(0)
    next_probs = pltpu.make_async_copy(probs_hbm.at[1], probs, local_sem.at[10])
    next_probs.start()
    by_second(3)
    next_probs.wait()
    one_tree(1)
    by_pair(3)
    loaded(13)

    def note(index, grads, plain):
        place_cols = tile(index)
        table[2:3, place_cols] += jnp.sum(grads, axis=0, keepdims=True)
        table[0:1, place_cols] += jnp.sum(grads * plain.astype(F32), axis=0, keepdims=True)

    def far_rows(index, carry):
        place_cols = tile(index)
        keys_part = grad_k[:, 0:384, :].reshape(768, 1024)
        values_part = grad_v[:, 0:384, :].reshape(768, 1024)
        grads = dot_nt(keys_part, weights[1, place_cols, :]) + dot_nt(
            values_part, weights[2, place_cols, :]
        )
        note(index, grads, normed[:, 0:384, place_cols].reshape(768, 256))
        grads = grads.astype(BF).reshape(2, 384, 256)
        for micro in range(2):
            trunk_rows[2 * micro, :, place_cols] = grads[micro, 0:128]
            trunk_rows[2 * micro + 1, :, place_cols] = grads[micro, 128:256]
            halo_rows[micro, :, place_cols] = grads[micro, 256:384]
        return carry

    lax.fori_loop(0, 4, far_rows, 0)

    def trunk_copy(index):
        return pltpu.make_async_remote_copy(
            src_ref=trunk_rows.at[index],
            dst_ref=trunk_got.at[index],
            send_sem=trunk_send.at[index],
            recv_sem=trunk_recv.at[index],
            device_id=place(me_f, lax.rem(me_z + 3, 4)),
            device_id_type=MESH,
        )

    halo_copy = pltpu.make_async_remote_copy(
        src_ref=halo_rows,
        dst_ref=halo_out,
        send_sem=trunk_send.at[4],
        recv_sem=trunk_recv.at[4],
        device_id=place(me_f, lax.rem(me_z + 3, 4)),
        device_id_type=MESH,
    )

    @pl.when(me_z == 3)
    def _():
        for index in range(4):
            trunk_copy(index).start()

    def pass_down(level):
        @pl.when(me_z == level)
        def _():
            for index in range(4):
                trunk_copy(index).wait_recv()
                add(trunk_rows.at[index], trunk_got.at[index])
                if level:
                    trunk_copy(index).start()

    def weight_sum(which, grads, begin):
        count = 2 * (640 - begin)

        def step(index, carry):
            left = normed[:, begin:640, tile(index)].reshape(count, 256)
            part = dot_tn(left, grads[...].reshape(count, 1024))
            sums[which, index] = part.astype(BF).reshape(2, 128, 1024)
            return carry

        lax.fori_loop(0, 4, step, 0)
        by_core(which)

    weight_sum(2, grad_v, 0)
    by_last(3)
    pass_down(2)
    weight_sum(1, grad_k, 0)
    by_first(2)
    pass_down(1)
    weight_sum(0, grad_q, 384)
    by_first(1)
    by_second(2)

    @pl.when(me_z > 1)
    def _():
        halo_copy.start()

    def near_rows(index, carry):
        place_cols = tile(index)
        keys_part = grad_k[:, 384:640, :].reshape(512, 1024)
        values_part = grad_v[:, 384:640, :].reshape(512, 1024)
        grads = (
            dot_nt(keys_part, weights[1, place_cols, :])
            + dot_nt(values_part, weights[2, place_cols, :])
            + dot_nt(grad_q[...].reshape(512, 1024), weights[0, place_cols, :])
        )
        note(index, grads, normed[:, 384:640, place_cols].reshape(512, 256))
        own_rows[:, :, place_cols] = grads.reshape(2, 256, 256)
        return carry

    shown[1].wait()
    lax.fori_loop(0, 4, near_rows, 0)
    by_first(0)
    by_second(1)
    by_pair(2)
    copy = pltpu.make_async_copy(own_rows, own_out, out_sem.at[6])
    copy.start()
    own.append(copy)

    gain, offset = known[0:1, :], known[2:3, :]
    table[0:1, :] = (table[0:1, :] - offset * table[2:3, :]) / gain
    table[14:15, :] = jnp.sum(grad_q[...].reshape(512, 1024).astype(F32), axis=0, keepdims=True)
    table[15:16, :] = jnp.sum(grad_v[...].reshape(1280, 1024).astype(F32), axis=0, keepdims=True)
    for fsdp in range(8):
        for tensor in range(4):
            target = 4 * fsdp + tensor
            small_mine[target, 0:16, :] = table[:, fsdp * 128 : fsdp * 128 + 128]
            for which in range(2):
                for half in range(2):
                    lane = tensor * 256 + half * 128
                    row = 16 + 2 * which + half
                    small_mine[target, row : row + 1, :] = table[
                        14 + which : 15 + which, lane : lane + 128
                    ]

    def small_copy(step):
        other = lax.rem(mine + step, 32)
        return pltpu.make_async_remote_copy(
            src_ref=small_mine.at[other], dst_ref=small_got.at[mine], send_sem=small_send.at[step],
            recv_sem=small_recv.at[step], device_id=place(other // 4, lax.rem(other, 4)),
            device_id_type=MESH,
        )

    def start_small(step, carry):
        small_copy(step).start()
        return carry

    lax.fori_loop(1, 32, start_small, 0)
    small_got[mine] = small_mine[mine]
    by_second(0)
    by_pair(1)
    by_last(2)
    pass_down(0)
    by_pair(0)
    by_last(1)
    by_end(3)
    by_end(2)
    by_last(0)
    by_end(1)
    by_end(0)
    trunk_done = pltpu.make_async_copy(trunk_rows, trunk_out, out_sem.at[7])
    trunk_done.start()
    own.append(trunk_done)

    @pl.when(me_z > 0)
    def _():
        for index in range(4):
            trunk_copy(index).wait_send()

    @pl.when(me_z > 1)
    def _():
        halo_copy.wait_send()

    @pl.when((me_z > 0) & (me_z < 3))
    def _():
        halo_copy.wait_recv()

    def end_small(step, carry):
        copy = small_copy(step)
        copy.wait_send()
        copy.wait_recv()
        return carry

    lax.fori_loop(1, 32, end_small, 0)

    def sum_small(index, total):
        return total + small_got[index]

    small_out[...] = lax.fori_loop(1, 32, sum_small, small_got[0])

    def end_step(step, carry):
        for copy in remote(step):
            copy.wait_send()
            copy.wait_recv()
        return carry

    lax.fori_loop(1, 32, end_step, 0)
    sender.finish()
    for copy in own:
        copy.wait()


def attend_back(*operands):
    dma = pltpu.SemaphoreType.DMA
    specs = any_spec(9)
    specs[3] = pl.BlockSpec(memory_space=pltpu.VMEM)
    tree, keyed = (2, 256, 1024), (2, 640, 1024)
    return pl.pallas_call(
        backward_kernel,
        out_shape=[
            jax.ShapeDtypeStruct((8, 128, 1024), BF),
            jax.ShapeDtypeStruct((8, 1024, 128), BF),
            jax.ShapeDtypeStruct((4, 128, 256), BF),
            jax.ShapeDtypeStruct((24, 128), F32),
            jax.ShapeDtypeStruct(tree, F32),
            jax.ShapeDtypeStruct((4, 128, 1024), BF),
            jax.ShapeDtypeStruct((2, 128, 1024), BF),
            jax.ShapeDtypeStruct(tree, BF),
            jax.ShapeDtypeStruct(tree, F32),
        ],
        in_specs=any_spec(16),
        out_specs=specs,
        scratch_shapes=[
            pltpu.VMEM((4, 1024, 1024), BF),
            pltpu.VMEM((4, 4, 2, 128, 1024), BF),
            pltpu.VMEM(tree, BF),
            pltpu.VMEM(tree, BF),
            pltpu.VMEM(tree, BF),
            pltpu.VMEM(tree, BF),
            pltpu.VMEM(keyed, BF),
            pltpu.VMEM(keyed, BF),
            pltpu.VMEM(keyed, BF),
            pltpu.VMEM((16, 256, 640), BF),
            pltpu.VMEM(tree, BF),
            pltpu.VMEM(keyed, BF),
            pltpu.VMEM(keyed, BF),
            pltpu.VMEM(tree, F32),
            pltpu.VMEM((4, 128, 1024), BF),
            pltpu.VMEM((2, 128, 1024), BF),
            pltpu.VMEM((4, 128, 1024), BF),
            pltpu.VMEM((4, 4, 128, 1024), BF),
            pltpu.VMEM((4, 2, 128, 1024), BF),
            pltpu.VMEM((4, 128, 1024), BF),
            pltpu.VMEM((4, 128, 512), BF),
            pltpu.VMEM((4, 128, 256), BF),
            pltpu.VMEM((16, 1024), F32),
            pltpu.VMEM((16, 1024), F32),
            pltpu.VMEM((32, 24, 128), F32),
            pltpu.VMEM((32, 24, 128), F32),
            pltpu.VMEM(operands[2].shape, BF),
            pltpu.VMEM(operands[3].shape, BF),
            pltpu.VMEM((2, 256, 128), F32),
            pltpu.VMEM((2, 256, 128), BF),
            pltpu.VMEM((128, 1024), BF),
            dma((24,)), dma((24,)), dma((14,)),
            dma((32,)), dma((32,)), dma((32,)), dma((32,)),
            dma((32,)), dma((32,)), dma((5,)), dma((5,)), dma((10,)),
        ],
        compiler_params=pltpu.CompilerParams(
            collective_id=3, has_side_effects=True, vmem_limit_bytes=63 << 20
        ),
        name="attend_back",
    )(*operands)


def fast_body(
    tokens, segment, route, w_qkv, bias_qv, w_o, w_router, w_up, w_down, norm_gains, shifts, cotangent
):
    micro_count, local_rows, width = tokens.shape
    expert_count = w_up.shape[0]
    cap = 3 * local_rows // (2 * expert_count)
    me_z = lax.axis_index("tensor")
    start = me_z * local_rows
    me_f = lax.axis_index("fsdp")
    lane = jnp.arange(128)
    mine = jnp.concatenate(
        [norm_gains, shifts, w_router.T, jnp.zeros((2, 32), BF)], axis=0
    )
    mine = jnp.where(lane // 32 == me_z, jnp.tile(mine, (1, 4)), 0)
    bias_lane = jnp.arange(64)
    bias_mine = jnp.where(bias_lane // 8 == me_f, jnp.tile(bias_qv, (1, 1, 8)), 0).reshape(4, 128)
    small = jnp.concatenate([mine, bias_mine, jnp.zeros((12, 128), BF)], axis=0)
    w4 = jnp.concatenate([w_qkv, w_o.T[None]], axis=0)
    own_index = start + jnp.arange(local_rows)
    key_index = jnp.concatenate([jnp.arange(256), start - 128 + jnp.arange(128), own_index])
    key_part = jnp.arange(640) < 256
    own_segs = lax.dynamic_slice_in_dim(segment, start, local_rows, axis=1)
    halo_segs = lax.dynamic_slice_in_dim(segment, jnp.maximum(start - 128, 0), 128, axis=1)
    key_segs = jnp.concatenate([segment[:, :256], halo_segs, own_segs], axis=1)
    query_seg, key_seg = own_segs[:, :, None], key_segs[:, None, :]
    allowed = (
        (key_seg == 0)
        | (key_seg == query_seg)
        | (query_seg >= 5) & (key_seg == (query_seg - 5) // 2 + 1)
    )
    allowed = allowed & (key_part | (key_index >= 256))[None, None, :]
    allowed = allowed & (key_index[None, :] <= own_index[:, None])[None]
    bias = jnp.where(allowed, 0.0, MASKED)
    own_routes = lax.dynamic_slice_in_dim(route[:, :, 0], start, local_rows, axis=1)
    chosen = (own_routes[:, :, None] == lane).astype(BF)
    (
        full4, params, rows_all, normed_all, queries, keys, values, heads_low, residual, probs_low,
        slots, pick, router_probs, up_own, down_own,
    ) = attend_all(w4, small, tokens, w_up, w_down, bias, chosen, cotangent, cap)
    slots = slots.reshape(2, micro_count, expert_count, cap, width)
    back, up_grad, down_grad = run_experts(slots, up_own, down_own)
    back = back.reshape(2, micro_count, expert_count * cap, width)
    (
        up_out, down_out, out4, small_out, grad_own, trunk_sum, halo_sum, output, grad_mixed,
    ) = attend_back(
        up_grad, down_grad, back, pick, residual, cotangent, router_probs, chosen,
        heads_low, queries, keys, values, normed_all, probs_low, full4, params,
    )
    gain = params[0]
    _, plain_in, scale_in = norm_rows(tokens.astype(F32), gain, params[2])

    def flat(value):
        return value.reshape(-1, value.shape[-1])

    trunk_sum = trunk_sum.reshape(2, 256, width).astype(F32)
    grad_normed = grad_own + jnp.where(me_z == 0, trunk_sum, 0.0)
    grad_normed = grad_normed.at[:, 128:].add(jnp.where((me_z > 0) & (me_z < 3), halo_sum.astype(F32), 0.0))
    grad_from_in, _, _ = norm_back(flat(grad_normed), flat(plain_in), flat(scale_in), gain)
    input_grad = grad_mixed + grad_from_in.reshape(grad_mixed.shape)
    bias_out = lax.dynamic_slice_in_dim(
        small_out[16:20].reshape(2, 4, 64), me_f * 8, 8, axis=2
    )
    small_out = lax.dynamic_slice_in_dim(small_out[:14], me_z * 32, 32, axis=1)
    return (
        output,
        input_grad,
        out4[:3].astype(F32),
        bias_out,
        out4[3].T.astype(F32),
        small_out[6:14].T,
        up_out.astype(F32),
        down_out.astype(F32),
        small_out[:2],
        small_out[2:5],
        small_out[5],
    )


def solution(mesh):
    placed = (
        P(None, ("fsdp", "tensor"), None),
        P(None, "fsdp"),
        P(None, "fsdp", None),
        P(None, "fsdp", "tensor"),
        P(None, "tensor", "fsdp"),
        P("tensor", "fsdp"),
        P(("fsdp", "tensor"), None),
        P(None, "fsdp", "tensor"),
        P(None, "tensor", "fsdp"),
        P(None, ("fsdp", "tensor")),
        P(None, ("fsdp", "tensor")),
        P(None, ("fsdp", "tensor"), None),
    )
    return jax.shard_map(
        fast_body if fits(mesh) else plain_body,
        mesh=mesh,
        in_specs=placed,
        out_specs=(
            P(None, ("fsdp", "tensor"), None),
            P(None, ("fsdp", "tensor"), None),
            P(None, "fsdp", "tensor"),
            P(None, "tensor", "fsdp"),
            P("tensor", "fsdp"),
            P(("fsdp", "tensor"), None),
            P(None, "fsdp", "tensor"),
            P(None, "tensor", "fsdp"),
            P(None, ("fsdp", "tensor")),
            P(None, ("fsdp", "tensor")),
            P(("fsdp", "tensor")),
        ),
        check_vma=False,
    )
```

```python
from functools import partial

import jax
import jax.numpy as jnp
from jax import lax
from jax.experimental import pallas as pl
from jax.experimental.pallas import tpu as pltpu
from jax.sharding import PartitionSpec as P

EPSILON = 1e-05
MASKED = -1e30
HIGHEST = lax.Precision.HIGHEST


def norm_rows(row_data, gain_row, shift_row):
    centered = row_data - jnp.mean(row_data, axis=-1, keepdims=True)
    inv_scale = lax.rsqrt(jnp.mean(centered * centered, axis=-1, keepdims=True) + EPSILON)
    normed = centered * inv_scale
    return (normed * gain_row + shift_row, normed, inv_scale)


def norm_back(grad_out, normed, inv_scale, gain_row):
    grad_normed = grad_out * gain_row
    interior = (
        grad_normed
        - jnp.mean(grad_normed, axis=-1, keepdims=True)
        - normed * jnp.mean(grad_normed * normed, axis=-1, keepdims=True)
    )
    return (inv_scale * interior, jnp.sum(grad_out * normed, axis=0), jnp.sum(grad_out, axis=0))


def tree_allowed(query_segs, key_segs, row_start):
    query_seg = query_segs[:, None]
    key_seg = key_segs[None, :]
    related = (
        (key_seg == 0)
        | (key_seg == query_seg)
        | (query_seg >= 5) & (key_seg == (query_seg - 5) // 2 + 1)
    )
    row_index = row_start + jnp.arange(query_segs.shape[0])[:, None]
    col_index = jnp.arange(key_segs.shape[0])[None, :]
    return related & (col_index <= row_index)


def block_scores(queries, key_rows, allowed, factor):
    scaled = (
        jnp.einsum("qhd,khd->hqk", queries, key_rows, preferred_element_type=jnp.float32) * factor
    )
    return jnp.where(allowed[None], scaled, MASKED)


def attend_forward(queries, key_rows, value_rows, segments, block_len):
    tree_len = queries.shape[0]
    factor = queries.shape[-1] ** (-0.5)
    outputs, totals = ([], [])
    for row_start in range(0, tree_len, block_len):
        row_stop = row_start + block_len
        allowed = tree_allowed(segments[row_start:row_stop], segments[:row_stop], row_start)
        scores = block_scores(queries[row_start:row_stop], key_rows[:row_stop], allowed, factor)
        peak_score = jnp.max(scores, axis=-1, keepdims=True)
        exponent = jnp.exp(scores - peak_score)
        denom_sum = jnp.sum(exponent, axis=-1, keepdims=True)
        weights = (exponent / denom_sum).astype(jnp.bfloat16)
        outputs.append(
            jnp.einsum(
                "hqk,khd->qhd", weights, value_rows[:row_stop], preferred_element_type=jnp.float32
            )
        )
        totals.append(peak_score + jnp.log(denom_sum))
    return (jnp.concatenate(outputs, axis=0), jnp.concatenate(totals, axis=1))


def attend_backward(queries, key_rows, value_rows, segments, grad_heads, log_sums, block_len):
    tree_len = queries.shape[0]
    factor = queries.shape[-1] ** (-0.5)
    grad_keys = jnp.zeros(key_rows.shape, jnp.float32)
    grad_values = jnp.zeros(value_rows.shape, jnp.float32)
    grad_queries = []
    for row_start in range(0, tree_len, block_len):
        row_stop = row_start + block_len
        allowed = tree_allowed(segments[row_start:row_stop], segments[:row_stop], row_start)
        scores = block_scores(queries[row_start:row_stop], key_rows[:row_stop], allowed, factor)
        weights = jnp.exp(scores - log_sums[:, row_start:row_stop])
        grad_weights = jnp.einsum(
            "qhd,khd->hqk",
            grad_heads[row_start:row_stop],
            value_rows[:row_stop],
            preferred_element_type=jnp.float32,
        )
        grad_scores = (
            weights * (grad_weights - jnp.sum(weights * grad_weights, axis=-1, keepdims=True))
        ).astype(jnp.bfloat16)
        grad_queries.append(
            jnp.einsum(
                "hqk,khd->qhd", grad_scores, key_rows[:row_stop], preferred_element_type=jnp.float32
            )
            * factor
        )
        grad_keys = grad_keys.at[:row_stop].add(
            jnp.einsum(
                "hqk,qhd->khd",
                grad_scores,
                queries[row_start:row_stop],
                preferred_element_type=jnp.float32,
            )
            * factor
        )
        grad_values = grad_values.at[:row_stop].add(
            jnp.einsum(
                "hqk,qhd->khd",
                weights.astype(jnp.bfloat16),
                grad_heads[row_start:row_stop],
                preferred_element_type=jnp.float32,
            )
        )
    return (jnp.concatenate(grad_queries, axis=0), grad_keys, grad_values)


def gelu_back(hidden, grad_act):
    return jax.vjp(partial(jax.nn.gelu, approximate=True), hidden)[1](grad_act)[0].astype(
        jnp.bfloat16
    )


def plain_body(
    tokens,
    segment,
    route,
    w_qkv,
    bias_qv,
    w_o,
    w_router,
    w_up,
    w_down,
    norm_gains,
    shifts,
    cotangent,
):
    micro_count, local_rows, model_width = tokens.shape
    tree_len = segment.shape[1]
    block_len = min(512, tree_len)
    expert_count = w_up.shape[0]
    tensor_count = lax.axis_size("tensor")
    local_cap = max(2, 3 * local_rows // (2 * expert_count))
    tree_cap = tensor_count * local_cap
    slot_count = expert_count * tree_cap
    position = lax.axis_index("tensor") * local_rows
    gains_all, shifts_all, router_all = (
        lax.all_gather(norm_gains, ("fsdp", "tensor"), axis=1, tiled=True),
        lax.all_gather(shifts, ("fsdp", "tensor"), axis=1, tiled=True),
        lax.all_gather(w_router, ("fsdp", "tensor"), axis=0, tiled=True),
    )
    gains_all = gains_all.astype(jnp.float32)
    shifts_all = shifts_all.astype(jnp.float32)
    router_wide = router_all.astype(jnp.float32)
    qkv_all, bias_all, out_all = (
        lax.all_gather(w_qkv, "fsdp", axis=1, tiled=True),
        lax.all_gather(bias_qv, "fsdp", axis=2, tiled=True),
        lax.all_gather(w_o, "fsdp", axis=1, tiled=True),
    )
    head_width = qkv_all.shape[2]
    head_count = bias_all.shape[1]
    bias_rows = bias_all.reshape(2, head_width).astype(jnp.float32)
    qkv_bias = jnp.stack([bias_rows[0], jnp.zeros_like(bias_rows[0]), bias_rows[1]])
    up_grad = jnp.zeros((expert_count, model_width, w_up.shape[2]), jnp.float32)
    down_grad = jnp.zeros((expert_count, w_down.shape[1], model_width), jnp.float32)
    qkv_grad = jnp.zeros(qkv_all.shape, jnp.float32)
    bias_grad = jnp.zeros((2, head_width), jnp.float32)
    out_grad = jnp.zeros(out_all.shape, jnp.float32)
    router_grad = jnp.zeros(router_wide.shape, jnp.float32)
    gain_grad = jnp.zeros(gains_all.shape, jnp.float32)
    shift_grad = jnp.zeros(shifts_all.shape, jnp.float32)
    expert_ids = jnp.arange(expert_count, dtype=jnp.int32)
    results, input_grads = ([], [])
    for micro_index in range(micro_count):
        segments = segment[micro_index]
        routes_all = route[micro_index, :, 0]
        inputs = tokens[micro_index].astype(jnp.float32)
        normed_in, plain_in, scale_in = norm_rows(inputs, gains_all[0], shifts_all[0])
        normed_tree = lax.all_gather(normed_in.astype(jnp.bfloat16), "tensor", axis=0, tiled=True)
        projected = (
            jnp.einsum("td,jdc->tjc", normed_tree, qkv_all, preferred_element_type=jnp.float32)
            + qkv_bias
        ).astype(jnp.bfloat16)
        queries = projected[:, 0].reshape(tree_len, head_count, -1)
        key_rows = projected[:, 1].reshape(tree_len, head_count, -1)
        value_rows = projected[:, 2].reshape(tree_len, head_count, -1)
        attended, log_sums = attend_forward(queries, key_rows, value_rows, segments, block_len)
        heads_low = attended.reshape(tree_len, head_width).astype(jnp.bfloat16)
        attention_rows = lax.psum_scatter(
            jnp.dot(heads_low, out_all, preferred_element_type=jnp.float32).astype(jnp.bfloat16),
            "tensor",
            scatter_dimension=0,
            tiled=True,
        ).astype(jnp.float32)
        residual = inputs + attention_rows + shifts_all[2]
        normed_mid, plain_mid, scale_mid = norm_rows(residual, gains_all[1], shifts_all[1])
        mid_low = normed_mid.astype(jnp.bfloat16)
        router_probs = jax.nn.softmax(
            jnp.dot(mid_low, router_all, preferred_element_type=jnp.float32), axis=-1
        )
        own_routes = lax.dynamic_slice_in_dim(routes_all, position, local_rows)
        own_choice = own_routes[:, None] == expert_ids[None, :]
        gate_value = jnp.sum(jnp.where(own_choice, router_probs, 0.0), axis=-1)
        grad_final = cotangent[micro_index].astype(jnp.float32)
        grad_returned = (gate_value[:, None] * grad_final).astype(jnp.bfloat16)
        up_all, down_all = (
            lax.all_gather(w_up, "fsdp", axis=1, tiled=True),
            lax.all_gather(w_down, "fsdp", axis=2, tiled=True),
        )
        chosen = routes_all[:, None] == expert_ids[None, :]
        running = jnp.cumsum(chosen.astype(jnp.int32), axis=0)
        slot_index = routes_all * tree_cap + jnp.sum(jnp.where(chosen, running, 0), axis=-1) - 1
        slot_token = (
            jnp.zeros((slot_count,), jnp.int32)
            .at[slot_index]
            .set(jnp.arange(tree_len, dtype=jnp.int32))
        )
        slot_filled = jnp.zeros((slot_count,), jnp.bool_).at[slot_index].set(True)
        mid_tree = lax.all_gather(mid_low, "tensor", axis=0, tiled=True)
        routed = jnp.where(slot_filled[:, None], mid_tree[slot_token], 0).reshape(
            expert_count, tree_cap, model_width
        )
        hidden = jnp.einsum("ecd,edf->ecf", routed, up_all, preferred_element_type=jnp.float32)
        activated = jax.nn.gelu(hidden, approximate=True).astype(jnp.bfloat16)
        expert_rows = jnp.einsum(
            "ecf,efd->ecd", activated, down_all, preferred_element_type=jnp.float32
        ).reshape(slot_count, model_width)
        returned = lax.psum_scatter(
            expert_rows[slot_index].astype(jnp.bfloat16), "tensor", scatter_dimension=0, tiled=True
        ).astype(jnp.float32)
        grad_tree = lax.all_gather(grad_returned, "tensor", axis=0, tiled=True)
        grad_expert = jnp.where(slot_filled[:, None], grad_tree[slot_token], 0).reshape(
            expert_count, tree_cap, model_width
        )
        down_grad = down_grad + jnp.einsum(
            "ecf,ecd->efd", activated, grad_expert, preferred_element_type=jnp.float32
        )
        grad_act = jnp.einsum(
            "ecd,efd->ecf", grad_expert, down_all, preferred_element_type=jnp.float32
        )
        grad_hidden = gelu_back(hidden, grad_act)
        up_grad = up_grad + jnp.einsum(
            "ecd,ecf->edf", routed, grad_hidden, preferred_element_type=jnp.float32
        )
        grad_routed = jnp.einsum(
            "ecf,edf->ecd", grad_hidden, up_all, preferred_element_type=jnp.float32
        ).reshape(slot_count, model_width)
        grad_mid = lax.psum_scatter(
            grad_routed[slot_index].astype(jnp.bfloat16), "tensor", scatter_dimension=0, tiled=True
        ).astype(jnp.float32)
        results.append(
            (residual + gate_value[:, None] * returned + shifts_all[3]).astype(jnp.bfloat16)
        )
        grad_gate = jnp.sum(grad_final * returned, axis=-1)
        grad_logits = router_probs * (
            jnp.where(own_choice, grad_gate[:, None], 0.0) - (gate_value * grad_gate)[:, None]
        )
        router_grad = router_grad + jnp.einsum(
            "td,te->de", mid_low.astype(jnp.float32), grad_logits, precision=HIGHEST
        )
        grad_mid = grad_mid + jnp.einsum("te,de->td", grad_logits, router_wide, precision=HIGHEST)
        grad_from_mid, gain_mid, shift_mid = norm_back(grad_mid, plain_mid, scale_mid, gains_all[1])
        grad_mixed = grad_final + grad_from_mid
        proj_tree = lax.all_gather(grad_mixed.astype(jnp.bfloat16), "tensor", axis=0, tiled=True)
        out_grad = out_grad + jnp.einsum(
            "tc,td->cd", heads_low, proj_tree, preferred_element_type=jnp.float32
        )
        grad_heads = jnp.einsum(
            "td,cd->tc", proj_tree, out_all, preferred_element_type=jnp.float32
        ).astype(jnp.bfloat16)
        grad_queries, grad_keys, grad_values = attend_backward(
            queries,
            key_rows,
            value_rows,
            segments,
            grad_heads.reshape(tree_len, head_count, -1),
            log_sums,
            block_len,
        )
        grad_proj_all = jnp.stack(
            [
                grad_queries.reshape(tree_len, head_width),
                grad_keys.reshape(tree_len, head_width),
                grad_values.reshape(tree_len, head_width),
            ],
            axis=1,
        ).astype(jnp.bfloat16)
        qkv_grad = qkv_grad + jnp.einsum(
            "td,tjc->jdc", normed_tree, grad_proj_all, preferred_element_type=jnp.float32
        )
        bias_grad = bias_grad + jnp.sum(grad_proj_all[:, 0::2].astype(jnp.float32), axis=0)
        grad_normed = lax.psum_scatter(
            jnp.einsum(
                "tjc,jdc->td", grad_proj_all, qkv_all, preferred_element_type=jnp.float32
            ).astype(jnp.bfloat16),
            "tensor",
            scatter_dimension=0,
            tiled=True,
        ).astype(jnp.float32)
        grad_from_in, gain_in, shift_in = norm_back(grad_normed, plain_in, scale_in, gains_all[0])
        input_grads.append(grad_mixed + grad_from_in)
        gain_grad = gain_grad + jnp.stack([gain_in, gain_mid])
        shift_grad = shift_grad + jnp.stack(
            [shift_in, shift_mid, jnp.sum(grad_mixed, axis=0), jnp.sum(grad_final, axis=0)]
        )
    weight_sums = (
        lax.psum_scatter(
            qkv_grad.astype(jnp.bfloat16), "fsdp", scatter_dimension=1, tiled=True
        ).astype(jnp.float32),
        lax.psum_scatter(
            bias_grad.reshape(2, head_count, -1).astype(jnp.bfloat16),
            "fsdp",
            scatter_dimension=2,
            tiled=True,
        ).astype(jnp.float32),
        lax.psum_scatter(
            out_grad.astype(jnp.bfloat16), "fsdp", scatter_dimension=1, tiled=True
        ).astype(jnp.float32),
    )
    up_final, down_final = (
        lax.psum_scatter(
            up_grad.astype(jnp.bfloat16), "fsdp", scatter_dimension=1, tiled=True
        ).astype(jnp.float32),
        lax.psum_scatter(
            down_grad.astype(jnp.bfloat16), "fsdp", scatter_dimension=2, tiled=True
        ).astype(jnp.float32),
    )
    small_sums = (
        lax.psum_scatter(gain_grad, ("fsdp", "tensor"), scatter_dimension=1, tiled=True),
        lax.psum_scatter(shift_grad, ("fsdp", "tensor"), scatter_dimension=1, tiled=True),
        lax.psum_scatter(router_grad, ("fsdp", "tensor"), scatter_dimension=0, tiled=True),
    )
    return (
        jnp.stack(results),
        jnp.stack(input_grads),
        weight_sums[0],
        weight_sums[1],
        weight_sums[2],
        small_sums[2],
        up_final,
        down_final,
        small_sums[0],
        small_sums[1][:3],
        small_sums[1][3],
    )


MESH = pl.DeviceIdType.MESH
BF = jnp.bfloat16
F32 = jnp.float32


def fits(mesh):
    return mesh.shape["fsdp"] == 8 and mesh.shape["tensor"] == 4


def flip(index, bit):
    return index + bit * (1 - 2 * (lax.rem(index // bit, 2)))


def place(fsdp, tensor):
    return {"fsdp": fsdp, "tensor": tensor}


def greet(partners):
    barrier = pltpu.get_barrier_semaphore()
    for fsdp, tensor in partners:
        pl.semaphore_signal(barrier, inc=1, device_id=place(fsdp, tensor), device_id_type=MESH)
    pl.semaphore_wait(barrier, len(partners))


def greet_all(mine):
    barrier = pltpu.get_barrier_semaphore()

    def signal(step, carry):
        other = lax.rem(mine + step, 32)
        pl.semaphore_signal(
            barrier, inc=1, device_id=place(other // 4, lax.rem(other, 4)), device_id_type=MESH
        )
        return carry

    lax.fori_loop(1, 32, signal, 0)
    pl.semaphore_wait(barrier, 31)


class Sender:
    def __init__(self, send_sem, recv_sem):
        self.send_sem, self.recv_sem, self.count = send_sem, recv_sem, 0
        self.open = []

    def copy(self, source, target, fsdp, tensor, when=None):
        made = pltpu.make_async_remote_copy(
            src_ref=source,
            dst_ref=target,
            send_sem=self.send_sem.at[self.count],
            recv_sem=self.recv_sem.at[self.count],
            device_id=place(fsdp, tensor),
            device_id_type=MESH,
        )
        self.count += 1
        if when is None:
            made.start()
        else:
            pl.when(when)(made.start)
        self.open.append((made, when))
        return made

    def finish(self):
        for made, when in self.open:
            if when is None:
                made.wait_send()
            else:
                pl.when(when)(made.wait_send)


def attend_kernel(
    w4, small, tokens, up, down, bias, chosen_hbm, cotangent,
    full4, params, rows_out, normed_out, q_out, k_out, v_out, heads_out, residual_out, probs_out,
    slots_out, pick_out, gates_out, up_own, down_own,
    weights, pieces, table, rows_all, normed, queries, keys, values, heads, residual, probs,
    slots, pick, gates, mask, chosen, grads, router,
    send_sem, recv_sem, local_sem, up_send, up_recv, down_send, down_recv, trunk_send, trunk_recv,
):
    cap = slots.shape[2] // 8
    me_f, me_z = lax.axis_index("fsdp"), lax.axis_index("tensor")
    mine = me_f * 4 + me_z
    core = lax.rem(me_f, 2)
    greet_all(mine)
    sender = Sender(send_sem, recv_sem)

    def rows(fsdp):
        return pl.ds(pl.multiple_of(fsdp * 128, 128), 128)

    def cols(first, width):
        return pl.ds(pl.multiple_of(first * 256, 256), width)

    trunk_rows, halo_rows, own_rows = pl.ds(0, 256), pl.ds(256, 128), pl.ds(384, 256)
    first = [
        sender.copy(w4, weights.at[:, rows(me_f), cols(me_z, 256)], me_f, flip(me_z, 1)),
        sender.copy(small, pieces.at[me_f, me_z], me_f, flip(me_z, 1)),
    ]
    local = [
        pltpu.make_async_copy(w4, weights.at[:, rows(me_f), cols(me_z, 256)], local_sem.at[0]),
        pltpu.make_async_copy(small, pieces.at[me_f, me_z], local_sem.at[1]),
        pltpu.make_async_copy(tokens, rows_all.at[:, own_rows], local_sem.at[2]),
        pltpu.make_async_copy(bias, mask, local_sem.at[3]),
        pltpu.make_async_copy(chosen_hbm, chosen, local_sem.at[16]),
        pltpu.make_async_copy(cotangent, grads, local_sem.at[17]),
    ]
    for copy in local:
        copy.start()

    piece = [(micro, half) for micro in range(2) for half in range(2)]

    def trunk_copy(index, from_tokens):
        micro, half = piece[index]
        part = pl.ds(half * 128, 128)
        return pltpu.make_async_remote_copy(
            src_ref=tokens.at[micro, part] if from_tokens else rows_all.at[micro, part],
            dst_ref=rows_all.at[micro, part],
            send_sem=trunk_send.at[index],
            recv_sem=trunk_recv.at[index],
            device_id=place(me_f, lax.rem(me_z + 1, 4)),
            device_id_type=MESH,
        )

    halo_copy = pltpu.make_async_remote_copy(
        src_ref=tokens.at[:, pl.ds(128, 128)],
        dst_ref=rows_all.at[:, halo_rows],
        send_sem=trunk_send.at[4],
        recv_sem=trunk_recv.at[4],
        device_id=place(me_f, lax.rem(me_z + 1, 4)),
        device_id_type=MESH,
    )

    def expert_copies(step):
        fsdp = (
            lax.rem(me_f // 4 + step // 16, 2) * 4
            + lax.rem(me_f // 2 + step // 8, 2) * 2
            + lax.rem(me_f + step // 4, 2)
        )
        tensor = lax.rem(me_z + step, 4)
        expert = 2 * tensor + fsdp // 4
        quarter = pl.ds(pl.multiple_of(lax.rem(fsdp, 4) * 256, 256), 256)
        return (
            (up.at[expert, :, quarter], up_own.at[rows(me_f), cols(me_z, 256)]),
            (down.at[expert, quarter, :], down_own.at[cols(me_z, 256), rows(me_f)]),
            (fsdp, tensor),
        )

    def remote(step):
        ups, downs, (fsdp, tensor) = expert_copies(step)
        return [
            pltpu.make_async_remote_copy(
                src_ref=pair[0], dst_ref=pair[1], send_sem=sems[0].at[step],
                recv_sem=sems[1].at[step], device_id=place(fsdp, tensor), device_id_type=MESH,
            )
            for pair, sems in ((ups, (up_send, up_recv)), (downs, (down_send, down_recv)))
        ]

    def start_step(step, carry):
        for copy in remote(step):
            copy.start()
        return carry

    @pl.when(me_z == 0)
    def _():
        trunk_copy(0, True).start()

    inner = (me_z == 1) | (me_z == 2)

    @pl.when(inner)
    def _():
        halo_copy.start()

    def pass_up(level, indices):
        @pl.when(me_z == level)
        def _():
            for index in indices:
                trunk_copy(index, False).wait_recv()
                if level < 3:
                    trunk_copy(index, False).start()

    for copy in first:
        copy.wait_recv()
    for copy in local:
        copy.wait()

    pair = me_z // 2 * 2

    def pair_views(number):
        return [
            weights.at[:, rows(me_f), cols(number, 512)],
            pieces.at[me_f, pl.ds(number, 2)],
        ]

    second = [
        sender.copy(view, view, me_f, 3 - me_z, inner) for view in pair_views(pair)
    ]

    @pl.when(inner)
    def _():
        for copy in second:
            copy.wait_recv()

    handed = [
        sender.copy(view, view, me_f, flip(me_z, 1), inner) for view in pair_views(2 - pair)
    ]

    @pl.when(me_z == 0)
    def _():
        for index in range(3):
            trunk_copy(index, True).wait_send()
            trunk_copy(index + 1, True).start()

    @pl.when(~inner)
    def _():
        for copy in handed:
            copy.wait_recv()

    across = flip(me_f, 2) * (1 - core) + flip(me_f, 4) * core
    along = flip(me_f, 4) * (1 - core) + flip(me_f, 2) * core

    def blocks(fsdp_list, target):
        made = []
        for fsdp in fsdp_list:
            view = weights.at[:, rows(fsdp)]
            made.append(sender.copy(view, view, target, me_z))
            made.append(sender.copy(pieces.at[fsdp], pieces.at[fsdp], target, me_z))
        return made

    third = blocks([me_f], across)
    pass_up(1, (0, 1, 2, 3))
    lax.fori_loop(1, 8, start_step, 0)
    pass_up(2, (0, 1))
    for copy in third:
        copy.wait_recv()
    fourth = blocks([me_f, across], along)
    ups, downs, _ = expert_copies(0)
    own = [
        pltpu.make_async_copy(ups[0], ups[1], local_sem.at[4]),
        pltpu.make_async_copy(downs[0], downs[1], local_sem.at[5]),
    ]
    for copy in own:
        copy.start()
    pass_up(2, (2, 3))
    pass_up(3, (0, 1, 2, 3))

    @pl.when(me_z > 1)
    def _():
        halo_copy.wait_recv()

    fill = [
        pltpu.make_async_copy(tokens, rows_all.at[:, trunk_rows], local_sem.at[0]),
        pltpu.make_async_copy(
            tokens.at[:, pl.ds(128, 128)], rows_all.at[:, halo_rows], local_sem.at[1]
        ),
    ]
    for copy, when in zip(fill, (me_z == 0, me_z < 2)):
        pl.when(when)(copy.start)
        pl.when(when)(copy.wait)

    for copy in fourth:
        copy.wait_recv()
    fifth = blocks([core, core + 2, core + 4, core + 6], flip(me_f, 1))
    lax.fori_loop(8, 32, start_step, 0)
    for copy in fifth:
        copy.wait_recv()

    for fsdp in range(8):
        total = pieces[fsdp, 0, 0:16].astype(F32)
        for tensor in range(1, 4):
            total = total + pieces[fsdp, tensor, 0:16].astype(F32)
        table[0:16, fsdp * 128 : fsdp * 128 + 128] = total
    for tensor in range(4):
        total = pieces[0, tensor, 16:32].astype(F32)
        for fsdp in range(1, 8):
            total = total + pieces[fsdp, tensor, 16:32].astype(F32)
        for which in range(2):
            for half in range(2):
                lane = tensor * 256 + half * 128
                table[14 + which : 15 + which, lane : lane + 128] = total[
                    2 * which + half : 2 * which + half + 1, :
                ]
    saves = [
        pltpu.make_async_copy(weights, full4, local_sem.at[6]),
        pltpu.make_async_copy(table, params, local_sem.at[7]),
        pltpu.make_async_copy(rows_all, rows_out, local_sem.at[8]),
    ]
    for copy in saves:
        copy.start()

    def tile(index):
        return pl.ds(pl.multiple_of(index * 256, 256), 256)

    def lanes(index):
        return pl.ds(pl.multiple_of(index * 128, 128), 128)

    def one_tree(micro, carry):
        def norm(index, carry):
            value = rows_all[micro, lanes(index), :].astype(F32)
            centered = value - jnp.mean(value, axis=-1, keepdims=True)
            scale = lax.rsqrt(jnp.mean(centered * centered, axis=-1, keepdims=True) + EPSILON)
            out = centered * scale * table[0:1, :] + table[2:3, :]
            normed[micro, lanes(index), :] = out.astype(BF)
            return carry

        lax.fori_loop(0, 5, norm, 0)

        def project(index, carry):
            place_cols = tile(index)
            key = dot_nn(normed[micro], weights[1, :, place_cols])
            keys[micro, :, place_cols] = key.astype(BF)
            value = dot_nn(normed[micro], weights[2, :, place_cols]) + table[15:16, place_cols]
            values[micro, :, place_cols] = value.astype(BF)
            query = dot_nn(normed[micro, own_rows], weights[0, :, place_cols])
            queries[micro, :, place_cols] = (query + table[14:15, place_cols]).astype(BF)
            return carry

        lax.fori_loop(0, 4, project, 0)

        def two_heads(index, carry):
            query, key, value = (
                part[micro, :, lanes(index)] for part in (queries, keys, values)
            )
            low = lax.broadcasted_iota(jnp.int32, (256, 128), 1) < 64
            outs = []
            for which in range(2):
                one = jnp.where(low if which == 0 else ~low, query, jnp.zeros_like(query))
                scores = dot_nt(one, key) * 0.125 + mask[micro]
                exponent = jnp.exp(scores - jnp.max(scores, axis=-1, keepdims=True))
                total = jnp.sum(exponent, axis=-1, keepdims=True)
                weight = (exponent * (1.0 / total)).astype(BF)
                probs[micro, 2 * index + which] = weight
                outs.append(dot_nn(weight, value))
            heads[micro, :, lanes(index)] = jnp.where(low, outs[0], outs[1]).astype(BF)
            return carry

        lax.fori_loop(0, 8, two_heads, 0)

        def mix(index, carry):
            place_cols = tile(index)
            out = dot_nt(heads[micro], weights[3, place_cols, :])
            residual[micro, :, place_cols] = (
                rows_all[micro, own_rows, place_cols].astype(F32) + out + table[4:5, place_cols]
            )
            return carry

        lax.fori_loop(0, 4, mix, 0)

        value = residual[micro]
        centered = value - jnp.mean(value, axis=-1, keepdims=True)
        scale = lax.rsqrt(jnp.mean(centered * centered, axis=-1, keepdims=True) + EPSILON)
        middle = (centered * scale * table[1:2, :] + table[3:4, :]).astype(BF)
        lane = lax.broadcasted_iota(jnp.int32, (256, 128), 1)
        logits = jnp.where(lane < 8, dot_nt(middle, router[...]), MASKED)
        exponent = jnp.exp(logits - jnp.max(logits, axis=-1, keepdims=True))
        share = exponent / jnp.sum(exponent, axis=-1, keepdims=True)
        gates[micro] = share
        choice = chosen[micro]
        wide = choice.astype(F32)
        gate = jnp.sum(share * wide, axis=-1, keepdims=True)
        earlier = (
            lax.broadcasted_iota(jnp.int32, (256, 256), 1)
            < lax.broadcasted_iota(jnp.int32, (256, 256), 0)
        ).astype(F32).astype(BF)
        rank = dot_nn(earlier, choice) + (lane * cap).astype(F32)
        slot = jnp.sum(wide * rank, axis=-1, keepdims=True)
        column = lax.broadcasted_iota(jnp.int32, (256, 8 * cap), 1).astype(F32)
        hit = (column == slot).astype(F32).astype(BF)
        pick[micro] = hit
        slots[0, micro] = dot_tn(hit, middle).astype(BF)
        returned = (gate * grads[micro].astype(F32)).astype(BF)
        slots[1, micro] = dot_tn(hit, returned).astype(BF)
        return carry

    router[...] = jnp.zeros_like(router)
    router[0:16, :] = jnp.concatenate(
        [table[6:14, :], jnp.zeros((8, 1024), F32)], axis=0
    ).astype(BF)
    lax.fori_loop(0, 2, one_tree, 0)
    late = [
        (normed, normed_out), (queries, q_out), (keys, k_out), (values, v_out),
        (heads, heads_out), (residual, residual_out), (probs, probs_out), (slots, slots_out),
        (pick, pick_out), (gates, gates_out),
    ]
    for index, (source, target) in enumerate(late):
        copy = pltpu.make_async_copy(source, target, local_sem.at[(9 + index) if index < 7 else (11 + index)])
        copy.start()
        saves.append(copy)

    @pl.when((me_z > 0) & (me_z < 3))
    def _():
        for index in range(4):
            trunk_copy(index, False).wait_send()

    @pl.when(me_z == 0)
    def _():
        trunk_copy(3, True).wait_send()

    @pl.when(inner)
    def _():
        halo_copy.wait_send()

    for copy in own:
        copy.wait()

    def end_step(step, carry):
        for copy in remote(step):
            copy.wait_send()
            copy.wait_recv()
        return carry

    lax.fori_loop(1, 32, end_step, 0)
    sender.finish()
    for copy in saves:
        copy.wait()


def any_spec(count):
    return [pl.BlockSpec(memory_space=pl.ANY)] * count


def attend_all(w4, small, tokens, up, down, bias, chosen, cotangent, cap):
    kept = [
        ((4, 1024, 1024), BF), ((16, 1024), F32), ((2, 640, 1024), BF), ((2, 640, 1024), BF),
        ((2, 256, 1024), BF), ((2, 640, 1024), BF), ((2, 640, 1024), BF), ((2, 256, 1024), BF),
        ((2, 256, 1024), F32), ((2, 16, 256, 640), BF), ((2, 2, 8 * cap, 1024), BF),
        ((2, 256, 8 * cap), BF), ((2, 256, 128), F32),
    ]
    dma = pltpu.SemaphoreType.DMA
    return pl.pallas_call(
        attend_kernel,
        out_shape=[
            *(jax.ShapeDtypeStruct(shape, dtype) for shape, dtype in kept),
            jax.ShapeDtypeStruct((1024, 1024), BF),
            jax.ShapeDtypeStruct((1024, 1024), BF),
        ],
        in_specs=any_spec(8),
        out_specs=any_spec(15),
        scratch_shapes=[
            pltpu.VMEM(*kept[0]),
            pltpu.VMEM((8, 4, 32, 128), BF),
            *(pltpu.VMEM(shape, dtype) for shape, dtype in kept[1:]),
            pltpu.VMEM((2, 256, 640), F32),
            pltpu.VMEM((2, 256, 128), BF),
            pltpu.VMEM((2, 256, 1024), BF),
            pltpu.VMEM((128, 1024), BF),
            dma((20,)), dma((20,)), dma((21,)),
            dma((32,)), dma((32,)), dma((32,)), dma((32,)), dma((5,)), dma((5,)),
        ],
        compiler_params=pltpu.CompilerParams(
            collective_id=0, has_side_effects=True, vmem_limit_bytes=60 << 20
        ),
        name="attend",
    )(w4, small, tokens, up, down, bias, chosen, cotangent)


def gelu_pair(hidden):
    scale = (2.0 / jnp.pi) ** 0.5
    square = hidden * hidden
    bend = jnp.tanh(scale * hidden * (1.0 + 0.044715 * square))
    half = 0.5 * (1.0 + bend)
    slope = half + 0.5 * hidden * (1.0 - bend * bend) * scale * (1.0 + 0.134145 * square)
    return hidden * half, slope


def dot_nn(left, right):
    return lax.dot_general(left, right, (((1,), (0,)), ((), ())), preferred_element_type=F32)


def dot_nt(left, right):
    return lax.dot_general(left, right, (((1,), (1,)), ((), ())), preferred_element_type=F32)


def dot_tn(left, right):
    return lax.dot_general(left, right, (((0,), (0,)), ((), ())), preferred_element_type=F32)


def expert_kernel(
    slots, up_hbm, down_hbm, returned, up_grad, down_grad,
    arrived, parts, got, got_x, up, down, up_sum, down_sum, act, slope,
    send_sem, recv_sem, local_sem,
):
    cap = slots.shape[3]
    group = 8 * cap
    rows = 2 * group
    me_f, me_z = lax.axis_index("fsdp"), lax.axis_index("tensor")
    me_y, me_x, core = me_f // 4, lax.rem(me_f // 2, 2), lax.rem(me_f, 2)
    far_x = 1 - me_x
    x_mate, core_mate = flip(me_f, 2), flip(me_f, 1)
    far = []
    for step in range(1, 8):
        far.append(
            (lax.rem(me_y + step // 4, 2) * 4 + lax.rem(me_f, 4), lax.rem(me_z + step, 4))
        )
    greet([(x_mate, me_z), (core_mate, me_z)] + far)
    sender = Sender(send_sem, recv_sem)
    load = [
        pltpu.make_async_copy(up_hbm, up, local_sem.at[0]),
        pltpu.make_async_copy(down_hbm, down, local_sem.at[1]),
    ]

    def origin_rows(fsdp, tensor):
        first = (fsdp // 4 * 4 + tensor) * cap
        return pl.ds(pl.multiple_of(first, cap), cap)

    chunks = [(kind, micro) for kind in range(2) for micro in range(2)]
    half_rows = 4 * cap
    incoming, own_in = {}, {}

    def half_of(half):
        first = (me_y + half - 2 * me_y * half) * half_rows
        return pl.ds(pl.multiple_of(first, half_rows), half_rows)

    def send_half(number):
        index, half = number // 2, number % 2
        kind, micro = chunks[index]
        target = arrived.at[kind, micro, me_x, core, origin_rows(me_f, me_z)]
        incoming[number] = [
            sender.copy(slots.at[kind, micro, 2 * tensor + fsdp // 4], target, fsdp, tensor)
            for fsdp, tensor in (far[:3] if half == 0 else far[3:])
        ]
        if half == 0:
            own = pltpu.make_async_copy(
                slots.at[kind, micro, 2 * me_z + me_y], target, local_sem.at[2 + index]
            )
            own.start()
            own_in[index] = own

    send_half(0)
    send_half(1)
    for copy in load:
        copy.start()

    def same_place(view, fsdp):
        return sender.copy(view, view, fsdp, me_z)

    across, beside, onward = {}, {}, {}

    def landed(index):
        kind, micro = chunks[index]
        across[index], beside[index] = [], []
        for half in range(2):
            for copy in incoming[2 * index + half]:
                copy.wait_recv()
            if half == 0:
                own_in[index].wait()
            if 2 * index + half + 2 < 8:
                send_half(2 * index + half + 2)
            view = arrived.at[kind, micro, me_x, core, half_of(half)]
            across[index].append(same_place(view, x_mate))
            beside[index].append(same_place(view, core_mate))

    def forwarded(index):
        kind, micro = chunks[index]
        onward[index] = []
        for half in range(2):
            across[index][half].wait_recv()
            onward[index].append(
                same_place(arrived.at[kind, micro, far_x, core, half_of(half)], core_mate)
            )

    def ready(copies):
        for copy in copies:
            copy.wait_recv()

    def tile(index):
        return pl.ds(pl.multiple_of(index * 256, 256), 256)

    def forward(micro, side):
        data = arrived.at[0, micro, side]

        def first(index, carry):
            hidden = dot_nn(data[...].reshape(rows, 1024), up[:, tile(index)])
            value, slope_value = gelu_pair(hidden)
            act[micro, side, :, tile(index)] = value.astype(BF)
            slope[micro, side, :, tile(index)] = slope_value.astype(BF)
            return carry

        lax.fori_loop(0, 4, first, 0)

        def second(index, carry):
            out = dot_nn(act[micro, side], down[:, tile(index)])
            parts[0, micro, side, :, :, tile(index)] = out.astype(BF).reshape(2, group, 256)
            return carry

        lax.fori_loop(0, 4, second, 0)

    def backward(micro, side, begin):
        data = arrived.at[0, micro, side]
        grads = arrived.at[1, micro, side]

        def first(index, carry):
            grad = grads[...].reshape(rows, 1024)
            grad_act = dot_nt(grad, down[tile(index), :])
            grad_hidden = (
                grad_act * slope[micro, side, :, tile(index)].astype(F32)
            ).astype(BF)
            slope[micro, side, :, tile(index)] = grad_hidden
            down_part = dot_tn(act[micro, side, :, tile(index)], grad)
            up_part = dot_tn(data[...].reshape(rows, 1024), grad_hidden)
            if begin:
                down_sum[tile(index), :] = down_part
                up_sum[:, tile(index)] = up_part
            else:
                down_sum[tile(index), :] += down_part
                up_sum[:, tile(index)] += up_part
            return carry

        lax.fori_loop(0, 4, first, 0)

        def second(index, carry):
            out = dot_nt(slope[micro, side], up[tile(index), :])
            parts[1, micro, side, :, :, tile(index)] = out.astype(BF).reshape(2, group, 256)
            return carry

        lax.fori_loop(0, 4, second, 0)

    def result(kind, micro):
        return parts.at[kind, micro]

    core_back, x_back, home = {}, {}, {}

    def back_core(index):
        kind, micro = chunks[index]
        core_back[index] = sender.copy(
            result(kind, micro).at[:, 1 - core], got.at[kind, micro], core_mate, me_z
        )

    def add_rows(target, source, count=8):
        def step(row, carry):
            part = pl.ds(pl.multiple_of(row * cap, cap), cap)
            target[part] = (target[part].astype(F32) + source[part].astype(F32)).astype(BF)
            return carry

        lax.fori_loop(0, count, step, 0)

    def back_x(index):
        kind, micro = chunks[index]
        core_back[index].wait_recv()
        mine = result(kind, micro)
        add_rows(mine.at[far_x, core], got.at[kind, micro, far_x])
        x_back[index] = [
            sender.copy(
                mine.at[far_x, core, half_of(half)], got_x.at[kind, micro, half_of(half)],
                x_mate, me_z,
            )
            for half in range(2)
        ]
        add_rows(mine.at[me_x, core], got.at[kind, micro, me_x])

    def back_home(index):
        kind, micro = chunks[index]
        mine = result(kind, micro).at[me_x, core]
        target = returned.at[kind, micro, 2 * me_z + me_y]
        home[index] = []
        for half in range(2):
            x_back[index][half].wait_recv()
            part = half_of(half)
            add_rows(mine.at[part], got_x.at[kind, micro, part], 4)
            for fsdp, tensor in far[:3] if half == 0 else far[3:]:
                home[index].append(
                    sender.copy(mine.at[origin_rows(fsdp, tensor)], target, fsdp, tensor)
                )
            if half == 0:
                own = pltpu.make_async_copy(
                    mine.at[origin_rows(me_f, me_z)], target, local_sem.at[2 + index]
                )
                own.start()
                own_in[index] = own

    landed(0)
    for copy in load:
        copy.wait()
    ready(beside[0])
    forward(0, me_x)
    landed(1)
    forwarded(0)
    ready(beside[1])
    forward(1, me_x)
    ready(onward[0])
    forward(0, far_x)
    back_core(0)
    landed(2)
    forwarded(1)
    ready(beside[2])
    backward(0, me_x, True)
    ready(onward[1])
    landed(3)
    forward(1, far_x)
    back_core(1)
    back_x(0)
    ready(beside[3])
    backward(1, me_x, False)
    forwarded(2)
    back_x(1)
    ready(onward[2])
    backward(0, far_x, False)
    back_core(2)
    back_home(0)
    forwarded(3)
    back_x(2)
    ready(onward[3])
    backward(1, far_x, False)
    back_core(3)
    back_home(1)
    back_x(3)

    def narrow(index, carry):
        part = pl.ds(pl.multiple_of(index * 64, 64), 64)
        up[part, :] = up_sum[part, :].astype(BF)
        down[part, :] = down_sum[part, :].astype(BF)
        return carry

    lax.fori_loop(0, 16, narrow, 0)
    store = [
        pltpu.make_async_copy(up, up_grad, local_sem.at[0]),
        pltpu.make_async_copy(down, down_grad, local_sem.at[1]),
    ]
    for copy in store:
        copy.start()
    back_home(2)
    back_home(3)
    for index in range(4):
        for copy in home[index]:
            copy.wait_recv()
        own_in[index].wait()
    for copy in store:
        copy.wait()
    sender.finish()


def run_experts(slots, up_own, down_own):
    cap = slots.shape[3]
    group = 8 * cap
    dma = pltpu.SemaphoreType.DMA
    return pl.pallas_call(
        expert_kernel,
        out_shape=[
            jax.ShapeDtypeStruct(slots.shape, BF),
            jax.ShapeDtypeStruct((1024, 1024), BF),
            jax.ShapeDtypeStruct((1024, 1024), BF),
        ],
        in_specs=any_spec(3),
        out_specs=any_spec(3),
        scratch_shapes=[
            pltpu.VMEM((2, 2, 2, 2, group, 1024), BF),
            pltpu.VMEM((2, 2, 2, 2, group, 1024), BF),
            pltpu.VMEM((2, 2, 2, group, 1024), BF),
            pltpu.VMEM((2, 2, group, 1024), BF),
            pltpu.VMEM((1024, 1024), BF),
            pltpu.VMEM((1024, 1024), BF),
            pltpu.VMEM((1024, 1024), F32),
            pltpu.VMEM((1024, 1024), F32),
            pltpu.VMEM((2, 2, 2 * group, 1024), BF),
            pltpu.VMEM((2, 2, 2 * group, 1024), BF),
            dma((92,)), dma((92,)), dma((6,)),
        ],
        compiler_params=pltpu.CompilerParams(
            collective_id=1, has_side_effects=True, vmem_limit_bytes=63 << 20
        ),
        cost_estimate=pl.CostEstimate(
            flops=12 * 4 * group * 2 * 1024 * 1024, bytes_accessed=20 << 20, transcendentals=0
        ),
        name="experts",
    )(slots, up_own, down_own)


def backward_kernel(
    up_grad, down_grad, back_hbm, pick_hbm, residual_hbm, cotangent, share_hbm, chosen_hbm,
    heads_hbm, q_hbm, k_hbm, v_hbm, normed_hbm, probs_hbm, full4, params,
    up_out, down_out, out4, small_out, own_out, trunk_out, halo_out, output, mixed_out,
    weights, sums, proj, heads, grad_heads, queries, keys, values, normed, probs,
    grad_q, grad_k, grad_v, own_rows, trunk_rows, halo_rows, trunk_got,
    got, cut, cut_x, cut_z, cut_m, cut_w, table, known, small_mine, small_got,
    pick, shares, chosen, router,
    send_sem, recv_sem, local_sem, up_send, up_recv, down_send, down_recv,
    small_send, small_recv, trunk_send, trunk_recv, out_sem,
):
    me_f, me_z = lax.axis_index("fsdp"), lax.axis_index("tensor")
    mine = me_f * 4 + me_z
    core = lax.rem(me_f, 2)
    me_y = me_f // 4
    greet_all(mine)
    sender = Sender(send_sem, recv_sem)

    def rows(fsdp):
        return pl.ds(pl.multiple_of(fsdp * 128, 128), 128)

    def cols(first, width):
        return pl.ds(pl.multiple_of(first * 256, 256), width)

    def tile(index):
        return pl.ds(pl.multiple_of(index * 256, 256), 256)

    def lanes(index):
        return pl.ds(pl.multiple_of(index * 128, 128), 128)

    loads = [
        pltpu.make_async_copy(source, target, local_sem.at[index])
        for index, (source, target) in enumerate([
            (pick_hbm, pick), (residual_hbm, own_rows), (cotangent, grad_q),
            (share_hbm, shares), (chosen_hbm, chosen), (params, known), (heads_hbm, heads),
            (full4, weights), (v_hbm, values), (probs_hbm.at[0], probs), (k_hbm, keys),
            (q_hbm, queries), (normed_hbm, normed),
        ])
    ]
    for index in range(4):
        for block in range(3):
            loads.append(
                pltpu.make_async_copy(
                    back_hbm.at[index, block], sums.at[index, block // 2, block % 2],
                    local_sem.at[13 + 3 * index + block],
                )
            )
    for copy in loads:
        copy.start()

    def expert_copies(step):
        other = lax.rem(mine + step, 32)
        fsdp, tensor = other // 4, lax.rem(other, 4)
        expert = 2 * me_z + me_y
        quarter = pl.ds(pl.multiple_of(lax.rem(me_f, 4) * 256, 256), 256)
        return (
            (up_grad.at[rows(fsdp), cols(tensor, 256)], up_out.at[expert, :, quarter]),
            (down_grad.at[cols(tensor, 256), rows(fsdp)], down_out.at[expert, quarter, :]),
            (fsdp, tensor),
        )

    def remote(step):
        ups, downs, (fsdp, tensor) = expert_copies(step)
        return [
            pltpu.make_async_remote_copy(
                src_ref=pair[0], dst_ref=pair[1], send_sem=sems[0].at[step],
                recv_sem=sems[1].at[step], device_id=place(fsdp, tensor), device_id_type=MESH,
            )
            for pair, sems in ((ups, (up_send, up_recv)), (downs, (down_send, down_recv)))
        ]

    def start_step(step, carry):
        for copy in remote(step):
            copy.start()
        return carry

    lax.fori_loop(1, 32, start_step, 0)
    ups, downs, _ = expert_copies(0)
    own = [
        pltpu.make_async_copy(ups[0], ups[1], out_sem.at[0]),
        pltpu.make_async_copy(downs[0], downs[1], out_sem.at[1]),
    ]
    for copy in own:
        copy.start()

    along = flip(me_f, 4) * (1 - core) + flip(me_f, 2) * core
    across = flip(me_f, 2) * (1 - core) + flip(me_f, 4) * core
    corner = flip(across, 4) * (1 - core) + flip(across, 2) * core
    sent, kept = [along, corner], [me_f, across]
    pair = me_z // 2 * 2
    flight = {}

    def add(target, source, part=None):
        def step(index, carry):
            place_rows = pl.ds(pl.multiple_of(index * 16, 16), 16)
            where = (place_rows,) if part is None else (place_rows, part)
            target[where] = (
                target[where].astype(F32) + source[place_rows, :].astype(F32)
            ).astype(BF)
            return carry

        lax.fori_loop(0, 8, step, 0)

    def by_core(which):
        flight[which] = [
            sender.copy(sums.at[which, :, 1 - core], got.at[which], flip(me_f, 1), me_z)
        ]

    inner = (me_z == 1) | (me_z == 2)

    def landed(which):
        for copy in flight[which]:
            copy.wait_recv()

    def by_first(which):
        landed(which)

        def step(block, carry):
            add(sums.at[which, block, core], got.at[which, block])
            return carry

        lax.fori_loop(0, 4, step, 0)
        flight[which] = [
            sender.copy(
                sums.at[which, sent[index] // 2, core], cut.at[which, index], along, me_z
            )
            for index in range(2)
        ]

    def by_second(which):
        landed(which)
        for index in range(2):
            add(sums.at[which, kept[index] // 2, core], cut.at[which, index])
        flight[which] = [
            sender.copy(sums.at[which, across // 2, core], cut_x.at[which], across, me_z)
        ]

    def by_pair(which):
        landed(which)
        block = sums.at[which, me_f // 2, core]
        add(block, cut_x.at[which])
        flight[which] = [
            sender.copy(
                block.at[:, cols(2 - pair, 512)], cut_z.at[which], me_f, flip(me_z, 1), ~inner
            )
        ]

    def by_middle(which):
        block = sums.at[which, me_f // 2, core]

        @pl.when(inner)
        def _():
            landed(which)
            add(block, cut_z.at[which], cols(2 - pair, 512))

        flight[which] = [
            sender.copy(
                block.at[:, cols(2 - pair, 512)], cut_m.at[which], me_f, 3 - me_z, inner
            )
        ]

    def by_last(which):
        block = sums.at[which, me_f // 2, core]

        @pl.when(inner)
        def _():
            landed(which)
            add(block, cut_m.at[which], cols(pair, 512))

        flight[which] = [
            sender.copy(
                block.at[:, cols(flip(me_z, 1), 256)], cut_w.at[which], me_f, flip(me_z, 1)
            )
        ]

    def by_end(which):
        landed(which)
        block = sums.at[which, me_f // 2, core]
        add(block, cut_w.at[which], cols(me_z, 256))
        copy = pltpu.make_async_copy(
            block.at[:, cols(me_z, 256)], out4.at[which], out_sem.at[2 + which]
        )
        copy.start()
        own.append(copy)

    def loaded(*indices):
        for index in indices:
            loads[index].wait()

    loaded(0, 1, 2, 3, 4, 5, *range(13, 25))
    table[...] = jnp.zeros_like(table)
    router[...] = jnp.zeros_like(router)
    router[0:16, :] = jnp.concatenate(
        [known[6:14, :], jnp.zeros((8, 1024), F32)], axis=0
    ).astype(BF)

    def three(value):
        high = value.astype(BF)
        rest = value - high.astype(F32)
        middle = rest.astype(BF)
        return high, middle, (rest - middle.astype(F32)).astype(BF)

    def finish_rows(index, carry):
        micro, part = index // 2, pl.ds(pl.multiple_of(lax.rem(index, 2) * 128, 128), 128)
        hit = pick[micro, part, :]
        returned = dot_nn(hit, sums[micro, 0:2].reshape(512, 1024)[0:384])
        grad_mid = dot_nn(hit, sums[2 + micro, 0:2].reshape(512, 1024)[0:384])
        value = own_rows[micro, part, :]
        final = grad_q[micro, part, :].astype(F32)
        share, choice = shares[micro, part, :], chosen[micro, part, :].astype(F32)
        gate = jnp.sum(share * choice, axis=-1, keepdims=True)
        grad_heads[micro, part, :] = (value + gate * returned + known[5:6, :]).astype(BF)
        grad_gate = jnp.sum(final * returned, axis=-1, keepdims=True)
        grad_logits = three(share * (choice * grad_gate - gate * grad_gate))
        centered = value - jnp.mean(value, axis=-1, keepdims=True)
        scale = lax.rsqrt(jnp.mean(centered * centered, axis=-1, keepdims=True) + EPSILON)
        plain = centered * scale
        middle = (plain * known[1:2, :] + known[3:4, :]).astype(BF)
        for piece in grad_logits:
            table[6:14, :] += dot_tn(piece, middle)[0:8, :]
            grad_mid = grad_mid + dot_nn(piece, router[...])
        table[1:2, :] += jnp.sum(grad_mid * plain, axis=0, keepdims=True)
        table[3:4, :] += jnp.sum(grad_mid, axis=0, keepdims=True)
        scaled = grad_mid * known[1:2, :]
        inside = (
            scaled
            - jnp.mean(scaled, axis=-1, keepdims=True)
            - plain * jnp.mean(scaled * plain, axis=-1, keepdims=True)
        )
        mixed = final + scale * inside
        own_rows[micro, part, :] = mixed
        proj[micro, part, :] = mixed.astype(BF)
        table[4:5, :] += jnp.sum(mixed, axis=0, keepdims=True)
        table[5:6, :] += jnp.sum(final, axis=0, keepdims=True)
        return carry

    lax.fori_loop(0, 4, finish_rows, 0)
    shown = [
        pltpu.make_async_copy(grad_heads, output, out_sem.at[8]),
        pltpu.make_async_copy(own_rows, mixed_out, out_sem.at[9]),
    ]
    for copy in shown:
        copy.start()
    loaded(7)
    shown[0].wait()

    def head_grads(index, carry):
        part = dot_nn(proj[...].reshape(512, 1024), weights[3, :, tile(index)])
        grad_heads[:, :, tile(index)] = part.astype(BF).reshape(2, 256, 256)
        return carry

    lax.fori_loop(0, 4, head_grads, 0)
    loaded(8, 9, 10, 11)

    def one_tree(micro):
        def two_heads(index, carry):
            query, key, value, grad = (
                part[micro, :, lanes(index)] for part in (queries, keys, values, grad_heads)
            )
            low = lax.broadcasted_iota(jnp.int32, (256, 128), 1) < 64
            low_keys = lax.broadcasted_iota(jnp.int32, (640, 128), 1) < 64
            outs = []
            for which in range(2):
                one = jnp.where(low if which == 0 else ~low, grad, jnp.zeros_like(grad))
                grad_probs = dot_nt(one, value)
                weight = probs[2 * index + which]
                wide = weight.astype(F32)
                scaled = wide * grad_probs
                total = jnp.sum(scaled, axis=-1, keepdims=True)
                grad_scores = (scaled - wide * total).astype(BF)
                outs.append((
                    dot_nn(grad_scores, key), dot_tn(grad_scores, query), dot_tn(weight, grad)
                ))
            grad_q[micro, :, lanes(index)] = (
                jnp.where(low, outs[0][0], outs[1][0]) * 0.125
            ).astype(BF)
            grad_k[micro, :, lanes(index)] = (
                jnp.where(low_keys, outs[0][1], outs[1][1]) * 0.125
            ).astype(BF)
            grad_v[micro, :, lanes(index)] = jnp.where(
                low_keys, outs[0][2], outs[1][2]
            ).astype(BF)
            return carry

        lax.fori_loop(0, 8, two_heads, 0)

    one_tree(0)
    next_probs = pltpu.make_async_copy(probs_hbm.at[1], probs, local_sem.at[9])
    next_probs.start()
    next_probs.wait()
    one_tree(1)
    loaded(12)

    def note(index, grads, plain):
        place_cols = tile(index)
        table[2:3, place_cols] += jnp.sum(grads, axis=0, keepdims=True)
        table[0:1, place_cols] += jnp.sum(grads * plain.astype(F32), axis=0, keepdims=True)

    def far_rows(index, carry):
        place_cols = tile(index)
        keys_part = grad_k[:, 0:384, :].reshape(768, 1024)
        values_part = grad_v[:, 0:384, :].reshape(768, 1024)
        grads = dot_nt(keys_part, weights[1, place_cols, :]) + dot_nt(
            values_part, weights[2, place_cols, :]
        )
        note(index, grads, normed[:, 0:384, place_cols].reshape(768, 256))
        grads = grads.astype(BF).reshape(2, 384, 256)
        for micro in range(2):
            trunk_rows[2 * micro, :, place_cols] = grads[micro, 0:128]
            trunk_rows[2 * micro + 1, :, place_cols] = grads[micro, 128:256]
            halo_rows[micro, :, place_cols] = grads[micro, 256:384]
        return carry

    lax.fori_loop(0, 4, far_rows, 0)

    def trunk_copy(index):
        return pltpu.make_async_remote_copy(
            src_ref=trunk_rows.at[index],
            dst_ref=trunk_got.at[index],
            send_sem=trunk_send.at[index],
            recv_sem=trunk_recv.at[index],
            device_id=place(me_f, lax.rem(me_z + 3, 4)),
            device_id_type=MESH,
        )

    halo_copy = pltpu.make_async_remote_copy(
        src_ref=halo_rows,
        dst_ref=halo_out,
        send_sem=trunk_send.at[4],
        recv_sem=trunk_recv.at[4],
        device_id=place(me_f, lax.rem(me_z + 3, 4)),
        device_id_type=MESH,
    )

    @pl.when(me_z == 3)
    def _():
        for index in range(4):
            trunk_copy(index).start()

    def pass_down(level, index):
        @pl.when(me_z == level)
        def _():
            trunk_copy(index).wait_recv()
            add(trunk_rows.at[index], trunk_got.at[index])
            if level:
                trunk_copy(index).start()

    def weight_sum(which, grads, begin):
        count = 2 * (640 - begin)

        def step(index, carry):
            left = normed[:, begin:640, tile(index)].reshape(count, 256)
            part = dot_tn(left, grads[...].reshape(count, 1024))
            sums[which, index] = part.astype(BF).reshape(2, 128, 1024)
            return carry

        lax.fori_loop(0, 4, step, 0)
        by_core(which)

    loaded(6)

    def out_sum(index, carry):
        left = proj[:, :, tile(index)].reshape(512, 256)
        part = dot_tn(left, heads[...].reshape(512, 1024))
        sums[3, index] = part.astype(BF).reshape(2, 128, 1024)
        return carry

    lax.fori_loop(0, 4, out_sum, 0)
    by_core(3)
    weight_sum(2, grad_v, 0)
    by_first(3)
    weight_sum(1, grad_k, 0)
    by_first(2)
    by_second(3)
    weight_sum(0, grad_q, 384)
    by_first(1)
    by_second(2)
    by_pair(3)

    @pl.when(me_z > 1)
    def _():
        halo_copy.start()

    def near_rows(index, carry):
        place_cols = tile(index)
        keys_part = grad_k[:, 384:640, :].reshape(512, 1024)
        values_part = grad_v[:, 384:640, :].reshape(512, 1024)
        grads = (
            dot_nt(keys_part, weights[1, place_cols, :])
            + dot_nt(values_part, weights[2, place_cols, :])
            + dot_nt(grad_q[...].reshape(512, 1024), weights[0, place_cols, :])
        )
        note(index, grads, normed[:, 384:640, place_cols].reshape(512, 256))
        own_rows[:, :, place_cols] = grads.reshape(2, 256, 256)
        return carry

    shown[1].wait()
    lax.fori_loop(0, 4, near_rows, 0)
    by_first(0)
    pass_down(2, 0)
    by_second(1)
    pass_down(2, 1)
    by_middle(3)
    pass_down(2, 2)
    pass_down(1, 0)
    by_pair(2)
    pass_down(2, 3)
    pass_down(1, 1)
    copy = pltpu.make_async_copy(own_rows, own_out, out_sem.at[6])
    copy.start()
    own.append(copy)

    gain, offset = known[0:1, :], known[2:3, :]
    table[0:1, :] = (table[0:1, :] - offset * table[2:3, :]) / gain
    table[14:15, :] = jnp.sum(grad_q[...].reshape(512, 1024).astype(F32), axis=0, keepdims=True)
    table[15:16, :] = jnp.sum(grad_v[...].reshape(1280, 1024).astype(F32), axis=0, keepdims=True)
    for fsdp in range(8):
        for tensor in range(4):
            target = 4 * fsdp + tensor
            small_mine[target, 0:16, :] = table[:, fsdp * 128 : fsdp * 128 + 128]
            for which in range(2):
                for half in range(2):
                    lane = tensor * 256 + half * 128
                    row = 16 + 2 * which + half
                    small_mine[target, row : row + 1, :] = table[
                        14 + which : 15 + which, lane : lane + 128
                    ]

    def small_copy(step):
        other = lax.rem(mine + step, 32)
        return pltpu.make_async_remote_copy(
            src_ref=small_mine.at[other], dst_ref=small_got.at[mine], send_sem=small_send.at[step],
            recv_sem=small_recv.at[step], device_id=place(other // 4, lax.rem(other, 4)),
            device_id_type=MESH,
        )

    def start_small(step, carry):
        small_copy(step).start()
        return carry

    lax.fori_loop(1, 32, start_small, 0)
    small_got[mine] = small_mine[mine]
    pass_down(1, 2)
    pass_down(0, 0)
    by_second(0)
    pass_down(1, 3)
    pass_down(0, 1)
    by_pair(1)
    by_last(3)
    by_middle(2)
    pass_down(0, 2)
    by_pair(0)
    by_middle(1)
    by_last(2)
    pass_down(0, 3)
    by_middle(0)
    by_last(1)
    by_end(3)
    by_end(2)
    by_last(0)
    by_end(1)
    by_end(0)
    trunk_done = pltpu.make_async_copy(trunk_rows, trunk_out, out_sem.at[7])
    trunk_done.start()
    own.append(trunk_done)

    @pl.when(me_z > 0)
    def _():
        for index in range(4):
            trunk_copy(index).wait_send()

    @pl.when(me_z > 1)
    def _():
        halo_copy.wait_send()

    @pl.when((me_z > 0) & (me_z < 3))
    def _():
        halo_copy.wait_recv()

    def end_small(step, carry):
        copy = small_copy(step)
        copy.wait_send()
        copy.wait_recv()
        return carry

    lax.fori_loop(1, 32, end_small, 0)

    def sum_small(index, total):
        return total + small_got[index]

    small_out[...] = lax.fori_loop(1, 32, sum_small, small_got[0])

    def end_step(step, carry):
        for copy in remote(step):
            copy.wait_send()
            copy.wait_recv()
        return carry

    lax.fori_loop(1, 32, end_step, 0)
    sender.finish()
    for copy in own:
        copy.wait()


def attend_back(*operands):
    dma = pltpu.SemaphoreType.DMA
    specs = any_spec(9)
    specs[3] = pl.BlockSpec(memory_space=pltpu.VMEM)
    tree, keyed = (2, 256, 1024), (2, 640, 1024)
    return pl.pallas_call(
        backward_kernel,
        out_shape=[
            jax.ShapeDtypeStruct((8, 128, 1024), BF),
            jax.ShapeDtypeStruct((8, 1024, 128), BF),
            jax.ShapeDtypeStruct((4, 128, 256), BF),
            jax.ShapeDtypeStruct((24, 128), F32),
            jax.ShapeDtypeStruct(tree, F32),
            jax.ShapeDtypeStruct((4, 128, 1024), BF),
            jax.ShapeDtypeStruct((2, 128, 1024), BF),
            jax.ShapeDtypeStruct(tree, BF),
            jax.ShapeDtypeStruct(tree, F32),
        ],
        in_specs=any_spec(16),
        out_specs=specs,
        scratch_shapes=[
            pltpu.VMEM((4, 1024, 1024), BF),
            pltpu.VMEM((4, 4, 2, 128, 1024), BF),
            pltpu.VMEM(tree, BF),
            pltpu.VMEM(tree, BF),
            pltpu.VMEM(tree, BF),
            pltpu.VMEM(tree, BF),
            pltpu.VMEM(keyed, BF),
            pltpu.VMEM(keyed, BF),
            pltpu.VMEM(keyed, BF),
            pltpu.VMEM((16, 256, 640), BF),
            pltpu.VMEM(tree, BF),
            pltpu.VMEM(keyed, BF),
            pltpu.VMEM(keyed, BF),
            pltpu.VMEM(tree, F32),
            pltpu.VMEM((4, 128, 1024), BF),
            pltpu.VMEM((2, 128, 1024), BF),
            pltpu.VMEM((4, 128, 1024), BF),
            pltpu.VMEM((4, 4, 128, 1024), BF),
            pltpu.VMEM((4, 2, 128, 1024), BF),
            pltpu.VMEM((4, 128, 1024), BF),
            pltpu.VMEM((4, 128, 512), BF),
            pltpu.VMEM((4, 128, 512), BF),
            pltpu.VMEM((4, 128, 256), BF),
            pltpu.VMEM((16, 1024), F32),
            pltpu.VMEM((16, 1024), F32),
            pltpu.VMEM((32, 24, 128), F32),
            pltpu.VMEM((32, 24, 128), F32),
            pltpu.VMEM(operands[3].shape, BF),
            pltpu.VMEM((2, 256, 128), F32),
            pltpu.VMEM((2, 256, 128), BF),
            pltpu.VMEM((128, 1024), BF),
            dma((28,)), dma((28,)), dma((25,)),
            dma((32,)), dma((32,)), dma((32,)), dma((32,)),
            dma((32,)), dma((32,)), dma((5,)), dma((5,)), dma((10,)),
        ],
        compiler_params=pltpu.CompilerParams(
            collective_id=3, has_side_effects=True, vmem_limit_bytes=63 << 20
        ),
        name="attend_back",
    )(*operands)


def fast_body(
    tokens, segment, route, w_qkv, bias_qv, w_o, w_router, w_up, w_down, norm_gains, shifts, cotangent
):
    micro_count, local_rows, width = tokens.shape
    expert_count = w_up.shape[0]
    cap = 3 * local_rows // (2 * expert_count)
    me_z = lax.axis_index("tensor")
    start = me_z * local_rows
    me_f = lax.axis_index("fsdp")
    lane = jnp.arange(128)
    mine = jnp.concatenate(
        [norm_gains, shifts, w_router.T, jnp.zeros((2, 32), BF)], axis=0
    )
    mine = jnp.where(lane // 32 == me_z, jnp.tile(mine, (1, 4)), 0)
    bias_lane = jnp.arange(64)
    bias_mine = jnp.where(bias_lane // 8 == me_f, jnp.tile(bias_qv, (1, 1, 8)), 0).reshape(4, 128)
    small = jnp.concatenate([mine, bias_mine, jnp.zeros((12, 128), BF)], axis=0)
    w4 = jnp.concatenate([w_qkv, w_o.T[None]], axis=0)
    own_index = start + jnp.arange(local_rows)
    key_index = jnp.concatenate([jnp.arange(256), start - 128 + jnp.arange(128), own_index])
    key_part = jnp.arange(640) < 256
    own_segs = lax.dynamic_slice_in_dim(segment, start, local_rows, axis=1)
    halo_segs = lax.dynamic_slice_in_dim(segment, jnp.maximum(start - 128, 0), 128, axis=1)
    key_segs = jnp.concatenate([segment[:, :256], halo_segs, own_segs], axis=1)
    query_seg, key_seg = own_segs[:, :, None], key_segs[:, None, :]
    allowed = (
        (key_seg == 0)
        | (key_seg == query_seg)
        | (query_seg >= 5) & (key_seg == (query_seg - 5) // 2 + 1)
    )
    allowed = allowed & (key_part | (key_index >= 256))[None, None, :]
    allowed = allowed & (key_index[None, :] <= own_index[:, None])[None]
    bias = jnp.where(allowed, 0.0, MASKED)
    own_routes = lax.dynamic_slice_in_dim(route[:, :, 0], start, local_rows, axis=1)
    chosen = (own_routes[:, :, None] == lane).astype(BF)
    (
        full4, params, rows_all, normed_all, queries, keys, values, heads_low, residual, probs_low,
        slots, pick, router_probs, up_own, down_own,
    ) = attend_all(w4, small, tokens, w_up, w_down, bias, chosen, cotangent, cap)
    slots = slots.reshape(2, micro_count, expert_count, cap, width)
    back, up_grad, down_grad = run_experts(slots, up_own, down_own)
    back = back.reshape(2 * micro_count, 3, 128, width)
    (
        up_out, down_out, out4, small_out, grad_own, trunk_sum, halo_sum, output, grad_mixed,
    ) = attend_back(
        up_grad, down_grad, back, pick, residual, cotangent, router_probs, chosen,
        heads_low, queries, keys, values, normed_all, probs_low, full4, params,
    )
    gain = params[0]
    _, plain_in, scale_in = norm_rows(tokens.astype(F32), gain, params[2])

    def flat(value):
        return value.reshape(-1, value.shape[-1])

    trunk_sum = trunk_sum.reshape(2, 256, width).astype(F32)
    grad_normed = grad_own + jnp.where(me_z == 0, trunk_sum, 0.0)
    grad_normed = grad_normed.at[:, 128:].add(jnp.where((me_z > 0) & (me_z < 3), halo_sum.astype(F32), 0.0))
    grad_from_in, _, _ = norm_back(flat(grad_normed), flat(plain_in), flat(scale_in), gain)
    input_grad = grad_mixed + grad_from_in.reshape(grad_mixed.shape)
    bias_out = lax.dynamic_slice_in_dim(
        small_out[16:20].reshape(2, 4, 64), me_f * 8, 8, axis=2
    )
    small_out = lax.dynamic_slice_in_dim(small_out[:14], me_z * 32, 32, axis=1)
    return (
        output,
        input_grad,
        out4[:3].astype(F32),
        bias_out,
        out4[3].T.astype(F32),
        small_out[6:14].T,
        up_out.astype(F32),
        down_out.astype(F32),
        small_out[:2],
        small_out[2:5],
        small_out[5],
    )


def solution(mesh):
    placed = (
        P(None, ("fsdp", "tensor"), None),
        P(None, "fsdp"),
        P(None, "fsdp", None),
        P(None, "fsdp", "tensor"),
        P(None, "tensor", "fsdp"),
        P("tensor", "fsdp"),
        P(("fsdp", "tensor"), None),
        P(None, "fsdp", "tensor"),
        P(None, "tensor", "fsdp"),
        P(None, ("fsdp", "tensor")),
        P(None, ("fsdp", "tensor")),
        P(None, ("fsdp", "tensor"), None),
    )
    return jax.shard_map(
        fast_body if fits(mesh) else plain_body,
        mesh=mesh,
        in_specs=placed,
        out_specs=(
            P(None, ("fsdp", "tensor"), None),
            P(None, ("fsdp", "tensor"), None),
            P(None, "fsdp", "tensor"),
            P(None, "tensor", "fsdp"),
            P("tensor", "fsdp"),
            P(("fsdp", "tensor"), None),
            P(None, "fsdp", "tensor"),
            P(None, "tensor", "fsdp"),
            P(None, ("fsdp", "tensor")),
            P(None, ("fsdp", "tensor")),
            P(("fsdp", "tensor")),
        ),
        check_vma=False,
    )
```

```python
from functools import partial

import jax
import jax.numpy as jnp
from jax import lax
from jax.experimental import pallas as pl
from jax.experimental.pallas import tpu as pltpu
from jax.sharding import PartitionSpec as P

EPSILON = 1e-05
MASKED = -1e30
HIGHEST = lax.Precision.HIGHEST


def norm_rows(row_data, gain_row, shift_row):
    centered = row_data - jnp.mean(row_data, axis=-1, keepdims=True)
    inv_scale = lax.rsqrt(jnp.mean(centered * centered, axis=-1, keepdims=True) + EPSILON)
    normed = centered * inv_scale
    return (normed * gain_row + shift_row, normed, inv_scale)


def norm_back(grad_out, normed, inv_scale, gain_row):
    grad_normed = grad_out * gain_row
    interior = (
        grad_normed
        - jnp.mean(grad_normed, axis=-1, keepdims=True)
        - normed * jnp.mean(grad_normed * normed, axis=-1, keepdims=True)
    )
    return (inv_scale * interior, jnp.sum(grad_out * normed, axis=0), jnp.sum(grad_out, axis=0))


def tree_allowed(query_segs, key_segs, row_start):
    query_seg = query_segs[:, None]
    key_seg = key_segs[None, :]
    related = (
        (key_seg == 0)
        | (key_seg == query_seg)
        | (query_seg >= 5) & (key_seg == (query_seg - 5) // 2 + 1)
    )
    row_index = row_start + jnp.arange(query_segs.shape[0])[:, None]
    col_index = jnp.arange(key_segs.shape[0])[None, :]
    return related & (col_index <= row_index)


def block_scores(queries, key_rows, allowed, factor):
    scaled = (
        jnp.einsum("qhd,khd->hqk", queries, key_rows, preferred_element_type=jnp.float32) * factor
    )
    return jnp.where(allowed[None], scaled, MASKED)


def attend_forward(queries, key_rows, value_rows, segments, block_len):
    tree_len = queries.shape[0]
    factor = queries.shape[-1] ** (-0.5)
    outputs, totals = ([], [])
    for row_start in range(0, tree_len, block_len):
        row_stop = row_start + block_len
        allowed = tree_allowed(segments[row_start:row_stop], segments[:row_stop], row_start)
        scores = block_scores(queries[row_start:row_stop], key_rows[:row_stop], allowed, factor)
        peak_score = jnp.max(scores, axis=-1, keepdims=True)
        exponent = jnp.exp(scores - peak_score)
        denom_sum = jnp.sum(exponent, axis=-1, keepdims=True)
        weights = (exponent / denom_sum).astype(jnp.bfloat16)
        outputs.append(
            jnp.einsum(
                "hqk,khd->qhd", weights, value_rows[:row_stop], preferred_element_type=jnp.float32
            )
        )
        totals.append(peak_score + jnp.log(denom_sum))
    return (jnp.concatenate(outputs, axis=0), jnp.concatenate(totals, axis=1))


def attend_backward(queries, key_rows, value_rows, segments, grad_heads, log_sums, block_len):
    tree_len = queries.shape[0]
    factor = queries.shape[-1] ** (-0.5)
    grad_keys = jnp.zeros(key_rows.shape, jnp.float32)
    grad_values = jnp.zeros(value_rows.shape, jnp.float32)
    grad_queries = []
    for row_start in range(0, tree_len, block_len):
        row_stop = row_start + block_len
        allowed = tree_allowed(segments[row_start:row_stop], segments[:row_stop], row_start)
        scores = block_scores(queries[row_start:row_stop], key_rows[:row_stop], allowed, factor)
        weights = jnp.exp(scores - log_sums[:, row_start:row_stop])
        grad_weights = jnp.einsum(
            "qhd,khd->hqk",
            grad_heads[row_start:row_stop],
            value_rows[:row_stop],
            preferred_element_type=jnp.float32,
        )
        grad_scores = (
            weights * (grad_weights - jnp.sum(weights * grad_weights, axis=-1, keepdims=True))
        ).astype(jnp.bfloat16)
        grad_queries.append(
            jnp.einsum(
                "hqk,khd->qhd", grad_scores, key_rows[:row_stop], preferred_element_type=jnp.float32
            )
            * factor
        )
        grad_keys = grad_keys.at[:row_stop].add(
            jnp.einsum(
                "hqk,qhd->khd",
                grad_scores,
                queries[row_start:row_stop],
                preferred_element_type=jnp.float32,
            )
            * factor
        )
        grad_values = grad_values.at[:row_stop].add(
            jnp.einsum(
                "hqk,qhd->khd",
                weights.astype(jnp.bfloat16),
                grad_heads[row_start:row_stop],
                preferred_element_type=jnp.float32,
            )
        )
    return (jnp.concatenate(grad_queries, axis=0), grad_keys, grad_values)


def gelu_back(hidden, grad_act):
    return jax.vjp(partial(jax.nn.gelu, approximate=True), hidden)[1](grad_act)[0].astype(
        jnp.bfloat16
    )


def plain_body(
    tokens,
    segment,
    route,
    w_qkv,
    bias_qv,
    w_o,
    w_router,
    w_up,
    w_down,
    norm_gains,
    shifts,
    cotangent,
):
    micro_count, local_rows, model_width = tokens.shape
    tree_len = segment.shape[1]
    block_len = min(512, tree_len)
    expert_count = w_up.shape[0]
    tensor_count = lax.axis_size("tensor")
    local_cap = max(2, 3 * local_rows // (2 * expert_count))
    tree_cap = tensor_count * local_cap
    slot_count = expert_count * tree_cap
    position = lax.axis_index("tensor") * local_rows
    gains_all, shifts_all, router_all = (
        lax.all_gather(norm_gains, ("fsdp", "tensor"), axis=1, tiled=True),
        lax.all_gather(shifts, ("fsdp", "tensor"), axis=1, tiled=True),
        lax.all_gather(w_router, ("fsdp", "tensor"), axis=0, tiled=True),
    )
    gains_all = gains_all.astype(jnp.float32)
    shifts_all = shifts_all.astype(jnp.float32)
    router_wide = router_all.astype(jnp.float32)
    qkv_all, bias_all, out_all = (
        lax.all_gather(w_qkv, "fsdp", axis=1, tiled=True),
        lax.all_gather(bias_qv, "fsdp", axis=2, tiled=True),
        lax.all_gather(w_o, "fsdp", axis=1, tiled=True),
    )
    head_width = qkv_all.shape[2]
    head_count = bias_all.shape[1]
    bias_rows = bias_all.reshape(2, head_width).astype(jnp.float32)
    qkv_bias = jnp.stack([bias_rows[0], jnp.zeros_like(bias_rows[0]), bias_rows[1]])
    up_grad = jnp.zeros((expert_count, model_width, w_up.shape[2]), jnp.float32)
    down_grad = jnp.zeros((expert_count, w_down.shape[1], model_width), jnp.float32)
    qkv_grad = jnp.zeros(qkv_all.shape, jnp.float32)
    bias_grad = jnp.zeros((2, head_width), jnp.float32)
    out_grad = jnp.zeros(out_all.shape, jnp.float32)
    router_grad = jnp.zeros(router_wide.shape, jnp.float32)
    gain_grad = jnp.zeros(gains_all.shape, jnp.float32)
    shift_grad = jnp.zeros(shifts_all.shape, jnp.float32)
    expert_ids = jnp.arange(expert_count, dtype=jnp.int32)
    results, input_grads = ([], [])
    for micro_index in range(micro_count):
        segments = segment[micro_index]
        routes_all = route[micro_index, :, 0]
        inputs = tokens[micro_index].astype(jnp.float32)
        normed_in, plain_in, scale_in = norm_rows(inputs, gains_all[0], shifts_all[0])
        normed_tree = lax.all_gather(normed_in.astype(jnp.bfloat16), "tensor", axis=0, tiled=True)
        projected = (
            jnp.einsum("td,jdc->tjc", normed_tree, qkv_all, preferred_element_type=jnp.float32)
            + qkv_bias
        ).astype(jnp.bfloat16)
        queries = projected[:, 0].reshape(tree_len, head_count, -1)
        key_rows = projected[:, 1].reshape(tree_len, head_count, -1)
        value_rows = projected[:, 2].reshape(tree_len, head_count, -1)
        attended, log_sums = attend_forward(queries, key_rows, value_rows, segments, block_len)
        heads_low = attended.reshape(tree_len, head_width).astype(jnp.bfloat16)
        attention_rows = lax.psum_scatter(
            jnp.dot(heads_low, out_all, preferred_element_type=jnp.float32).astype(jnp.bfloat16),
            "tensor",
            scatter_dimension=0,
            tiled=True,
        ).astype(jnp.float32)
        residual = inputs + attention_rows + shifts_all[2]
        normed_mid, plain_mid, scale_mid = norm_rows(residual, gains_all[1], shifts_all[1])
        mid_low = normed_mid.astype(jnp.bfloat16)
        router_probs = jax.nn.softmax(
            jnp.dot(mid_low, router_all, preferred_element_type=jnp.float32), axis=-1
        )
        own_routes = lax.dynamic_slice_in_dim(routes_all, position, local_rows)
        own_choice = own_routes[:, None] == expert_ids[None, :]
        gate_value = jnp.sum(jnp.where(own_choice, router_probs, 0.0), axis=-1)
        grad_final = cotangent[micro_index].astype(jnp.float32)
        grad_returned = (gate_value[:, None] * grad_final).astype(jnp.bfloat16)
        up_all, down_all = (
            lax.all_gather(w_up, "fsdp", axis=1, tiled=True),
            lax.all_gather(w_down, "fsdp", axis=2, tiled=True),
        )
        chosen = routes_all[:, None] == expert_ids[None, :]
        running = jnp.cumsum(chosen.astype(jnp.int32), axis=0)
        slot_index = routes_all * tree_cap + jnp.sum(jnp.where(chosen, running, 0), axis=-1) - 1
        slot_token = (
            jnp.zeros((slot_count,), jnp.int32)
            .at[slot_index]
            .set(jnp.arange(tree_len, dtype=jnp.int32))
        )
        slot_filled = jnp.zeros((slot_count,), jnp.bool_).at[slot_index].set(True)
        mid_tree = lax.all_gather(mid_low, "tensor", axis=0, tiled=True)
        routed = jnp.where(slot_filled[:, None], mid_tree[slot_token], 0).reshape(
            expert_count, tree_cap, model_width
        )
        hidden = jnp.einsum("ecd,edf->ecf", routed, up_all, preferred_element_type=jnp.float32)
        activated = jax.nn.gelu(hidden, approximate=True).astype(jnp.bfloat16)
        expert_rows = jnp.einsum(
            "ecf,efd->ecd", activated, down_all, preferred_element_type=jnp.float32
        ).reshape(slot_count, model_width)
        returned = lax.psum_scatter(
            expert_rows[slot_index].astype(jnp.bfloat16), "tensor", scatter_dimension=0, tiled=True
        ).astype(jnp.float32)
        grad_tree = lax.all_gather(grad_returned, "tensor", axis=0, tiled=True)
        grad_expert = jnp.where(slot_filled[:, None], grad_tree[slot_token], 0).reshape(
            expert_count, tree_cap, model_width
        )
        down_grad = down_grad + jnp.einsum(
            "ecf,ecd->efd", activated, grad_expert, preferred_element_type=jnp.float32
        )
        grad_act = jnp.einsum(
            "ecd,efd->ecf", grad_expert, down_all, preferred_element_type=jnp.float32
        )
        grad_hidden = gelu_back(hidden, grad_act)
        up_grad = up_grad + jnp.einsum(
            "ecd,ecf->edf", routed, grad_hidden, preferred_element_type=jnp.float32
        )
        grad_routed = jnp.einsum(
            "ecf,edf->ecd", grad_hidden, up_all, preferred_element_type=jnp.float32
        ).reshape(slot_count, model_width)
        grad_mid = lax.psum_scatter(
            grad_routed[slot_index].astype(jnp.bfloat16), "tensor", scatter_dimension=0, tiled=True
        ).astype(jnp.float32)
        results.append(
            (residual + gate_value[:, None] * returned + shifts_all[3]).astype(jnp.bfloat16)
        )
        grad_gate = jnp.sum(grad_final * returned, axis=-1)
        grad_logits = router_probs * (
            jnp.where(own_choice, grad_gate[:, None], 0.0) - (gate_value * grad_gate)[:, None]
        )
        router_grad = router_grad + jnp.einsum(
            "td,te->de", mid_low.astype(jnp.float32), grad_logits, precision=HIGHEST
        )
        grad_mid = grad_mid + jnp.einsum("te,de->td", grad_logits, router_wide, precision=HIGHEST)
        grad_from_mid, gain_mid, shift_mid = norm_back(grad_mid, plain_mid, scale_mid, gains_all[1])
        grad_mixed = grad_final + grad_from_mid
        proj_tree = lax.all_gather(grad_mixed.astype(jnp.bfloat16), "tensor", axis=0, tiled=True)
        out_grad = out_grad + jnp.einsum(
            "tc,td->cd", heads_low, proj_tree, preferred_element_type=jnp.float32
        )
        grad_heads = jnp.einsum(
            "td,cd->tc", proj_tree, out_all, preferred_element_type=jnp.float32
        ).astype(jnp.bfloat16)
        grad_queries, grad_keys, grad_values = attend_backward(
            queries,
            key_rows,
            value_rows,
            segments,
            grad_heads.reshape(tree_len, head_count, -1),
            log_sums,
            block_len,
        )
        grad_proj_all = jnp.stack(
            [
                grad_queries.reshape(tree_len, head_width),
                grad_keys.reshape(tree_len, head_width),
                grad_values.reshape(tree_len, head_width),
            ],
            axis=1,
        ).astype(jnp.bfloat16)
        qkv_grad = qkv_grad + jnp.einsum(
            "td,tjc->jdc", normed_tree, grad_proj_all, preferred_element_type=jnp.float32
        )
        bias_grad = bias_grad + jnp.sum(grad_proj_all[:, 0::2].astype(jnp.float32), axis=0)
        grad_normed = lax.psum_scatter(
            jnp.einsum(
                "tjc,jdc->td", grad_proj_all, qkv_all, preferred_element_type=jnp.float32
            ).astype(jnp.bfloat16),
            "tensor",
            scatter_dimension=0,
            tiled=True,
        ).astype(jnp.float32)
        grad_from_in, gain_in, shift_in = norm_back(grad_normed, plain_in, scale_in, gains_all[0])
        input_grads.append(grad_mixed + grad_from_in)
        gain_grad = gain_grad + jnp.stack([gain_in, gain_mid])
        shift_grad = shift_grad + jnp.stack(
            [shift_in, shift_mid, jnp.sum(grad_mixed, axis=0), jnp.sum(grad_final, axis=0)]
        )
    weight_sums = (
        lax.psum_scatter(
            qkv_grad.astype(jnp.bfloat16), "fsdp", scatter_dimension=1, tiled=True
        ).astype(jnp.float32),
        lax.psum_scatter(
            bias_grad.reshape(2, head_count, -1).astype(jnp.bfloat16),
            "fsdp",
            scatter_dimension=2,
            tiled=True,
        ).astype(jnp.float32),
        lax.psum_scatter(
            out_grad.astype(jnp.bfloat16), "fsdp", scatter_dimension=1, tiled=True
        ).astype(jnp.float32),
    )
    up_final, down_final = (
        lax.psum_scatter(
            up_grad.astype(jnp.bfloat16), "fsdp", scatter_dimension=1, tiled=True
        ).astype(jnp.float32),
        lax.psum_scatter(
            down_grad.astype(jnp.bfloat16), "fsdp", scatter_dimension=2, tiled=True
        ).astype(jnp.float32),
    )
    small_sums = (
        lax.psum_scatter(gain_grad, ("fsdp", "tensor"), scatter_dimension=1, tiled=True),
        lax.psum_scatter(shift_grad, ("fsdp", "tensor"), scatter_dimension=1, tiled=True),
        lax.psum_scatter(router_grad, ("fsdp", "tensor"), scatter_dimension=0, tiled=True),
    )
    return (
        jnp.stack(results),
        jnp.stack(input_grads),
        weight_sums[0],
        weight_sums[1],
        weight_sums[2],
        small_sums[2],
        up_final,
        down_final,
        small_sums[0],
        small_sums[1][:3],
        small_sums[1][3],
    )


MESH = pl.DeviceIdType.MESH
BF = jnp.bfloat16
F32 = jnp.float32


def fits(mesh):
    return mesh.shape["fsdp"] == 8 and mesh.shape["tensor"] == 4


def flip(index, bit):
    return index + bit * (1 - 2 * (lax.rem(index // bit, 2)))


def place(fsdp, tensor):
    return {"fsdp": fsdp, "tensor": tensor}


def greet(partners):
    barrier = pltpu.get_barrier_semaphore()
    for fsdp, tensor in partners:
        pl.semaphore_signal(barrier, inc=1, device_id=place(fsdp, tensor), device_id_type=MESH)
    pl.semaphore_wait(barrier, len(partners))


def greet_all(mine):
    barrier = pltpu.get_barrier_semaphore()

    def signal(step, carry):
        other = lax.rem(mine + step, 32)
        pl.semaphore_signal(
            barrier, inc=1, device_id=place(other // 4, lax.rem(other, 4)), device_id_type=MESH
        )
        return carry

    lax.fori_loop(1, 32, signal, 0)
    pl.semaphore_wait(barrier, 31)


class Sender:
    def __init__(self, send_sem, recv_sem):
        self.send_sem, self.recv_sem, self.count = send_sem, recv_sem, 0
        self.open = []

    def copy(self, source, target, fsdp, tensor, when=None):
        made = pltpu.make_async_remote_copy(
            src_ref=source,
            dst_ref=target,
            send_sem=self.send_sem.at[self.count],
            recv_sem=self.recv_sem.at[self.count],
            device_id=place(fsdp, tensor),
            device_id_type=MESH,
        )
        self.count += 1
        if when is None:
            made.start()
        else:
            pl.when(when)(made.start)
        self.open.append((made, when))
        return made

    def finish(self):
        for made, when in self.open:
            if when is None:
                made.wait_send()
            else:
                pl.when(when)(made.wait_send)


def attend_kernel(
    w4, small, tokens, up, down, bias, chosen_hbm, cotangent,
    full4, params, rows_out, normed_out, q_out, k_out, v_out, heads_out, residual_out, probs_out,
    slots_out, pick_out, gates_out, up_own, down_own,
    weights, pieces, table, rows_all, normed, queries, keys, values, heads, residual, probs,
    slots, pick, gates, mask, chosen, grads, router,
    send_sem, recv_sem, local_sem, up_send, up_recv, down_send, down_recv, trunk_send, trunk_recv,
):
    cap = slots.shape[2] // 8
    me_f, me_z = lax.axis_index("fsdp"), lax.axis_index("tensor")
    mine = me_f * 4 + me_z
    core = lax.rem(me_f, 2)
    greet_all(mine)
    sender = Sender(send_sem, recv_sem)

    def rows(fsdp):
        return pl.ds(pl.multiple_of(fsdp * 128, 128), 128)

    def cols(first, width):
        return pl.ds(pl.multiple_of(first * 256, 256), width)

    trunk_rows, halo_rows, own_rows = pl.ds(0, 256), pl.ds(256, 128), pl.ds(384, 256)
    first = [
        sender.copy(w4, weights.at[:, rows(me_f), cols(me_z, 256)], me_f, flip(me_z, 1)),
        sender.copy(small, pieces.at[me_f, me_z], me_f, flip(me_z, 1)),
    ]
    local = [
        pltpu.make_async_copy(w4, weights.at[:, rows(me_f), cols(me_z, 256)], local_sem.at[0]),
        pltpu.make_async_copy(small, pieces.at[me_f, me_z], local_sem.at[1]),
        pltpu.make_async_copy(tokens, rows_all.at[:, own_rows], local_sem.at[2]),
        pltpu.make_async_copy(bias, mask, local_sem.at[3]),
        pltpu.make_async_copy(chosen_hbm, chosen, local_sem.at[16]),
        pltpu.make_async_copy(cotangent, grads, local_sem.at[17]),
    ]
    for copy in local:
        copy.start()

    piece = [(micro, half) for micro in range(2) for half in range(2)]

    def trunk_copy(index, from_tokens):
        micro, half = piece[index]
        part = pl.ds(half * 128, 128)
        return pltpu.make_async_remote_copy(
            src_ref=tokens.at[micro, part] if from_tokens else rows_all.at[micro, part],
            dst_ref=rows_all.at[micro, part],
            send_sem=trunk_send.at[index],
            recv_sem=trunk_recv.at[index],
            device_id=place(me_f, lax.rem(me_z + 1, 4)),
            device_id_type=MESH,
        )

    halo_copy = pltpu.make_async_remote_copy(
        src_ref=tokens.at[:, pl.ds(128, 128)],
        dst_ref=rows_all.at[:, halo_rows],
        send_sem=trunk_send.at[4],
        recv_sem=trunk_recv.at[4],
        device_id=place(me_f, lax.rem(me_z + 1, 4)),
        device_id_type=MESH,
    )

    def expert_copies(step):
        fsdp = (
            lax.rem(me_f // 4 + step // 16, 2) * 4
            + lax.rem(me_f // 2 + step // 8, 2) * 2
            + lax.rem(me_f + step // 4, 2)
        )
        tensor = lax.rem(me_z + step, 4)
        expert = 2 * tensor + fsdp // 4
        quarter = pl.ds(pl.multiple_of(lax.rem(fsdp, 4) * 256, 256), 256)
        return (
            (up.at[expert, :, quarter], up_own.at[rows(me_f), cols(me_z, 256)]),
            (down.at[expert, quarter, :], down_own.at[cols(me_z, 256), rows(me_f)]),
            (fsdp, tensor),
        )

    def remote(step):
        ups, downs, (fsdp, tensor) = expert_copies(step)
        return [
            pltpu.make_async_remote_copy(
                src_ref=pair[0], dst_ref=pair[1], send_sem=sems[0].at[step],
                recv_sem=sems[1].at[step], device_id=place(fsdp, tensor), device_id_type=MESH,
            )
            for pair, sems in ((ups, (up_send, up_recv)), (downs, (down_send, down_recv)))
        ]

    def start_step(step, carry):
        for copy in remote(step):
            copy.start()
        return carry

    @pl.when(me_z == 0)
    def _():
        trunk_copy(0, True).start()

    inner = (me_z == 1) | (me_z == 2)

    @pl.when(inner)
    def _():
        halo_copy.start()

    def pass_up(level, indices):
        @pl.when(me_z == level)
        def _():
            for index in indices:
                trunk_copy(index, False).wait_recv()
                if level < 3:
                    trunk_copy(index, False).start()

    for copy in first:
        copy.wait_recv()
    for copy in local:
        copy.wait()

    pair = me_z // 2 * 2

    def pair_views(number):
        return [
            weights.at[:, rows(me_f), cols(number, 512)],
            pieces.at[me_f, pl.ds(number, 2)],
        ]

    second = [
        sender.copy(view, view, me_f, 3 - me_z, inner) for view in pair_views(pair)
    ]

    @pl.when(inner)
    def _():
        for copy in second:
            copy.wait_recv()

    handed = [
        sender.copy(view, view, me_f, flip(me_z, 1), inner) for view in pair_views(2 - pair)
    ]

    @pl.when(me_z == 0)
    def _():
        for index in range(3):
            trunk_copy(index, True).wait_send()
            trunk_copy(index + 1, True).start()

    @pl.when(~inner)
    def _():
        for copy in handed:
            copy.wait_recv()

    across = flip(me_f, 2) * (1 - core) + flip(me_f, 4) * core
    along = flip(me_f, 4) * (1 - core) + flip(me_f, 2) * core

    def blocks(fsdp_list, target):
        made = []
        for fsdp in fsdp_list:
            view = weights.at[:, rows(fsdp)]
            made.append(sender.copy(view, view, target, me_z))
            made.append(sender.copy(pieces.at[fsdp], pieces.at[fsdp], target, me_z))
        return made

    third = blocks([me_f], across)
    pass_up(1, (0, 1, 2, 3))
    lax.fori_loop(1, 8, start_step, 0)
    pass_up(2, (0, 1))
    for copy in third:
        copy.wait_recv()
    fourth = blocks([me_f, across], along)
    ups, downs, _ = expert_copies(0)
    own = [
        pltpu.make_async_copy(ups[0], ups[1], local_sem.at[4]),
        pltpu.make_async_copy(downs[0], downs[1], local_sem.at[5]),
    ]
    for copy in own:
        copy.start()
    pass_up(2, (2, 3))
    pass_up(3, (0, 1, 2, 3))

    @pl.when(me_z > 1)
    def _():
        halo_copy.wait_recv()

    fill = [
        pltpu.make_async_copy(tokens, rows_all.at[:, trunk_rows], local_sem.at[0]),
        pltpu.make_async_copy(
            tokens.at[:, pl.ds(128, 128)], rows_all.at[:, halo_rows], local_sem.at[1]
        ),
    ]
    for copy, when in zip(fill, (me_z == 0, me_z < 2)):
        pl.when(when)(copy.start)
        pl.when(when)(copy.wait)

    for copy in fourth:
        copy.wait_recv()
    fifth = blocks([core, core + 2, core + 4, core + 6], flip(me_f, 1))
    lax.fori_loop(8, 32, start_step, 0)
    for copy in fifth:
        copy.wait_recv()

    for fsdp in range(8):
        total = pieces[fsdp, 0, 0:16].astype(F32)
        for tensor in range(1, 4):
            total = total + pieces[fsdp, tensor, 0:16].astype(F32)
        table[0:16, fsdp * 128 : fsdp * 128 + 128] = total
    for tensor in range(4):
        total = pieces[0, tensor, 16:32].astype(F32)
        for fsdp in range(1, 8):
            total = total + pieces[fsdp, tensor, 16:32].astype(F32)
        for which in range(2):
            for half in range(2):
                lane = tensor * 256 + half * 128
                table[14 + which : 15 + which, lane : lane + 128] = total[
                    2 * which + half : 2 * which + half + 1, :
                ]
    saves = [
        pltpu.make_async_copy(weights, full4, local_sem.at[6]),
        pltpu.make_async_copy(table, params, local_sem.at[7]),
        pltpu.make_async_copy(rows_all, rows_out, local_sem.at[8]),
    ]
    for copy in saves:
        copy.start()

    def tile(index):
        return pl.ds(pl.multiple_of(index * 256, 256), 256)

    def lanes(index):
        return pl.ds(pl.multiple_of(index * 128, 128), 128)

    def one_tree(micro, carry):
        def norm(index, carry):
            value = rows_all[micro, lanes(index), :].astype(F32)
            centered = value - jnp.mean(value, axis=-1, keepdims=True)
            scale = lax.rsqrt(jnp.mean(centered * centered, axis=-1, keepdims=True) + EPSILON)
            out = centered * scale * table[0:1, :] + table[2:3, :]
            normed[micro, lanes(index), :] = out.astype(BF)
            return carry

        lax.fori_loop(0, 5, norm, 0)

        def project(index, carry):
            place_cols = tile(index)
            key = dot_nn(normed[micro], weights[1, :, place_cols])
            keys[micro, :, place_cols] = key.astype(BF)
            value = dot_nn(normed[micro], weights[2, :, place_cols]) + table[15:16, place_cols]
            values[micro, :, place_cols] = value.astype(BF)
            query = dot_nn(normed[micro, own_rows], weights[0, :, place_cols])
            queries[micro, :, place_cols] = (query + table[14:15, place_cols]).astype(BF)
            return carry

        lax.fori_loop(0, 4, project, 0)

        def two_heads(index, carry):
            query, key, value = (
                part[micro, :, lanes(index)] for part in (queries, keys, values)
            )
            low = lax.broadcasted_iota(jnp.int32, (256, 128), 1) < 64
            outs = []
            for which in range(2):
                one = jnp.where(low if which == 0 else ~low, query, jnp.zeros_like(query))
                scores = dot_nt(one, key) * 0.125 + mask[micro]
                exponent = jnp.exp(scores - jnp.max(scores, axis=-1, keepdims=True))
                total = jnp.sum(exponent, axis=-1, keepdims=True)
                weight = (exponent * (1.0 / total)).astype(BF)
                probs[micro, 2 * index + which] = weight
                outs.append(dot_nn(weight, value))
            heads[micro, :, lanes(index)] = jnp.where(low, outs[0], outs[1]).astype(BF)
            return carry

        lax.fori_loop(0, 8, two_heads, 0)

        def mix(index, carry):
            place_cols = tile(index)
            out = dot_nt(heads[micro], weights[3, place_cols, :])
            residual[micro, :, place_cols] = (
                rows_all[micro, own_rows, place_cols].astype(F32) + out + table[4:5, place_cols]
            )
            return carry

        lax.fori_loop(0, 4, mix, 0)

        value = residual[micro]
        centered = value - jnp.mean(value, axis=-1, keepdims=True)
        scale = lax.rsqrt(jnp.mean(centered * centered, axis=-1, keepdims=True) + EPSILON)
        middle = (centered * scale * table[1:2, :] + table[3:4, :]).astype(BF)
        lane = lax.broadcasted_iota(jnp.int32, (256, 128), 1)
        logits = jnp.where(lane < 8, dot_nt(middle, router[...]), MASKED)
        exponent = jnp.exp(logits - jnp.max(logits, axis=-1, keepdims=True))
        share = exponent / jnp.sum(exponent, axis=-1, keepdims=True)
        gates[micro] = share
        choice = chosen[micro]
        wide = choice.astype(F32)
        gate = jnp.sum(share * wide, axis=-1, keepdims=True)
        earlier = (
            lax.broadcasted_iota(jnp.int32, (256, 256), 1)
            < lax.broadcasted_iota(jnp.int32, (256, 256), 0)
        ).astype(F32).astype(BF)
        rank = dot_nn(earlier, choice) + (lane * cap).astype(F32)
        slot = jnp.sum(wide * rank, axis=-1, keepdims=True)
        column = lax.broadcasted_iota(jnp.int32, (256, 8 * cap), 1).astype(F32)
        hit = (column == slot).astype(F32).astype(BF)
        pick[micro] = hit
        slots[0, micro] = dot_tn(hit, middle).astype(BF)
        returned = (gate * grads[micro].astype(F32)).astype(BF)
        slots[1, micro] = dot_tn(hit, returned).astype(BF)
        return carry

    router[...] = jnp.zeros_like(router)
    router[0:16, :] = jnp.concatenate(
        [table[6:14, :], jnp.zeros((8, 1024), F32)], axis=0
    ).astype(BF)
    lax.fori_loop(0, 2, one_tree, 0)
    late = [
        (normed, normed_out), (queries, q_out), (keys, k_out), (values, v_out),
        (heads, heads_out), (residual, residual_out), (probs, probs_out), (slots, slots_out),
        (pick, pick_out), (gates, gates_out),
    ]
    for index, (source, target) in enumerate(late):
        copy = pltpu.make_async_copy(source, target, local_sem.at[(9 + index) if index < 7 else (11 + index)])
        copy.start()
        saves.append(copy)

    @pl.when((me_z > 0) & (me_z < 3))
    def _():
        for index in range(4):
            trunk_copy(index, False).wait_send()

    @pl.when(me_z == 0)
    def _():
        trunk_copy(3, True).wait_send()

    @pl.when(inner)
    def _():
        halo_copy.wait_send()

    for copy in own:
        copy.wait()

    def end_step(step, carry):
        for copy in remote(step):
            copy.wait_send()
            copy.wait_recv()
        return carry

    lax.fori_loop(1, 32, end_step, 0)
    sender.finish()
    for copy in saves:
        copy.wait()


def any_spec(count):
    return [pl.BlockSpec(memory_space=pl.ANY)] * count


def attend_all(w4, small, tokens, up, down, bias, chosen, cotangent, cap):
    kept = [
        ((4, 1024, 1024), BF), ((16, 1024), F32), ((2, 640, 1024), BF), ((2, 640, 1024), BF),
        ((2, 256, 1024), BF), ((2, 640, 1024), BF), ((2, 640, 1024), BF), ((2, 256, 1024), BF),
        ((2, 256, 1024), F32), ((2, 16, 256, 640), BF), ((2, 2, 8 * cap, 1024), BF),
        ((2, 256, 8 * cap), BF), ((2, 256, 128), F32),
    ]
    dma = pltpu.SemaphoreType.DMA
    return pl.pallas_call(
        attend_kernel,
        out_shape=[
            *(jax.ShapeDtypeStruct(shape, dtype) for shape, dtype in kept),
            jax.ShapeDtypeStruct((1024, 1024), BF),
            jax.ShapeDtypeStruct((1024, 1024), BF),
        ],
        in_specs=any_spec(8),
        out_specs=any_spec(15),
        scratch_shapes=[
            pltpu.VMEM(*kept[0]),
            pltpu.VMEM((8, 4, 32, 128), BF),
            *(pltpu.VMEM(shape, dtype) for shape, dtype in kept[1:]),
            pltpu.VMEM((2, 256, 640), F32),
            pltpu.VMEM((2, 256, 128), BF),
            pltpu.VMEM((2, 256, 1024), BF),
            pltpu.VMEM((128, 1024), BF),
            dma((20,)), dma((20,)), dma((21,)),
            dma((32,)), dma((32,)), dma((32,)), dma((32,)), dma((5,)), dma((5,)),
        ],
        compiler_params=pltpu.CompilerParams(
            collective_id=0, has_side_effects=True, vmem_limit_bytes=60 << 20
        ),
        name="attend",
    )(w4, small, tokens, up, down, bias, chosen, cotangent)


def gelu_pair(hidden):
    scale = (2.0 / jnp.pi) ** 0.5
    square = hidden * hidden
    bend = jnp.tanh(scale * hidden * (1.0 + 0.044715 * square))
    half = 0.5 * (1.0 + bend)
    slope = half + 0.5 * hidden * (1.0 - bend * bend) * scale * (1.0 + 0.134145 * square)
    return hidden * half, slope


def dot_nn(left, right):
    return lax.dot_general(left, right, (((1,), (0,)), ((), ())), preferred_element_type=F32)


def dot_nt(left, right):
    return lax.dot_general(left, right, (((1,), (1,)), ((), ())), preferred_element_type=F32)


def dot_tn(left, right):
    return lax.dot_general(left, right, (((0,), (0,)), ((), ())), preferred_element_type=F32)


def expert_kernel(
    slots, up_hbm, down_hbm, returned, up_grad, down_grad,
    arrived, parts, got, got_x, up, down, up_sum, down_sum, act, slope,
    send_sem, recv_sem, local_sem,
):
    cap = slots.shape[3]
    group = 8 * cap
    rows = 2 * group
    me_f, me_z = lax.axis_index("fsdp"), lax.axis_index("tensor")
    me_y, me_x, core = me_f // 4, lax.rem(me_f // 2, 2), lax.rem(me_f, 2)
    far_x = 1 - me_x
    x_mate, core_mate = flip(me_f, 2), flip(me_f, 1)
    far = []
    for step in range(1, 8):
        far.append(
            (lax.rem(me_y + step // 4, 2) * 4 + lax.rem(me_f, 4), lax.rem(me_z + step, 4))
        )
    greet([(x_mate, me_z), (core_mate, me_z)] + far)
    sender = Sender(send_sem, recv_sem)
    load = [
        pltpu.make_async_copy(up_hbm, up, local_sem.at[0]),
        pltpu.make_async_copy(down_hbm, down, local_sem.at[1]),
    ]

    def origin_rows(fsdp, tensor):
        first = (fsdp // 4 * 4 + tensor) * cap
        return pl.ds(pl.multiple_of(first, cap), cap)

    chunks = [(kind, micro) for kind in range(2) for micro in range(2)]
    half_rows = 4 * cap
    incoming, own_in = {}, {}

    def half_of(half):
        first = (me_y + half - 2 * me_y * half) * half_rows
        return pl.ds(pl.multiple_of(first, half_rows), half_rows)

    def send_half(number):
        index, half = number // 2, number % 2
        kind, micro = chunks[index]
        target = arrived.at[kind, micro, me_x, core, origin_rows(me_f, me_z)]
        incoming[number] = [
            sender.copy(slots.at[kind, micro, 2 * tensor + fsdp // 4], target, fsdp, tensor)
            for fsdp, tensor in (far[:3] if half == 0 else far[3:])
        ]
        if half == 0:
            own = pltpu.make_async_copy(
                slots.at[kind, micro, 2 * me_z + me_y], target, local_sem.at[2 + index]
            )
            own.start()
            own_in[index] = own

    send_half(0)
    send_half(1)
    for copy in load:
        copy.start()

    own_across = [
        sender.copy(
            slots.at[kind, micro, 2 * me_z + me_y],
            arrived.at[kind, micro, me_x, core, origin_rows(me_f, me_z)],
            x_mate, me_z,
        )
        for kind, micro in chunks
    ]

    def same_place(view, fsdp):
        return sender.copy(view, view, fsdp, me_z)

    across, beside, onward = {}, {}, {}

    def landed(index):
        kind, micro = chunks[index]
        across[index], beside[index] = [], []
        for half in range(2):
            for copy in incoming[2 * index + half]:
                copy.wait_recv()
            if half == 0:
                own_in[index].wait()
            if 2 * index + half + 2 < 8:
                send_half(2 * index + half + 2)
            view = arrived.at[kind, micro, me_x, core, half_of(half)]
            if half == 0:
                lane = arrived.at[kind, micro, me_x, core]
                moved = [
                    same_place(lane.at[origin_rows(me_f, lax.rem(me_z + step, 4))], x_mate)
                    for step in range(1, 4)
                ]
                across[index].append(moved + [own_across[index]])
            else:
                across[index].append([same_place(view, x_mate)])
            beside[index].append(same_place(view, core_mate))

    def forwarded(index):
        kind, micro = chunks[index]
        onward[index] = []
        for half in range(2):
            ready(across[index][half])
            onward[index].append(
                same_place(arrived.at[kind, micro, far_x, core, half_of(half)], core_mate)
            )

    def ready(copies):
        for copy in copies:
            copy.wait_recv()

    def tile(index):
        return pl.ds(pl.multiple_of(index * 256, 256), 256)

    def forward(micro, side):
        data = arrived.at[0, micro, side]

        def first(index, carry):
            hidden = dot_nn(data[...].reshape(rows, 1024), up[:, tile(index)])
            value, slope_value = gelu_pair(hidden)
            act[micro, side, :, tile(index)] = value.astype(BF)
            slope[micro, side, :, tile(index)] = slope_value.astype(BF)
            return carry

        lax.fori_loop(0, 4, first, 0)

        def second(index, carry):
            out = dot_nn(act[micro, side], down[:, tile(index)])
            parts[0, micro, side, :, :, tile(index)] = out.astype(BF).reshape(2, group, 256)
            return carry

        lax.fori_loop(0, 4, second, 0)

    def backward(micro, side, begin):
        data = arrived.at[0, micro, side]
        grads = arrived.at[1, micro, side]

        def first(index, carry):
            grad = grads[...].reshape(rows, 1024)
            grad_act = dot_nt(grad, down[tile(index), :])
            grad_hidden = (
                grad_act * slope[micro, side, :, tile(index)].astype(F32)
            ).astype(BF)
            slope[micro, side, :, tile(index)] = grad_hidden
            down_part = dot_tn(act[micro, side, :, tile(index)], grad)
            up_part = dot_tn(data[...].reshape(rows, 1024), grad_hidden)
            if begin:
                down_sum[tile(index), :] = down_part
                up_sum[:, tile(index)] = up_part
            else:
                down_sum[tile(index), :] += down_part
                up_sum[:, tile(index)] += up_part
            return carry

        lax.fori_loop(0, 4, first, 0)

        def second(index, carry):
            out = dot_nt(slope[micro, side], up[tile(index), :])
            parts[1, micro, side, :, :, tile(index)] = out.astype(BF).reshape(2, group, 256)
            return carry

        lax.fori_loop(0, 4, second, 0)

    def result(kind, micro):
        return parts.at[kind, micro]

    core_back, x_back, home = {}, {}, {}

    def back_core(index):
        kind, micro = chunks[index]
        core_back[index] = sender.copy(
            result(kind, micro).at[:, 1 - core], got.at[kind, micro], core_mate, me_z
        )

    def add_rows(target, source, count=8):
        def step(row, carry):
            part = pl.ds(pl.multiple_of(row * cap, cap), cap)
            target[part] = (target[part].astype(F32) + source[part].astype(F32)).astype(BF)
            return carry

        lax.fori_loop(0, count, step, 0)

    def back_x(index):
        kind, micro = chunks[index]
        core_back[index].wait_recv()
        mine = result(kind, micro)
        add_rows(mine.at[far_x, core], got.at[kind, micro, far_x])
        x_back[index] = [
            sender.copy(
                mine.at[far_x, core, half_of(half)], got_x.at[kind, micro, half_of(half)],
                x_mate, me_z,
            )
            for half in range(2)
        ]
        add_rows(mine.at[me_x, core], got.at[kind, micro, me_x])

    def back_home(index):
        kind, micro = chunks[index]
        mine = result(kind, micro).at[me_x, core]
        target = returned.at[kind, micro, 2 * me_z + me_y]
        home[index] = []
        for half in range(2):
            x_back[index][half].wait_recv()
            part = half_of(half)
            add_rows(mine.at[part], got_x.at[kind, micro, part], 4)
            for fsdp, tensor in far[:3] if half == 0 else far[3:]:
                home[index].append(
                    sender.copy(mine.at[origin_rows(fsdp, tensor)], target, fsdp, tensor)
                )
            if half == 0:
                own = pltpu.make_async_copy(
                    mine.at[origin_rows(me_f, me_z)], target, local_sem.at[2 + index]
                )
                own.start()
                own_in[index] = own

    landed(0)
    for copy in load:
        copy.wait()
    ready(beside[0])
    forward(0, me_x)
    landed(1)
    forwarded(0)
    ready(beside[1])
    forward(1, me_x)
    ready(onward[0])
    forward(0, far_x)
    back_core(0)
    landed(2)
    forwarded(1)
    ready(beside[2])
    backward(0, me_x, True)
    ready(onward[1])
    landed(3)
    back_x(0)
    forward(1, far_x)
    back_core(1)
    ready(beside[3])
    backward(1, me_x, False)
    forwarded(2)
    back_x(1)
    ready(onward[2])
    backward(0, far_x, False)
    back_core(2)
    back_home(0)
    forwarded(3)
    back_x(2)
    ready(onward[3])
    backward(1, far_x, False)
    back_core(3)
    back_x(3)
    back_home(1)

    def narrow(index, carry):
        part = pl.ds(pl.multiple_of(index * 64, 64), 64)
        up[part, :] = up_sum[part, :].astype(BF)
        down[part, :] = down_sum[part, :].astype(BF)
        return carry

    lax.fori_loop(0, 16, narrow, 0)
    store = [
        pltpu.make_async_copy(up, up_grad, local_sem.at[0]),
        pltpu.make_async_copy(down, down_grad, local_sem.at[1]),
    ]
    for copy in store:
        copy.start()
    back_home(2)
    back_home(3)
    for index in range(4):
        for copy in home[index]:
            copy.wait_recv()
        own_in[index].wait()
    for copy in store:
        copy.wait()
    sender.finish()


def run_experts(slots, up_own, down_own):
    cap = slots.shape[3]
    group = 8 * cap
    dma = pltpu.SemaphoreType.DMA
    return pl.pallas_call(
        expert_kernel,
        out_shape=[
            jax.ShapeDtypeStruct(slots.shape, BF),
            jax.ShapeDtypeStruct((1024, 1024), BF),
            jax.ShapeDtypeStruct((1024, 1024), BF),
        ],
        in_specs=any_spec(3),
        out_specs=any_spec(3),
        scratch_shapes=[
            pltpu.VMEM((2, 2, 2, 2, group, 1024), BF),
            pltpu.VMEM((2, 2, 2, 2, group, 1024), BF),
            pltpu.VMEM((2, 2, 2, group, 1024), BF),
            pltpu.VMEM((2, 2, group, 1024), BF),
            pltpu.VMEM((1024, 1024), BF),
            pltpu.VMEM((1024, 1024), BF),
            pltpu.VMEM((1024, 1024), F32),
            pltpu.VMEM((1024, 1024), F32),
            pltpu.VMEM((2, 2, 2 * group, 1024), BF),
            pltpu.VMEM((2, 2, 2 * group, 1024), BF),
            dma((104,)), dma((104,)), dma((6,)),
        ],
        compiler_params=pltpu.CompilerParams(
            collective_id=1, has_side_effects=True, vmem_limit_bytes=63 << 20
        ),
        cost_estimate=pl.CostEstimate(
            flops=12 * 4 * group * 2 * 1024 * 1024, bytes_accessed=20 << 20, transcendentals=0
        ),
        name="experts",
    )(slots, up_own, down_own)


def backward_kernel(
    up_grad, down_grad, back_hbm, pick_hbm, residual_hbm, cotangent, share_hbm, chosen_hbm,
    heads_hbm, q_hbm, k_hbm, v_hbm, normed_hbm, probs_hbm, full4, params,
    up_out, down_out, out4, small_out, own_out, trunk_out, halo_out, output, mixed_out,
    weights, sums, proj, heads, grad_heads, queries, keys, values, normed, probs,
    grad_q, grad_k, grad_v, own_rows, trunk_rows, halo_rows, trunk_got,
    got, cut, cut_x, cut_z, cut_m, cut_w, table, known, small_mine, small_got,
    pick, shares, chosen, router,
    send_sem, recv_sem, local_sem, up_send, up_recv, down_send, down_recv,
    small_send, small_recv, trunk_send, trunk_recv, out_sem,
):
    me_f, me_z = lax.axis_index("fsdp"), lax.axis_index("tensor")
    mine = me_f * 4 + me_z
    core = lax.rem(me_f, 2)
    me_y = me_f // 4
    greet_all(mine)
    sender = Sender(send_sem, recv_sem)

    def rows(fsdp):
        return pl.ds(pl.multiple_of(fsdp * 128, 128), 128)

    def cols(first, width):
        return pl.ds(pl.multiple_of(first * 256, 256), width)

    def tile(index):
        return pl.ds(pl.multiple_of(index * 256, 256), 256)

    def lanes(index):
        return pl.ds(pl.multiple_of(index * 128, 128), 128)

    loads = [
        pltpu.make_async_copy(source, target, local_sem.at[index])
        for index, (source, target) in enumerate([
            (pick_hbm, pick), (residual_hbm, own_rows), (cotangent, grad_q),
            (share_hbm, shares), (chosen_hbm, chosen), (params, known), (heads_hbm, heads),
            (full4, weights), (v_hbm, values), (probs_hbm.at[0], probs), (k_hbm, keys),
            (q_hbm, queries), (normed_hbm, normed),
        ])
    ]
    for index in range(4):
        for block in range(3):
            loads.append(
                pltpu.make_async_copy(
                    back_hbm.at[index, block], sums.at[index, block // 2, block % 2],
                    local_sem.at[13 + 3 * index + block],
                )
            )
    for copy in loads:
        copy.start()

    def expert_copies(step):
        other = lax.rem(mine + step, 32)
        fsdp, tensor = other // 4, lax.rem(other, 4)
        expert = 2 * me_z + me_y
        quarter = pl.ds(pl.multiple_of(lax.rem(me_f, 4) * 256, 256), 256)
        return (
            (up_grad.at[rows(fsdp), cols(tensor, 256)], up_out.at[expert, :, quarter]),
            (down_grad.at[cols(tensor, 256), rows(fsdp)], down_out.at[expert, quarter, :]),
            (fsdp, tensor),
        )

    def remote(step):
        ups, downs, (fsdp, tensor) = expert_copies(step)
        return [
            pltpu.make_async_remote_copy(
                src_ref=pair[0], dst_ref=pair[1], send_sem=sems[0].at[step],
                recv_sem=sems[1].at[step], device_id=place(fsdp, tensor), device_id_type=MESH,
            )
            for pair, sems in ((ups, (up_send, up_recv)), (downs, (down_send, down_recv)))
        ]

    def start_step(step, carry):
        for copy in remote(step):
            copy.start()
        return carry

    lax.fori_loop(1, 32, start_step, 0)
    ups, downs, _ = expert_copies(0)
    own = [
        pltpu.make_async_copy(ups[0], ups[1], out_sem.at[0]),
        pltpu.make_async_copy(downs[0], downs[1], out_sem.at[1]),
    ]
    for copy in own:
        copy.start()

    along = flip(me_f, 4) * (1 - core) + flip(me_f, 2) * core
    across = flip(me_f, 2) * (1 - core) + flip(me_f, 4) * core
    corner = flip(across, 4) * (1 - core) + flip(across, 2) * core
    sent, kept = [along, corner], [me_f, across]
    pair = me_z // 2 * 2
    flight = {}

    def add(target, source, part=None):
        def step(index, carry):
            place_rows = pl.ds(pl.multiple_of(index * 16, 16), 16)
            where = (place_rows,) if part is None else (place_rows, part)
            target[where] = (
                target[where].astype(F32) + source[place_rows, :].astype(F32)
            ).astype(BF)
            return carry

        lax.fori_loop(0, 8, step, 0)

    def by_core(which):
        flight[which] = [
            sender.copy(sums.at[which, :, 1 - core], got.at[which], flip(me_f, 1), me_z)
        ]

    inner = (me_z == 1) | (me_z == 2)

    def landed(which):
        for copy in flight[which]:
            copy.wait_recv()

    def by_first(which):
        landed(which)

        def step(block, carry):
            add(sums.at[which, block, core], got.at[which, block])
            return carry

        lax.fori_loop(0, 4, step, 0)
        flight[which] = [
            sender.copy(
                sums.at[which, sent[index] // 2, core], cut.at[which, index], along, me_z
            )
            for index in range(2)
        ]

    def by_second(which):
        landed(which)
        for index in range(2):
            add(sums.at[which, kept[index] // 2, core], cut.at[which, index])
        flight[which] = [
            sender.copy(sums.at[which, across // 2, core], cut_x.at[which], across, me_z)
        ]

    def by_pair(which):
        landed(which)
        block = sums.at[which, me_f // 2, core]
        add(block, cut_x.at[which])
        flight[which] = [
            sender.copy(
                block.at[:, cols(2 - pair, 512)], cut_z.at[which], me_f, flip(me_z, 1), ~inner
            )
        ]

    def by_middle(which):
        block = sums.at[which, me_f // 2, core]

        @pl.when(inner)
        def _():
            landed(which)
            add(block, cut_z.at[which], cols(2 - pair, 512))

        flight[which] = [
            sender.copy(
                block.at[:, cols(2 - pair, 512)], cut_m.at[which], me_f, 3 - me_z, inner
            )
        ]

    def by_last(which):
        block = sums.at[which, me_f // 2, core]

        @pl.when(inner)
        def _():
            landed(which)
            add(block, cut_m.at[which], cols(pair, 512))

        flight[which] = [
            sender.copy(
                block.at[:, cols(flip(me_z, 1), 256)], cut_w.at[which], me_f, flip(me_z, 1)
            )
        ]

    def by_end(which):
        landed(which)
        block = sums.at[which, me_f // 2, core]
        add(block, cut_w.at[which], cols(me_z, 256))
        copy = pltpu.make_async_copy(
            block.at[:, cols(me_z, 256)], out4.at[which], out_sem.at[2 + which]
        )
        copy.start()
        own.append(copy)

    def loaded(*indices):
        for index in indices:
            loads[index].wait()

    loaded(0, 1, 2, 3, 4, 5, *range(13, 25))
    table[...] = jnp.zeros_like(table)
    router[...] = jnp.zeros_like(router)
    router[0:16, :] = jnp.concatenate(
        [known[6:14, :], jnp.zeros((8, 1024), F32)], axis=0
    ).astype(BF)

    def three(value):
        high = value.astype(BF)
        rest = value - high.astype(F32)
        middle = rest.astype(BF)
        return high, middle, (rest - middle.astype(F32)).astype(BF)

    def finish_rows(index, carry):
        micro, part = index // 2, pl.ds(pl.multiple_of(lax.rem(index, 2) * 128, 128), 128)
        hit = pick[micro, part, :]
        returned = dot_nn(hit, sums[micro, 0:2].reshape(512, 1024)[0:384])
        grad_mid = dot_nn(hit, sums[2 + micro, 0:2].reshape(512, 1024)[0:384])
        value = own_rows[micro, part, :]
        final = grad_q[micro, part, :].astype(F32)
        share, choice = shares[micro, part, :], chosen[micro, part, :].astype(F32)
        gate = jnp.sum(share * choice, axis=-1, keepdims=True)
        grad_heads[micro, part, :] = (value + gate * returned + known[5:6, :]).astype(BF)
        grad_gate = jnp.sum(final * returned, axis=-1, keepdims=True)
        grad_logits = three(share * (choice * grad_gate - gate * grad_gate))
        centered = value - jnp.mean(value, axis=-1, keepdims=True)
        scale = lax.rsqrt(jnp.mean(centered * centered, axis=-1, keepdims=True) + EPSILON)
        plain = centered * scale
        middle = (plain * known[1:2, :] + known[3:4, :]).astype(BF)
        for piece in grad_logits:
            table[6:14, :] += dot_tn(piece, middle)[0:8, :]
            grad_mid = grad_mid + dot_nn(piece, router[...])
        table[1:2, :] += jnp.sum(grad_mid * plain, axis=0, keepdims=True)
        table[3:4, :] += jnp.sum(grad_mid, axis=0, keepdims=True)
        scaled = grad_mid * known[1:2, :]
        inside = (
            scaled
            - jnp.mean(scaled, axis=-1, keepdims=True)
            - plain * jnp.mean(scaled * plain, axis=-1, keepdims=True)
        )
        mixed = final + scale * inside
        own_rows[micro, part, :] = mixed
        proj[micro, part, :] = mixed.astype(BF)
        table[4:5, :] += jnp.sum(mixed, axis=0, keepdims=True)
        table[5:6, :] += jnp.sum(final, axis=0, keepdims=True)
        return carry

    lax.fori_loop(0, 4, finish_rows, 0)
    shown = [
        pltpu.make_async_copy(grad_heads, output, out_sem.at[8]),
        pltpu.make_async_copy(own_rows, mixed_out, out_sem.at[9]),
    ]
    for copy in shown:
        copy.start()
    loaded(7)
    shown[0].wait()

    def head_grads(index, carry):
        part = dot_nn(proj[...].reshape(512, 1024), weights[3, :, tile(index)])
        grad_heads[:, :, tile(index)] = part.astype(BF).reshape(2, 256, 256)
        return carry

    lax.fori_loop(0, 4, head_grads, 0)
    loaded(8, 9, 10, 11)

    def one_tree(micro):
        def two_heads(index, carry):
            query, key, value, grad = (
                part[micro, :, lanes(index)] for part in (queries, keys, values, grad_heads)
            )
            low = lax.broadcasted_iota(jnp.int32, (256, 128), 1) < 64
            low_keys = lax.broadcasted_iota(jnp.int32, (640, 128), 1) < 64
            outs = []
            for which in range(2):
                one = jnp.where(low if which == 0 else ~low, grad, jnp.zeros_like(grad))
                grad_probs = dot_nt(one, value)
                weight = probs[2 * index + which]
                wide = weight.astype(F32)
                scaled = wide * grad_probs
                total = jnp.sum(scaled, axis=-1, keepdims=True)
                grad_scores = (scaled - wide * total).astype(BF)
                outs.append((
                    dot_nn(grad_scores, key), dot_tn(grad_scores, query), dot_tn(weight, grad)
                ))
            grad_q[micro, :, lanes(index)] = (
                jnp.where(low, outs[0][0], outs[1][0]) * 0.125
            ).astype(BF)
            grad_k[micro, :, lanes(index)] = (
                jnp.where(low_keys, outs[0][1], outs[1][1]) * 0.125
            ).astype(BF)
            grad_v[micro, :, lanes(index)] = jnp.where(
                low_keys, outs[0][2], outs[1][2]
            ).astype(BF)
            return carry

        lax.fori_loop(0, 8, two_heads, 0)

    one_tree(0)
    next_probs = pltpu.make_async_copy(probs_hbm.at[1], probs, local_sem.at[9])
    next_probs.start()
    next_probs.wait()
    one_tree(1)
    loaded(12)

    def note(index, grads, plain):
        place_cols = tile(index)
        table[2:3, place_cols] += jnp.sum(grads, axis=0, keepdims=True)
        table[0:1, place_cols] += jnp.sum(grads * plain.astype(F32), axis=0, keepdims=True)

    def far_rows(index, carry):
        place_cols = tile(index)
        keys_part = grad_k[:, 0:384, :].reshape(768, 1024)
        values_part = grad_v[:, 0:384, :].reshape(768, 1024)
        grads = dot_nt(keys_part, weights[1, place_cols, :]) + dot_nt(
            values_part, weights[2, place_cols, :]
        )
        note(index, grads, normed[:, 0:384, place_cols].reshape(768, 256))
        grads = grads.astype(BF).reshape(2, 384, 256)
        for micro in range(2):
            trunk_rows[2 * micro, :, place_cols] = grads[micro, 0:128]
            trunk_rows[2 * micro + 1, :, place_cols] = grads[micro, 128:256]
            halo_rows[micro, :, place_cols] = grads[micro, 256:384]
        return carry

    lax.fori_loop(0, 4, far_rows, 0)

    def trunk_copy(index):
        return pltpu.make_async_remote_copy(
            src_ref=trunk_rows.at[index],
            dst_ref=trunk_got.at[index],
            send_sem=trunk_send.at[index],
            recv_sem=trunk_recv.at[index],
            device_id=place(me_f, lax.rem(me_z + 3, 4)),
            device_id_type=MESH,
        )

    halo_copy = pltpu.make_async_remote_copy(
        src_ref=halo_rows,
        dst_ref=halo_out,
        send_sem=trunk_send.at[4],
        recv_sem=trunk_recv.at[4],
        device_id=place(me_f, lax.rem(me_z + 3, 4)),
        device_id_type=MESH,
    )

    @pl.when(me_z == 3)
    def _():
        for index in range(4):
            trunk_copy(index).start()

    def pass_down(level, index):
        @pl.when(me_z == level)
        def _():
            trunk_copy(index).wait_recv()
            add(trunk_rows.at[index], trunk_got.at[index])
            if level:
                trunk_copy(index).start()

    def weight_sum(which, grads, begin):
        count = 2 * (640 - begin)

        def step(index, carry):
            left = normed[:, begin:640, tile(index)].reshape(count, 256)
            part = dot_tn(left, grads[...].reshape(count, 1024))
            sums[which, index] = part.astype(BF).reshape(2, 128, 1024)
            return carry

        lax.fori_loop(0, 4, step, 0)
        by_core(which)

    loaded(6)

    def out_sum(index, carry):
        left = proj[:, :, tile(index)].reshape(512, 256)
        part = dot_tn(left, heads[...].reshape(512, 1024))
        sums[3, index] = part.astype(BF).reshape(2, 128, 1024)
        return carry

    lax.fori_loop(0, 4, out_sum, 0)
    by_core(3)
    weight_sum(2, grad_v, 0)
    by_first(3)
    weight_sum(1, grad_k, 0)
    by_first(2)
    by_second(3)
    weight_sum(0, grad_q, 384)
    by_first(1)
    by_second(2)
    by_pair(3)

    @pl.when(me_z > 1)
    def _():
        halo_copy.start()

    def near_rows(index, carry):
        place_cols = tile(index)
        keys_part = grad_k[:, 384:640, :].reshape(512, 1024)
        values_part = grad_v[:, 384:640, :].reshape(512, 1024)
        grads = (
            dot_nt(keys_part, weights[1, place_cols, :])
            + dot_nt(values_part, weights[2, place_cols, :])
            + dot_nt(grad_q[...].reshape(512, 1024), weights[0, place_cols, :])
        )
        note(index, grads, normed[:, 384:640, place_cols].reshape(512, 256))
        own_rows[:, :, place_cols] = grads.reshape(2, 256, 256)
        return carry

    shown[1].wait()
    lax.fori_loop(0, 4, near_rows, 0)
    by_first(0)
    pass_down(2, 0)
    by_second(1)
    pass_down(2, 1)
    by_middle(3)
    pass_down(2, 2)
    pass_down(1, 0)
    by_pair(2)
    pass_down(2, 3)
    pass_down(1, 1)
    copy = pltpu.make_async_copy(own_rows, own_out, out_sem.at[6])
    copy.start()
    own.append(copy)

    gain, offset = known[0:1, :], known[2:3, :]
    table[0:1, :] = (table[0:1, :] - offset * table[2:3, :]) / gain
    table[14:15, :] = jnp.sum(grad_q[...].reshape(512, 1024).astype(F32), axis=0, keepdims=True)
    table[15:16, :] = jnp.sum(grad_v[...].reshape(1280, 1024).astype(F32), axis=0, keepdims=True)
    for fsdp in range(8):
        for tensor in range(4):
            target = 4 * fsdp + tensor
            small_mine[target, 0:16, :] = table[:, fsdp * 128 : fsdp * 128 + 128]
            for which in range(2):
                for half in range(2):
                    lane = tensor * 256 + half * 128
                    row = 16 + 2 * which + half
                    small_mine[target, row : row + 1, :] = table[
                        14 + which : 15 + which, lane : lane + 128
                    ]

    def small_copy(step):
        other = lax.rem(mine + step, 32)
        return pltpu.make_async_remote_copy(
            src_ref=small_mine.at[other], dst_ref=small_got.at[mine], send_sem=small_send.at[step],
            recv_sem=small_recv.at[step], device_id=place(other // 4, lax.rem(other, 4)),
            device_id_type=MESH,
        )

    def start_small(step, carry):
        small_copy(step).start()
        return carry

    lax.fori_loop(1, 32, start_small, 0)
    small_got[mine] = small_mine[mine]
    pass_down(1, 2)
    pass_down(0, 0)
    by_second(0)
    pass_down(1, 3)
    pass_down(0, 1)
    by_pair(1)
    by_last(3)
    by_middle(2)
    pass_down(0, 2)
    by_pair(0)
    by_middle(1)
    by_last(2)
    pass_down(0, 3)
    by_middle(0)
    by_last(1)
    by_end(3)
    by_end(2)
    by_last(0)
    by_end(1)
    by_end(0)
    trunk_done = pltpu.make_async_copy(trunk_rows, trunk_out, out_sem.at[7])
    trunk_done.start()
    own.append(trunk_done)

    @pl.when(me_z > 0)
    def _():
        for index in range(4):
            trunk_copy(index).wait_send()

    @pl.when(me_z > 1)
    def _():
        halo_copy.wait_send()

    @pl.when((me_z > 0) & (me_z < 3))
    def _():
        halo_copy.wait_recv()

    def end_small(step, carry):
        copy = small_copy(step)
        copy.wait_send()
        copy.wait_recv()
        return carry

    lax.fori_loop(1, 32, end_small, 0)

    def sum_small(index, total):
        return total + small_got[index]

    small_out[...] = lax.fori_loop(1, 32, sum_small, small_got[0])

    def end_step(step, carry):
        for copy in remote(step):
            copy.wait_send()
            copy.wait_recv()
        return carry

    lax.fori_loop(1, 32, end_step, 0)
    sender.finish()
    for copy in own:
        copy.wait()


def attend_back(*operands):
    dma = pltpu.SemaphoreType.DMA
    specs = any_spec(9)
    specs[3] = pl.BlockSpec(memory_space=pltpu.VMEM)
    tree, keyed = (2, 256, 1024), (2, 640, 1024)
    return pl.pallas_call(
        backward_kernel,
        out_shape=[
            jax.ShapeDtypeStruct((8, 128, 1024), BF),
            jax.ShapeDtypeStruct((8, 1024, 128), BF),
            jax.ShapeDtypeStruct((4, 128, 256), BF),
            jax.ShapeDtypeStruct((24, 128), F32),
            jax.ShapeDtypeStruct(tree, F32),
            jax.ShapeDtypeStruct((4, 128, 1024), BF),
            jax.ShapeDtypeStruct((2, 128, 1024), BF),
            jax.ShapeDtypeStruct(tree, BF),
            jax.ShapeDtypeStruct(tree, F32),
        ],
        in_specs=any_spec(16),
        out_specs=specs,
        scratch_shapes=[
            pltpu.VMEM((4, 1024, 1024), BF),
            pltpu.VMEM((4, 4, 2, 128, 1024), BF),
            pltpu.VMEM(tree, BF),
            pltpu.VMEM(tree, BF),
            pltpu.VMEM(tree, BF),
            pltpu.VMEM(tree, BF),
            pltpu.VMEM(keyed, BF),
            pltpu.VMEM(keyed, BF),
            pltpu.VMEM(keyed, BF),
            pltpu.VMEM((16, 256, 640), BF),
            pltpu.VMEM(tree, BF),
            pltpu.VMEM(keyed, BF),
            pltpu.VMEM(keyed, BF),
            pltpu.VMEM(tree, F32),
            pltpu.VMEM((4, 128, 1024), BF),
            pltpu.VMEM((2, 128, 1024), BF),
            pltpu.VMEM((4, 128, 1024), BF),
            pltpu.VMEM((4, 4, 128, 1024), BF),
            pltpu.VMEM((4, 2, 128, 1024), BF),
            pltpu.VMEM((4, 128, 1024), BF),
            pltpu.VMEM((4, 128, 512), BF),
            pltpu.VMEM((4, 128, 512), BF),
            pltpu.VMEM((4, 128, 256), BF),
            pltpu.VMEM((16, 1024), F32),
            pltpu.VMEM((16, 1024), F32),
            pltpu.VMEM((32, 24, 128), F32),
            pltpu.VMEM((32, 24, 128), F32),
            pltpu.VMEM(operands[3].shape, BF),
            pltpu.VMEM((2, 256, 128), F32),
            pltpu.VMEM((2, 256, 128), BF),
            pltpu.VMEM((128, 1024), BF),
            dma((28,)), dma((28,)), dma((25,)),
            dma((32,)), dma((32,)), dma((32,)), dma((32,)),
            dma((32,)), dma((32,)), dma((5,)), dma((5,)), dma((10,)),
        ],
        compiler_params=pltpu.CompilerParams(
            collective_id=3, has_side_effects=True, vmem_limit_bytes=63 << 20
        ),
        name="attend_back",
    )(*operands)


def fast_body(
    tokens, segment, route, w_qkv, bias_qv, w_o, w_router, w_up, w_down, norm_gains, shifts, cotangent
):
    micro_count, local_rows, width = tokens.shape
    expert_count = w_up.shape[0]
    cap = 3 * local_rows // (2 * expert_count)
    me_z = lax.axis_index("tensor")
    start = me_z * local_rows
    me_f = lax.axis_index("fsdp")
    lane = jnp.arange(128)
    mine = jnp.concatenate(
        [norm_gains, shifts, w_router.T, jnp.zeros((2, 32), BF)], axis=0
    )
    mine = jnp.where(lane // 32 == me_z, jnp.tile(mine, (1, 4)), 0)
    bias_lane = jnp.arange(64)
    bias_mine = jnp.where(bias_lane // 8 == me_f, jnp.tile(bias_qv, (1, 1, 8)), 0).reshape(4, 128)
    small = jnp.concatenate([mine, bias_mine, jnp.zeros((12, 128), BF)], axis=0)
    w4 = jnp.concatenate([w_qkv, w_o.T[None]], axis=0)
    own_index = start + jnp.arange(local_rows)
    key_index = jnp.concatenate([jnp.arange(256), start - 128 + jnp.arange(128), own_index])
    key_part = jnp.arange(640) < 256
    own_segs = lax.dynamic_slice_in_dim(segment, start, local_rows, axis=1)
    halo_segs = lax.dynamic_slice_in_dim(segment, jnp.maximum(start - 128, 0), 128, axis=1)
    key_segs = jnp.concatenate([segment[:, :256], halo_segs, own_segs], axis=1)
    query_seg, key_seg = own_segs[:, :, None], key_segs[:, None, :]
    allowed = (
        (key_seg == 0)
        | (key_seg == query_seg)
        | (query_seg >= 5) & (key_seg == (query_seg - 5) // 2 + 1)
    )
    allowed = allowed & (key_part | (key_index >= 256))[None, None, :]
    allowed = allowed & (key_index[None, :] <= own_index[:, None])[None]
    bias = jnp.where(allowed, 0.0, MASKED)
    own_routes = lax.dynamic_slice_in_dim(route[:, :, 0], start, local_rows, axis=1)
    chosen = (own_routes[:, :, None] == lane).astype(BF)
    (
        full4, params, rows_all, normed_all, queries, keys, values, heads_low, residual, probs_low,
        slots, pick, router_probs, up_own, down_own,
    ) = attend_all(w4, small, tokens, w_up, w_down, bias, chosen, cotangent, cap)
    slots = slots.reshape(2, micro_count, expert_count, cap, width)
    back, up_grad, down_grad = run_experts(slots, up_own, down_own)
    back = back.reshape(2 * micro_count, 3, 128, width)
    (
        up_out, down_out, out4, small_out, grad_own, trunk_sum, halo_sum, output, grad_mixed,
    ) = attend_back(
        up_grad, down_grad, back, pick, residual, cotangent, router_probs, chosen,
        heads_low, queries, keys, values, normed_all, probs_low, full4, params,
    )
    gain = params[0]
    _, plain_in, scale_in = norm_rows(tokens.astype(F32), gain, params[2])

    def flat(value):
        return value.reshape(-1, value.shape[-1])

    trunk_sum = trunk_sum.reshape(2, 256, width).astype(F32)
    grad_normed = grad_own + jnp.where(me_z == 0, trunk_sum, 0.0)
    grad_normed = grad_normed.at[:, 128:].add(jnp.where((me_z > 0) & (me_z < 3), halo_sum.astype(F32), 0.0))
    grad_from_in, _, _ = norm_back(flat(grad_normed), flat(plain_in), flat(scale_in), gain)
    input_grad = grad_mixed + grad_from_in.reshape(grad_mixed.shape)
    bias_out = lax.dynamic_slice_in_dim(
        small_out[16:20].reshape(2, 4, 64), me_f * 8, 8, axis=2
    )
    small_out = lax.dynamic_slice_in_dim(small_out[:14], me_z * 32, 32, axis=1)
    return (
        output,
        input_grad,
        out4[:3].astype(F32),
        bias_out,
        out4[3].T.astype(F32),
        small_out[6:14].T,
        up_out.astype(F32),
        down_out.astype(F32),
        small_out[:2],
        small_out[2:5],
        small_out[5],
    )


def solution(mesh):
    placed = (
        P(None, ("fsdp", "tensor"), None),
        P(None, "fsdp"),
        P(None, "fsdp", None),
        P(None, "fsdp", "tensor"),
        P(None, "tensor", "fsdp"),
        P("tensor", "fsdp"),
        P(("fsdp", "tensor"), None),
        P(None, "fsdp", "tensor"),
        P(None, "tensor", "fsdp"),
        P(None, ("fsdp", "tensor")),
        P(None, ("fsdp", "tensor")),
        P(None, ("fsdp", "tensor"), None),
    )
    return jax.shard_map(
        fast_body if fits(mesh) else plain_body,
        mesh=mesh,
        in_specs=placed,
        out_specs=(
            P(None, ("fsdp", "tensor"), None),
            P(None, ("fsdp", "tensor"), None),
            P(None, "fsdp", "tensor"),
            P(None, "tensor", "fsdp"),
            P("tensor", "fsdp"),
            P(("fsdp", "tensor"), None),
            P(None, "fsdp", "tensor"),
            P(None, "tensor", "fsdp"),
            P(None, ("fsdp", "tensor")),
            P(None, ("fsdp", "tensor")),
            P(("fsdp", "tensor")),
        ),
        check_vma=False,
    )
```
